32 devices in a mesh: brick: 8 (over y, x, core), tile: 4 (over z).
Axes of the slice: x: 2, y: 2, z: 4, core: 2. Of those that a mesh axis runs over, the one named last changes fastest.
Arguments:
- sample_grad: bfloat16 [28, 32768], P(None, ('brick', 'tile')), may hold values from -6 to 6
- sample_brick: int32 [32768], P(('brick', 'tile')), may hold values from 0 to 255, as said below
- sample_slot: int32 [32768], P(('brick', 'tile')), may hold values from 0 to 511
- neighbour: int32 [32, 6], P('brick'), may hold values from 0 to 31, as said below
Outputs:
- fine_grad: float32 [256, 28, 512], P(('brick', 'tile'))
- coarse_grad: float32 [32, 28, 512], P('brick', None, 'tile')
The draws below stay inside these ranges and needn't reach their ends.
Inputs may be any that keep to these rules, and one draw needn't show every extreme that they name: `sample_brick`: of the 1024 samples of one device (consecutive along the samples), exactly 256 fall in the bricks of each of 4 owners (owner = brick // 32) and none in the others' bricks; some owners get 256 from every device. Of the 256 samples that one device has in one owner's bricks, exactly 64 lie in each group of 8 consecutive bricks of that owner. The relation is symmetric: neighbour[neighbour[b, k], k'] = b for the opposite face k'; no brick is its own neighbour. All face neighbours of a brick lie in its block of 4 consecutive coarse ids, the blocks starting at 2 and the last one wrapping around to id 0.
All inputs are finite; a program needn't handle non-finite values.
Results may differ from the reference program's by a relative error of at most 0.0003.
Values may be sent and summed in bfloat16 or wider, within the bound.
No kernel may reach another device: no remote copies, remote signals or barrier semaphores. Data moves between devices by JAX's collectives and lax.ppermute only.
A program may use at most 64 MiB of HBM per device.

```python
import jax
import jax.numpy as jnp
import numpy as np
from jax import lax

C = 28
E = 8
V = 512
FACE = 64
CB_DEV = 4
FB_DEV = 32
S_DEV = 1024
SAMPLES = 32768
FINE = 256
COARSE = 32
CAP = 256
BS = 8
SLICE_CAP = 64


def sample_layout(key):
    base_key = jax.random.fold_in(key, 7)
    owners = FINE // FB_DEV
    block_total = SAMPLES // S_DEV
    group_count = S_DEV // CAP
    hot_rank = jax.random.permutation(jax.random.fold_in(base_key, 1), owners)
    hot_flag = (hot_rank < max(owners // 8, 1)).astype(jnp.int32)

    def one_block(block_id):
        block_key = jax.random.fold_in(base_key, block_id + 100)
        key_score, key_order, key_brick, key_slot = jax.random.split(block_key, 4)
        scores = jax.random.randint(key_score, (owners,), 0, 4096) * owners + jnp.arange(owners, dtype=jnp.int32) + hot_flag * (4096 * owners)
        _, owner_table = lax.top_k(scores, group_count)
        position = jax.random.permutation(key_order, S_DEV)
        owner_of = owner_table[position // CAP]
        group_id = position % CAP // SLICE_CAP
        local_brick = group_id * BS + jax.random.randint(key_brick, (S_DEV,), 0, BS)
        slot_drawn = jax.random.randint(key_slot, (S_DEV,), 0, V)
        return (owner_of * FB_DEV + local_brick, slot_drawn)
    bricks_all, slots_all = jax.vmap(one_block)(jnp.arange(block_total, dtype=jnp.int32))
    return (bricks_all.reshape(-1).astype(jnp.int32), slots_all.reshape(-1).astype(jnp.int32))


def draw_sample_brick(key, part):
    return sample_layout(key)[0]


def draw_sample_slot(key, part):
    return sample_layout(key)[1]


def draw_neighbour(key, part):
    base_key = jax.random.fold_in(key, 11)
    window = CB_DEV
    windows = COARSE // window
    columns = []
    for axis_id in range(3):
        window_keys = jax.random.split(jax.random.fold_in(base_key, axis_id), windows)
        cycle_orders = jax.vmap(lambda one_key: jax.random.permutation(one_key, window))(window_keys).astype(jnp.int32)
        members = (jnp.arange(windows, dtype=jnp.int32)[:, None] * window + window // 2 + cycle_orders) % COARSE
        followers = jnp.roll(members, -1, axis=1)
        upper_of = jnp.zeros((COARSE,), jnp.int32).at[members.reshape(-1)].set(followers.reshape(-1))
        lower_of = jnp.zeros((COARSE,), jnp.int32).at[followers.reshape(-1)].set(members.reshape(-1))
        columns.append(lower_of)
        columns.append(upper_of)
    return jnp.stack(columns, axis=1)


def block_levels(key, shape, cuts, least, high):
    def one(axis_at, shards_of):
        heights = jax.random.uniform(jax.random.fold_in(jax.random.fold_in(key, 6), axis_at), (shards_of,), jnp.float32, least / len(cuts), high / len(cuts))
        return jnp.repeat(jnp.exp(heights), shape[axis_at] // shards_of).reshape((-1,) + (1,) * (len(shape) - axis_at - 1))

    loudness = one(*cuts[0])
    for cut in cuts[1:]:
        loudness = loudness * one(*cut)
    return loudness


def gaussian(stream_key, extent, scale, limit, cuts=(), held_as=jnp.bfloat16):
    factor_of = block_levels(stream_key, extent, cuts, -0.22, 0.18) if cuts else 1.0
    values = jax.random.normal(stream_key, extent, jnp.float32) * scale * factor_of
    return jnp.minimum(jnp.maximum(values, -limit), limit).astype(held_as)


def setup_inputs(seed: int = 0) -> dict:
    key_of = jax.random.split(jax.random.key(seed), 5)
    return {
        "sample_grad": gaussian(key_of[0], (C, SAMPLES), 1.0, 6.0, ((1, 32),)),
        "sample_brick": draw_sample_brick(jax.random.fold_in(key_of[4], 71), 0),
        "sample_slot": draw_sample_slot(jax.random.fold_in(key_of[4], 71), 0),
        "neighbour": draw_neighbour(jax.random.fold_in(key_of[4], 71), 0),
    }


def corners(fine_pos):
    is_even = (fine_pos % 2) == 0
    lower_at = jnp.where(is_even, fine_pos // 2, fine_pos // 2 + 1)
    lower_w = jnp.where(is_even, 0.25, 0.75).astype(jnp.float32)
    return ((lower_at, lower_w), (lower_at + 1, 1.0 - lower_w))


def fold_column(pos_a, pos_b, pos_c, brick_edge):
    out_a = (pos_a == 0) | (pos_a == brick_edge + 1)
    out_b = (pos_b == 0) | (pos_b == brick_edge + 1)
    out_c = (pos_c == 0) | (pos_c == brick_edge + 1)
    outside = out_a.astype(jnp.int32) + out_b.astype(jnp.int32) + out_c.astype(jnp.int32)
    clamp_a = jnp.clip(pos_a, 1, brick_edge) - 1
    clamp_b = jnp.clip(pos_b, 1, brick_edge) - 1
    clamp_c = jnp.clip(pos_c, 1, brick_edge) - 1
    inner_col = clamp_a * brick_edge * brick_edge + clamp_b * brick_edge + clamp_c
    face_cells = brick_edge * brick_edge
    face_base = brick_edge ** 3
    face_a = face_base + jnp.where(pos_a == 0, 0, 1) * face_cells + (pos_b - 1) * brick_edge + (pos_c - 1)
    face_b = face_base + (2 + jnp.where(pos_b == 0, 0, 1)) * face_cells + (pos_a - 1) * brick_edge + (pos_c - 1)
    face_c = face_base + (4 + jnp.where(pos_c == 0, 0, 1)) * face_cells + (pos_a - 1) * brick_edge + (pos_b - 1)
    single = outside == 1
    return jnp.where(single & out_a, face_a, jnp.where(single & out_b, face_b, jnp.where(single & out_c, face_c, inner_col)))


def child_matrix(child_id, first_slot, row_count, brick_edge):
    slot_ids = first_slot + jnp.arange(row_count, dtype=jnp.int32)
    coord_x = slot_ids // (brick_edge * brick_edge)
    coord_y = (slot_ids // brick_edge) % brick_edge
    coord_z = slot_ids % brick_edge
    fine_x = ((child_id >> 2) & 1) * brick_edge + coord_x
    fine_y = ((child_id >> 1) & 1) * brick_edge + coord_y
    fine_z = (child_id & 1) * brick_edge + coord_z
    column_total = brick_edge ** 3 + 6 * brick_edge * brick_edge
    column_ids = jnp.arange(column_total, dtype=jnp.int32)
    matrix = jnp.zeros((row_count, column_total), jnp.float32)
    for pos_a, weight_a in corners(fine_x):
        for pos_b, weight_b in corners(fine_y):
            for pos_c, weight_c in corners(fine_z):
                column = fold_column(pos_a, pos_b, pos_c, brick_edge)
                weight = weight_a * weight_b * weight_c
                matrix = matrix + jnp.where(column[:, None] == column_ids[None, :], weight[:, None], 0.0).astype(jnp.float32)
    return matrix


def layer_index(brick_edge):
    grid_p, grid_q = np.meshgrid(np.arange(brick_edge), np.arange(brick_edge), indexing="ij")
    grid_p = grid_p.reshape(-1)
    grid_q = grid_q.reshape(-1)
    square = brick_edge * brick_edge
    last = brick_edge - 1
    layers = [grid_p * brick_edge + grid_q, last * square + grid_p * brick_edge + grid_q,
              grid_p * square + grid_q, grid_p * square + last * brick_edge + grid_q,
              grid_p * square + grid_q * brick_edge, grid_p * square + grid_q * brick_edge + last]
    return np.concatenate(layers).astype(np.int32)


def reference(sample_grad, sample_brick, sample_slot, neighbour):
    values = sample_grad.astype(jnp.float32).T
    target = (sample_brick * V + sample_slot).astype(jnp.int32)
    flat_sum = jnp.zeros((FINE * V, C), jnp.float32).at[target].add(values)
    fine_grad = flat_sum.reshape(FINE, V, C).transpose(0, 2, 1)
    families = fine_grad.reshape(COARSE, 8, C, V)
    padded = jnp.zeros((COARSE, C, V + 6 * FACE), jnp.float32)
    for child_id in range(8):
        matrix = child_matrix(child_id, 0, V, E)
        padded = padded + jnp.einsum("bcv,vo->bco", families[:, child_id], matrix, precision=lax.Precision.HIGHEST)
    own_part = padded[:, :, :V]
    face_skins = padded[:, :, V:].reshape(COARSE, C, 6, FACE)
    arrived = jnp.stack([face_skins[:, :, face_id ^ 1, :][neighbour[:, face_id]] for face_id in range(6)], axis=2)
    layer_cells = jnp.asarray(layer_index(E))
    coarse_grad = own_part.at[:, :, layer_cells].add(arrived.reshape(COARSE, C, 6 * FACE))
    return fine_grad, coarse_grad
```

```python
import functools

import jax
import jax.numpy as jnp
import numpy as np
from jax import lax
from jax.experimental import pallas as pl
from jax.experimental.pallas import tpu as pltpu
from jax.sharding import PartitionSpec as P

E = 8
V = 512
FACE = 64
CB_DEV = 4
FB_DEV = 32


row_block = 256


def extended_2(block, sides, width):
    for axis, dim in sides:
        count = lax.axis_size(axis)
        forward = [(i, i + 1) for i in range(count - 1)]
        forward.append((count - 1, 0))
        backward = [(target, source) for source, target in forward]
        low = lax.ppermute(
            lax.slice_in_dim(block, block.shape[dim] - width, None, axis=dim), axis, forward
        )
        high = lax.ppermute(lax.slice_in_dim(block, 0, width, axis=dim), axis, backward)
        block = jnp.concatenate([low, block, high], axis=dim)
    return block


def corners(fine_pos):
    is_even = fine_pos % 2 == 0
    lower_at = jnp.where(is_even, fine_pos // 2, fine_pos // 2 + 1)
    lower_w = jnp.where(is_even, 0.25, 0.75).astype(jnp.float32)
    return ((lower_at, lower_w), (lower_at + 1, 1.0 - lower_w))


def fold_column(pos_a, pos_b, pos_c, brick_edge):
    out_a = (pos_a == 0) | (pos_a == brick_edge + 1)
    out_b = (pos_b == 0) | (pos_b == brick_edge + 1)
    out_c = (pos_c == 0) | (pos_c == brick_edge + 1)
    outside = out_a.astype(jnp.int32) + out_b.astype(jnp.int32) + out_c.astype(jnp.int32)
    clamp_a = jnp.clip(pos_a, 1, brick_edge) - 1
    clamp_b = jnp.clip(pos_b, 1, brick_edge) - 1
    clamp_c = jnp.clip(pos_c, 1, brick_edge) - 1
    inner_col = clamp_a * brick_edge * brick_edge + clamp_b * brick_edge + clamp_c
    face_cells = brick_edge * brick_edge
    face_base = brick_edge**3
    face_a = (
        face_base
        + jnp.where(pos_a == 0, 0, 1) * face_cells
        + (pos_b - 1) * brick_edge
        + (pos_c - 1)
    )
    face_b = (
        face_base
        + (2 + jnp.where(pos_b == 0, 0, 1)) * face_cells
        + (pos_a - 1) * brick_edge
        + (pos_c - 1)
    )
    face_c = (
        face_base
        + (4 + jnp.where(pos_c == 0, 0, 1)) * face_cells
        + (pos_a - 1) * brick_edge
        + (pos_b - 1)
    )
    single = outside == 1
    return jnp.where(
        single & out_a,
        face_a,
        jnp.where(single & out_b, face_b, jnp.where(single & out_c, face_c, inner_col)),
    )


def child_matrix(child_id, row_count, brick_edge):
    slot_ids = jnp.arange(row_count, dtype=jnp.int32)
    coord_x = slot_ids // (brick_edge * brick_edge)
    coord_y = slot_ids // brick_edge % brick_edge
    coord_z = slot_ids % brick_edge
    fine_x = (child_id >> 2 & 1) * brick_edge + coord_x
    fine_y = (child_id >> 1 & 1) * brick_edge + coord_y
    fine_z = (child_id & 1) * brick_edge + coord_z
    column_total = brick_edge**3 + 6 * brick_edge * brick_edge
    column_ids = jnp.arange(column_total, dtype=jnp.int32)
    matrix = jnp.zeros((row_count, column_total), jnp.float32)
    for pos_a, weight_a in corners(fine_x):
        for pos_b, weight_b in corners(fine_y):
            for pos_c, weight_c in corners(fine_z):
                column = fold_column(pos_a, pos_b, pos_c, brick_edge)
                weight = weight_a * weight_b * weight_c
                matrix = matrix + jnp.where(
                    column[:, None] == column_ids[None, :], weight[:, None], 0.0
                )
    return matrix


def layer_matrix(brick_edge):
    grid_p, grid_q = np.meshgrid(np.arange(brick_edge), np.arange(brick_edge), indexing="ij")
    grid_p = grid_p.reshape(-1)
    grid_q = grid_q.reshape(-1)
    square = brick_edge * brick_edge
    last = brick_edge - 1
    layers = [
        grid_p * brick_edge + grid_q,
        last * square + grid_p * brick_edge + grid_q,
        grid_p * square + grid_q,
        grid_p * square + last * brick_edge + grid_q,
        grid_p * square + grid_q * brick_edge,
        grid_p * square + grid_q * brick_edge + last,
    ]
    cells = np.concatenate(layers)
    table = np.zeros((cells.shape[0], brick_edge**3), dtype=np.float32)
    table[np.arange(cells.shape[0]), cells] = 1.0
    return table


def rank_within(bucket_key):
    count = bucket_key.shape[0]
    order = jnp.arange(count, dtype=jnp.int32)
    earlier = (bucket_key[:, None] == bucket_key[None, :]) & (order[None, :] < order[:, None])
    return jnp.sum(earlier.astype(jnp.int32), axis=1)


def pack_rows(sample_grad, slot_code, bucket_at, slot_total):
    channels = sample_grad.shape[0]
    high_part = (slot_code // 128).astype(jnp.bfloat16)
    low_part = (slot_code % 128).astype(jnp.bfloat16)
    stacked = jnp.concatenate([sample_grad, high_part[None, :], low_part[None, :]], axis=0)
    hits = bucket_at[:, None] == jnp.arange(slot_total, dtype=jnp.int32)[None, :]
    placed = jnp.dot(stacked, hits.astype(jnp.bfloat16), preferred_element_type=jnp.float32)
    filled = jnp.any(hits, axis=0)
    high_row = jnp.where(filled, placed[channels], -1.0)
    moved = jnp.concatenate([placed[:channels], high_row[None, :], placed[channels + 1 :]], axis=0)
    return moved.astype(jnp.bfloat16)


def unpack_rows(arrived, channels):
    grad_rows = arrived[:channels]
    code_rows = arrived[channels].astype(jnp.int32) * 128 + arrived[channels + 1].astype(jnp.int32)
    return (grad_rows, code_rows)


def accumulate(grad_rows, code_rows, brick_count, slot_count):
    channels = grad_rows.shape[0]
    block_total = code_rows.shape[0] // row_block

    def add_block(block_id, running):
        start_row = block_id * row_block
        grad_part = lax.dynamic_slice_in_dim(grad_rows, start_row, row_block, 1)
        code_part = lax.dynamic_slice_in_dim(code_rows, start_row, row_block, 0)
        brick_part = jnp.where(code_part >= 0, code_part // slot_count, -1)
        slot_part = code_part % slot_count
        brick_hot = brick_part[None, :] == jnp.arange(brick_count, dtype=jnp.int32)[:, None]
        masked = jnp.where(brick_hot[:, None, :], grad_part[None, :, :], 0)
        slot_hot = (slot_part[:, None] == jnp.arange(slot_count, dtype=jnp.int32)[None, :]).astype(
            jnp.bfloat16
        )
        product = jnp.dot(
            masked.reshape(brick_count * channels, row_block),
            slot_hot,
            preferred_element_type=jnp.float32,
        )
        return running + product

    running = lax.fori_loop(
        0, block_total, add_block, jnp.zeros((brick_count * channels, slot_count), jnp.float32)
    )
    return running.reshape(brick_count, channels, slot_count)


def body(sample_grad, sample_brick, sample_slot, neighbour):
    tile_count = lax.axis_size("tile")
    owners = lax.axis_size("brick")
    tile_id = lax.axis_index("tile")
    brick_id = lax.axis_index("brick")
    samples = sample_brick.shape[0]
    channels = sample_grad.shape[0]
    capacity = 2 * samples // owners
    group_len = FB_DEV // tile_count
    group_cap = capacity // tile_count
    owner_of = sample_brick // FB_DEV
    local_brick = sample_brick - owner_of * FB_DEV
    group_of = local_brick // group_len
    bucket_key = owner_of * tile_count + group_of
    slot_code = (local_brick - group_of * group_len) * V + sample_slot
    bucket_at = bucket_key * group_cap + rank_within(bucket_key)
    packed = pack_rows(sample_grad, slot_code, bucket_at, owners * tile_count * group_cap)
    arrived = lax.all_to_all(
        lax.all_to_all(
            packed.reshape(channels + 2, owners, tile_count, group_cap),
            "brick",
            split_axis=1,
            concat_axis=1,
            tiled=True,
        ),
        "tile",
        split_axis=2,
        concat_axis=2,
        tiled=True,
    )
    grad_rows, code_rows = unpack_rows(
        arrived.reshape(channels + 2, owners * tile_count * group_cap), channels
    )
    fine_grad = accumulate(grad_rows, code_rows, group_len, V)
    family_count = max(group_len // 8, 1)
    first_fine = tile_id * group_len
    holder = jnp.zeros((family_count * 8, channels, V), jnp.float32)
    holder = lax.dynamic_update_slice_in_dim(holder, fine_grad, first_fine % (family_count * 8), 0)
    families = holder.reshape(family_count, 8, channels, V)
    part_padded = jnp.zeros((family_count, channels, V + 6 * FACE), jnp.float32)
    for child_id in range(8):
        matrix = child_matrix(child_id, V, E)
        part_padded = part_padded + jnp.einsum(
            "bcv,vo->bco", families[:, child_id], matrix, precision=lax.Precision.HIGHEST
        )
    padded = jnp.zeros((CB_DEV, channels, V + 6 * FACE), jnp.float32)
    padded = lax.dynamic_update_slice_in_dim(padded, part_padded, first_fine // 8, 0)
    face_skins = padded[:, :, V:]
    extended = extended_2(face_skins, (("brick", 0),), CB_DEV // 2)
    coarse_total = CB_DEV * owners
    offset = (neighbour - (brick_id * CB_DEV - CB_DEV // 2)) % coarse_total
    opposite = np.array([1, 0, 3, 2, 5, 4], dtype=np.int32)
    facing = extended.reshape(2 * CB_DEV, channels, 6, FACE)[:, :, opposite, :]
    selector = (
        offset[:, :, None] == jnp.arange(2 * CB_DEV, dtype=jnp.int32)[None, None, :]
    ).astype(jnp.float32)
    incoming = jnp.einsum("bke,eckf->bckf", selector, facing, precision=lax.Precision.HIGHEST)
    layer_table = jnp.asarray(layer_matrix(E))
    spread = jnp.einsum(
        "bcf,fv->bcv",
        incoming.reshape(CB_DEV, channels, 6 * FACE),
        layer_table,
        precision=lax.Precision.HIGHEST,
    )
    own_part = padded[:, :, :V] + spread
    coarse_grad = lax.psum_scatter(own_part, "tile", scatter_dimension=2, tiled=True)
    return (fine_grad, coarse_grad)


LANES = 128


def tri_table():
    below = np.arange(LANES)[:, None] < np.arange(LANES)[None, :]
    return np.concatenate([below, np.ones((LANES, LANES), bool)], axis=1).astype(np.float32)


def plane_weights(brick_edge):
    table = np.zeros((2, brick_edge, brick_edge + 2), np.float32)
    for half in range(2):
        for cell in range(brick_edge):
            at = half * brick_edge + cell
            table[half, cell, at // 2 + 1] += 0.75
            table[half, cell, at // 2 - 1 + 2 * (at % 2) + 1] += 0.25
    return table


def plane_matrices(brick_edge):
    weight = plane_weights(brick_edge)
    square = brick_edge * brick_edge
    full = np.einsum("aym,bzn->abyzmn", weight, weight).reshape(4 * square, brick_edge + 2, brick_edge + 2)
    out = np.zeros((4, 4 * square, 2 * LANES), np.float32)
    last = brick_edge - 1
    for m2 in range(-1, brick_edge + 1):
        for m3 in range(-1, brick_edge + 1):
            column = full[:, m2 + 1, m3 + 1]
            out_y = m2 < 0 or m2 > last
            out_z = m3 < 0 or m3 > last
            cell = min(max(m2, 0), last) * brick_edge + min(max(m3, 0), last)
            for odd in range(2):
                if out_y == out_z:
                    out[odd, :, odd * square + cell] += column
                elif out_y:
                    face = 0 if m2 < 0 else 1
                    out[odd, :, LANES + (odd * 4 + face) * brick_edge + m3] += column
                else:
                    face = 2 if m3 < 0 else 3
                    out[odd, :, LANES + (odd * 4 + face) * brick_edge + m2] += column
            for side in range(2):
                if out_y or out_z:
                    out[2 + side, :, side * square + cell] += column
                else:
                    out[2 + side, :, LANES + square + cell] += column
    return out


def expand_tables(brick_edge):
    square = brick_edge * brick_edge
    last = brick_edge - 1
    out = np.zeros((2, LANES, LANES), np.float32)
    for side in range(2):
        for odd in range(2):
            for at in range(brick_edge):
                base = odd * 4 * brick_edge + at
                out[side, base, odd * square + last * brick_edge + at] = 1
                out[side, base + brick_edge, odd * square + at] = 1
                out[side, base + 2 * brick_edge, odd * square + at * brick_edge + last] = 1
                out[side, base + 3 * brick_edge, odd * square + at * brick_edge] = 1
        for cell in range(square):
            out[side, square + cell, side * square + cell] = 1
    return out


def split_two(value):
    high = value.astype(jnp.bfloat16)
    low = (value - high.astype(jnp.float32)).astype(jnp.bfloat16)
    return high, low


def contract_last(left, right):
    return lax.dot_general(left, right, (((1,), (1,)), ((), ())), preferred_element_type=jnp.float32)


def pack_kernel(group_len, dests, brick_ref, slot_ref, grad_ref, tri_ref, out_ref, full_ref):
    channels = grad_ref.shape[0]
    blocks = brick_ref.shape[0]
    square = E * E
    brick = brick_ref[...]
    slot = slot_ref[...]
    bucket = brick // group_len
    local = brick - bucket * group_len
    plane = slot // square
    cell = slot - plane * square
    bucket_f = bucket.astype(jnp.float32)
    dest_ids = lax.broadcasted_iota(jnp.int32, (dests, LANES), 0).astype(jnp.float32)
    hots = [
        jnp.where(jnp.broadcast_to(bucket_f[i : i + 1], (dests, LANES)) == dest_ids, 1.0, 0.0)
        for i in range(blocks)
    ]
    counts = jnp.dot(
        jnp.concatenate(hots, axis=0).astype(jnp.bfloat16), tri_ref[...], preferred_element_type=jnp.float32
    )
    before = jnp.zeros((dests, LANES), jnp.float32)
    ranks = []
    for i in range(blocks):
        part = counts[i * dests : (i + 1) * dests]
        ranks.append(jnp.sum(hots[i] * (part[:, :LANES] + before), axis=0, keepdims=True))
        before = before + part[:, LANES:]
    rank = jnp.concatenate(ranks, axis=1)

    rows = lax.broadcasted_iota(jnp.int32, (4, LANES), 0)
    local_f = (local + 1).astype(jnp.float32)
    plane_f = plane.astype(jnp.float32)
    cell_f = cell.astype(jnp.float32)
    full_ref[:channels, :] = grad_ref[...]
    for i in range(blocks):
        code = jnp.where(
            rows == 0,
            local_f[i : i + 1],
            jnp.where(rows == 1, plane_f[i : i + 1], jnp.where(rows == 2, cell_f[i : i + 1], 0.0)),
        )
        full_ref[channels : channels + 4, i * LANES : (i + 1) * LANES] = code.astype(jnp.bfloat16)
    low = full_ref[:16, :]
    high = full_ref[16:32, :]
    bucket16 = jnp.concatenate(
        [jnp.broadcast_to(bucket_f[i : i + 1], (16, LANES)) for i in range(blocks)], axis=1
    ).astype(jnp.bfloat16)
    zero = jnp.zeros_like(low)
    low_rows = []
    high_rows = []
    for dest in range(dests):
        mask = bucket16 == jnp.bfloat16(dest)
        low_rows.append(jnp.where(mask, low, zero))
        high_rows.append(jnp.where(mask, high, zero))
    rank_ids = lax.broadcasted_iota(jnp.int32, (LANES, rank.shape[1]), 0).astype(jnp.float32)
    half = LANES // 2
    hot_low = jnp.where(rank_ids == rank, 1.0, 0.0).astype(jnp.bfloat16)
    hot_high = jnp.where(rank_ids == rank + half, 1.0, 0.0).astype(jnp.bfloat16)
    placed = contract_last(jnp.concatenate(low_rows, axis=0), hot_low)
    placed = placed + contract_last(jnp.concatenate(high_rows, axis=0), hot_high)
    out_ref[...] = placed.astype(jnp.bfloat16).reshape(dests, 16, LANES)


def grid_kernel(channels, arrived_ref, plane_ref, fine_ref, own_ref, skin_ref, quarter_ref, turn_ref):
    tile_id = lax.axis_index("tile")
    sources = arrived_ref.shape[0]
    half = LANES // 2
    lows = []
    highs = []
    for p in range(sources // 2):
        first = arrived_ref[p]
        second = arrived_ref[p + sources // 2]
        lows.append(jnp.concatenate([first[:, :half], second[:, :half]], axis=1))
        highs.append(jnp.concatenate([first[:, half:], second[:, half:]], axis=1))
    low = jnp.concatenate(lows, axis=1)
    high = jnp.concatenate(highs, axis=1)
    total = low.shape[1]
    codes = high.astype(jnp.float32)
    at = channels - 16
    brick16 = jnp.broadcast_to(codes[at : at + 1], (16, total)).astype(jnp.bfloat16)
    plane16 = jnp.broadcast_to(codes[at + 1 : at + 2], (16, total)).astype(jnp.bfloat16)
    cell16 = jnp.broadcast_to(codes[at + 2 : at + 3], (16, total)).astype(jnp.bfloat16)
    zero = jnp.zeros_like(low)
    one = jnp.ones_like(low)
    left = []
    for child in range(8):
        mask = brick16 == jnp.bfloat16(child + 1)
        left.append(jnp.where(mask, low, zero))
        left.append(jnp.where(mask, high, zero))
    row_ids = lax.broadcasted_iota(jnp.int32, (16, total), 0).astype(jnp.float32)
    cells = [
        jnp.where(cell16 == (row_ids + 16.0 * g).astype(jnp.bfloat16), one, zero) for g in range(E * E // 16)
    ]
    right = []
    for plane in range(E):
        mask = plane16 == jnp.bfloat16(plane)
        for g in range(E * E // 16):
            right.append(jnp.where(mask, cells[g], zero))
    fine = contract_last(jnp.concatenate(left, axis=0), jnp.concatenate(right, axis=0))
    parts = [fine[32 * child : 32 * child + 32] for child in range(8)]
    for i in range(V // LANES):
        for child in range(8):
            turn_ref[i, pl.ds(child, channels, stride=8), :] = parts[child][:channels, i * LANES : (i + 1) * LANES]
        fine_ref[:, i * LANES : (i + 1) * LANES] = turn_ref[i]

    lane = lax.broadcasted_iota(jnp.int32, (32, LANES), 1)
    first_half = lane < half
    blank = jnp.zeros((32, LANES), jnp.float32)

    def slab(child, m):
        return parts[child][:, m * LANES : (m + 1) * LANES] if 0 <= m < E // 2 else blank

    def along_x(child, m):
        value = 0.25 * jnp.where(first_half, slab(child, m + 1), slab(child, m - 1))
        return value + 0.75 * slab(child, m) if 0 <= m < E // 2 else value

    def layer(m):
        columns = []
        for kyz in range(4):
            if m <= E // 2 and m >= E // 2 - 1:
                columns.append(along_x(kyz, m) + along_x(4 + kyz, m - E // 2))
            elif m < E // 2:
                columns.append(along_x(kyz, m))
            else:
                columns.append(along_x(4 + kyz, m - E // 2))
        return jnp.concatenate(columns, axis=1)

    def matrix(which):
        pieces = []
        for kyz in range(4):
            piece = plane_ref[which, kyz * half : (kyz + 1) * half, :]
            pieces += [piece, piece]
        return jnp.concatenate(pieces, axis=0)

    def apply(stack, table):
        high_part, low_part = split_two(stack)
        return jnp.dot(high_part, table, preferred_element_type=jnp.float32) + jnp.dot(
            low_part, table, preferred_element_type=jnp.float32
        )

    even = jnp.concatenate([layer(2 * q) for q in range(4)], axis=0)
    odd = jnp.concatenate([layer(2 * q + 1) for q in range(4)], axis=0)
    inner = apply(even, matrix(0)) + apply(odd, matrix(1))
    below = apply(layer(-1), matrix(2))
    above = apply(layer(E), matrix(3))
    for q in range(4):
        own = inner[32 * q : 32 * q + 32, :LANES]
        skin = inner[32 * q : 32 * q + 32, LANES:]
        if q == 0:
            own = own + below[:, :LANES]
            skin = skin + above[:, LANES:]
        if q == 3:
            own = own + above[:, :LANES]
            skin = skin + below[:, LANES:]
        quarter_ref[q, 0] = own
        quarter_ref[q, 1] = skin
    for delta in range(4):
        own_ref[delta] = quarter_ref[tile_id ^ delta, 0][:channels]
        skin_ref[delta] = quarter_ref[tile_id ^ delta, 1][:channels]


def combine_kernel(channels, coarse_total, near_ref, own_ref, skin_ref, far_ref, one_ref, two_ref, three_ref,
                   table_ref, out_ref, hold_ref):
    tile_id = lax.axis_index("tile")
    brick_id = lax.axis_index("brick")
    hold_ref[tile_id, 0] = own_ref[0]
    hold_ref[tile_id, 1] = skin_ref[0]
    hold_ref[tile_id, 2] = far_ref[0]
    for delta, ref in ((1, one_ref), (2, two_ref), (3, three_ref)):
        hold_ref[tile_id ^ delta] = ref[...]
    lane = lax.broadcasted_iota(jnp.int32, (channels, LANES), 1)
    group = jnp.where(lane < LANES // 2, (lane // E) % 4, 4)
    skins = [hold_ref[2, 2], hold_ref[3, 2]]
    skins += [hold_ref[j, 1] for j in range(4)]
    skins += [hold_ref[0, 2], hold_ref[1, 2]]
    x_face = jnp.where(tile_id < 2, 0, 1)
    gathered = []
    for i in range(4):
        near = [
            (near_ref[i, face] - (brick_id * 4 - 2) + coarse_total) % coarse_total for face in (3, 2, 5, 4)
        ]
        near.append((near_ref[i, x_face] - (brick_id * 4 - 2) + coarse_total) % coarse_total)
        source = jnp.where(
            group == 0,
            near[0],
            jnp.where(group == 1, near[1], jnp.where(group == 2, near[2], jnp.where(group == 3, near[3], near[4]))),
        )
        first = 0 if i < 2 else 4
        value = jnp.zeros((channels, LANES), jnp.float32)
        for e in range(first, first + 4):
            value = jnp.where(source == e, skins[e], value)
        gathered.append(value)
    table = table_ref[tile_id // 2]
    for i in range(4):
        high_part, low_part = split_two(gathered[i])
        moved = jnp.dot(high_part, table, preferred_element_type=jnp.float32) + jnp.dot(
            low_part, table, preferred_element_type=jnp.float32
        )
        out_ref[pl.ds(i, channels, stride=4), :] = hold_ref[i, 0] + moved


def family_body(sample_grad, sample_brick, sample_slot, neighbour):
    tile_count = lax.axis_size("tile")
    owners = lax.axis_size("brick")
    channels, samples = sample_grad.shape
    dests = owners * tile_count
    group_len = FB_DEV // tile_count
    vmem = pl.BlockSpec(memory_space=pltpu.VMEM)
    packed = pl.pallas_call(
        functools.partial(pack_kernel, group_len, dests),
        out_shape=jax.ShapeDtypeStruct((dests, 16, LANES), jnp.bfloat16),
        in_specs=[vmem] * 4,
        out_specs=vmem,
        scratch_shapes=[pltpu.VMEM((32, samples), jnp.bfloat16)],
        name="pack",
    )(
        sample_brick.reshape(samples // LANES, LANES),
        sample_slot.reshape(samples // LANES, LANES),
        sample_grad,
        jnp.asarray(tri_table(), jnp.bfloat16),
    )
    arrived = lax.all_to_all(packed, ("brick", "tile"), 0, 0, tiled=True)
    quarter = jax.ShapeDtypeStruct((4, channels, LANES), jnp.float32)
    fine, own, skin = pl.pallas_call(
        functools.partial(grid_kernel, channels),
        out_shape=(jax.ShapeDtypeStruct((channels * 8, V), jnp.float32), quarter, quarter),
        in_specs=[vmem] * 2,
        out_specs=(vmem,) * 3,
        scratch_shapes=[
            pltpu.VMEM((4, 2, 32, LANES), jnp.float32),
            pltpu.VMEM((V // LANES, channels * 8, LANES), jnp.float32),
        ],
        name="grid",
    )(arrived, jnp.asarray(plane_matrices(E), jnp.bfloat16))
    pairs = []
    for b in range(owners):
        for t in range(tile_count):
            step = 1 if t >= tile_count // 2 else -1
            pairs.append((b * tile_count + t, (b + step) % owners * tile_count + t))
    far = lax.ppermute(skin, ("brick", "tile"), pairs)
    arrivals = []
    for delta in (3, 2, 1):
        message = jnp.stack([own[delta], skin[delta], far[delta]])
        arrivals.append(lax.ppermute(message, "tile", [(t, t ^ delta) for t in range(tile_count)]))
    coarse = pl.pallas_call(
        functools.partial(combine_kernel, channels, CB_DEV * owners),
        out_shape=jax.ShapeDtypeStruct((channels * CB_DEV, LANES), jnp.float32),
        in_specs=[pl.BlockSpec(memory_space=pltpu.SMEM)] + [vmem] * 7,
        out_specs=vmem,
        scratch_shapes=[pltpu.VMEM((4, 3, channels, LANES), jnp.float32)],
        name="combine",
    )(neighbour, own, skin, far, arrivals[2], arrivals[1], arrivals[0], jnp.asarray(expand_tables(E), jnp.bfloat16))
    fine_grad = fine.reshape(channels, 8, V).transpose(1, 0, 2)
    coarse_grad = coarse.reshape(channels, CB_DEV, LANES).transpose(1, 0, 2)
    return fine_grad, coarse_grad


def solution(mesh):
    in_specs = (
        P(None, ("brick", "tile")),
        P(("brick", "tile")),
        P(("brick", "tile")),
        P("brick", None),
    )
    out_specs = (P(("brick", "tile"), None, None), P("brick", None, "tile"))

    def step(sample_grad, sample_brick, sample_slot, neighbour):
        owners, tile_count = mesh.shape["brick"], mesh.shape["tile"]
        samples = sample_grad.shape[1] // (owners * tile_count)
        whole_family = FB_DEV == 8 * tile_count == 2 * 4 * CB_DEV and tile_count == CB_DEV
        full_messages = 2 * samples == (LANES // 2) * owners * tile_count and samples % LANES == 0
        fits = whole_family and full_messages and sample_grad.shape[0] == 28 and owners > 2
        chosen = family_body if fits else body
        return jax.shard_map(chosen, mesh=mesh, in_specs=in_specs, out_specs=out_specs, check_vma=False)(
            sample_grad, sample_brick, sample_slot, neighbour
        )

    return step
```

```python
import functools

import jax
import jax.numpy as jnp
import numpy as np
from jax import lax
from jax.experimental import pallas as pl
from jax.experimental.pallas import tpu as pltpu
from jax.sharding import PartitionSpec as P


E = 8
V = 512
FACE = 64
CB_DEV = 4
FB_DEV = 32


row_block = 256


def extended_2(block, sides, width):
    for axis, dim in sides:
        count = lax.axis_size(axis)
        forward = [(i, i + 1) for i in range(count - 1)]
        forward.append((count - 1, 0))
        backward = [(target, source) for source, target in forward]
        low = lax.ppermute(
            lax.slice_in_dim(block, block.shape[dim] - width, None, axis=dim), axis, forward
        )
        high = lax.ppermute(lax.slice_in_dim(block, 0, width, axis=dim), axis, backward)
        block = jnp.concatenate([low, block, high], axis=dim)
    return block


def corners(fine_pos):
    is_even = fine_pos % 2 == 0
    lower_at = jnp.where(is_even, fine_pos // 2, fine_pos // 2 + 1)
    lower_w = jnp.where(is_even, 0.25, 0.75).astype(jnp.float32)
    return ((lower_at, lower_w), (lower_at + 1, 1.0 - lower_w))


def fold_column(pos_a, pos_b, pos_c, brick_edge):
    out_a = (pos_a == 0) | (pos_a == brick_edge + 1)
    out_b = (pos_b == 0) | (pos_b == brick_edge + 1)
    out_c = (pos_c == 0) | (pos_c == brick_edge + 1)
    outside = out_a.astype(jnp.int32) + out_b.astype(jnp.int32) + out_c.astype(jnp.int32)
    clamp_a = jnp.clip(pos_a, 1, brick_edge) - 1
    clamp_b = jnp.clip(pos_b, 1, brick_edge) - 1
    clamp_c = jnp.clip(pos_c, 1, brick_edge) - 1
    inner_col = clamp_a * brick_edge * brick_edge + clamp_b * brick_edge + clamp_c
    face_cells = brick_edge * brick_edge
    face_base = brick_edge**3
    face_a = (
        face_base
        + jnp.where(pos_a == 0, 0, 1) * face_cells
        + (pos_b - 1) * brick_edge
        + (pos_c - 1)
    )
    face_b = (
        face_base
        + (2 + jnp.where(pos_b == 0, 0, 1)) * face_cells
        + (pos_a - 1) * brick_edge
        + (pos_c - 1)
    )
    face_c = (
        face_base
        + (4 + jnp.where(pos_c == 0, 0, 1)) * face_cells
        + (pos_a - 1) * brick_edge
        + (pos_b - 1)
    )
    single = outside == 1
    return jnp.where(
        single & out_a,
        face_a,
        jnp.where(single & out_b, face_b, jnp.where(single & out_c, face_c, inner_col)),
    )


def child_matrix(child_id, row_count, brick_edge):
    slot_ids = jnp.arange(row_count, dtype=jnp.int32)
    coord_x = slot_ids // (brick_edge * brick_edge)
    coord_y = slot_ids // brick_edge % brick_edge
    coord_z = slot_ids % brick_edge
    fine_x = (child_id >> 2 & 1) * brick_edge + coord_x
    fine_y = (child_id >> 1 & 1) * brick_edge + coord_y
    fine_z = (child_id & 1) * brick_edge + coord_z
    column_total = brick_edge**3 + 6 * brick_edge * brick_edge
    column_ids = jnp.arange(column_total, dtype=jnp.int32)
    matrix = jnp.zeros((row_count, column_total), jnp.float32)
    for pos_a, weight_a in corners(fine_x):
        for pos_b, weight_b in corners(fine_y):
            for pos_c, weight_c in corners(fine_z):
                column = fold_column(pos_a, pos_b, pos_c, brick_edge)
                weight = weight_a * weight_b * weight_c
                matrix = matrix + jnp.where(
                    column[:, None] == column_ids[None, :], weight[:, None], 0.0
                )
    return matrix


def layer_matrix(brick_edge):
    grid_p, grid_q = np.meshgrid(np.arange(brick_edge), np.arange(brick_edge), indexing="ij")
    grid_p = grid_p.reshape(-1)
    grid_q = grid_q.reshape(-1)
    square = brick_edge * brick_edge
    last = brick_edge - 1
    layers = [
        grid_p * brick_edge + grid_q,
        last * square + grid_p * brick_edge + grid_q,
        grid_p * square + grid_q,
        grid_p * square + last * brick_edge + grid_q,
        grid_p * square + grid_q * brick_edge,
        grid_p * square + grid_q * brick_edge + last,
    ]
    cells = np.concatenate(layers)
    table = np.zeros((cells.shape[0], brick_edge**3), dtype=np.float32)
    table[np.arange(cells.shape[0]), cells] = 1.0
    return table


def rank_within(bucket_key):
    count = bucket_key.shape[0]
    order = jnp.arange(count, dtype=jnp.int32)
    earlier = (bucket_key[:, None] == bucket_key[None, :]) & (order[None, :] < order[:, None])
    return jnp.sum(earlier.astype(jnp.int32), axis=1)


def pack_rows(sample_grad, slot_code, bucket_at, slot_total):
    channels = sample_grad.shape[0]
    high_part = (slot_code // 128).astype(jnp.bfloat16)
    low_part = (slot_code % 128).astype(jnp.bfloat16)
    stacked = jnp.concatenate([sample_grad, high_part[None, :], low_part[None, :]], axis=0)
    hits = bucket_at[:, None] == jnp.arange(slot_total, dtype=jnp.int32)[None, :]
    placed = jnp.dot(stacked, hits.astype(jnp.bfloat16), preferred_element_type=jnp.float32)
    filled = jnp.any(hits, axis=0)
    high_row = jnp.where(filled, placed[channels], -1.0)
    moved = jnp.concatenate([placed[:channels], high_row[None, :], placed[channels + 1 :]], axis=0)
    return moved.astype(jnp.bfloat16)


def unpack_rows(arrived, channels):
    grad_rows = arrived[:channels]
    code_rows = arrived[channels].astype(jnp.int32) * 128 + arrived[channels + 1].astype(jnp.int32)
    return (grad_rows, code_rows)


def accumulate(grad_rows, code_rows, brick_count, slot_count):
    channels = grad_rows.shape[0]
    block_total = code_rows.shape[0] // row_block

    def add_block(block_id, running):
        start_row = block_id * row_block
        grad_part = lax.dynamic_slice_in_dim(grad_rows, start_row, row_block, 1)
        code_part = lax.dynamic_slice_in_dim(code_rows, start_row, row_block, 0)
        brick_part = jnp.where(code_part >= 0, code_part // slot_count, -1)
        slot_part = code_part % slot_count
        brick_hot = brick_part[None, :] == jnp.arange(brick_count, dtype=jnp.int32)[:, None]
        masked = jnp.where(brick_hot[:, None, :], grad_part[None, :, :], 0)
        slot_hot = (slot_part[:, None] == jnp.arange(slot_count, dtype=jnp.int32)[None, :]).astype(
            jnp.bfloat16
        )
        product = jnp.dot(
            masked.reshape(brick_count * channels, row_block),
            slot_hot,
            preferred_element_type=jnp.float32,
        )
        return running + product

    running = lax.fori_loop(
        0, block_total, add_block, jnp.zeros((brick_count * channels, slot_count), jnp.float32)
    )
    return running.reshape(brick_count, channels, slot_count)


def body(sample_grad, sample_brick, sample_slot, neighbour):
    tile_count = lax.axis_size("tile")
    owners = lax.axis_size("brick")
    tile_id = lax.axis_index("tile")
    brick_id = lax.axis_index("brick")
    samples = sample_brick.shape[0]
    channels = sample_grad.shape[0]
    capacity = 2 * samples // owners
    group_len = FB_DEV // tile_count
    group_cap = capacity // tile_count
    owner_of = sample_brick // FB_DEV
    local_brick = sample_brick - owner_of * FB_DEV
    group_of = local_brick // group_len
    bucket_key = owner_of * tile_count + group_of
    slot_code = (local_brick - group_of * group_len) * V + sample_slot
    bucket_at = bucket_key * group_cap + rank_within(bucket_key)
    packed = pack_rows(sample_grad, slot_code, bucket_at, owners * tile_count * group_cap)
    arrived = lax.all_to_all(
        lax.all_to_all(
            packed.reshape(channels + 2, owners, tile_count, group_cap),
            "brick",
            split_axis=1,
            concat_axis=1,
            tiled=True,
        ),
        "tile",
        split_axis=2,
        concat_axis=2,
        tiled=True,
    )
    grad_rows, code_rows = unpack_rows(
        arrived.reshape(channels + 2, owners * tile_count * group_cap), channels
    )
    fine_grad = accumulate(grad_rows, code_rows, group_len, V)
    family_count = max(group_len // 8, 1)
    first_fine = tile_id * group_len
    holder = jnp.zeros((family_count * 8, channels, V), jnp.float32)
    holder = lax.dynamic_update_slice_in_dim(holder, fine_grad, first_fine % (family_count * 8), 0)
    families = holder.reshape(family_count, 8, channels, V)
    part_padded = jnp.zeros((family_count, channels, V + 6 * FACE), jnp.float32)
    for child_id in range(8):
        matrix = child_matrix(child_id, V, E)
        part_padded = part_padded + jnp.einsum(
            "bcv,vo->bco", families[:, child_id], matrix, precision=lax.Precision.HIGHEST
        )
    padded = jnp.zeros((CB_DEV, channels, V + 6 * FACE), jnp.float32)
    padded = lax.dynamic_update_slice_in_dim(padded, part_padded, first_fine // 8, 0)
    face_skins = padded[:, :, V:]
    extended = extended_2(face_skins, (("brick", 0),), CB_DEV // 2)
    coarse_total = CB_DEV * owners
    offset = (neighbour - (brick_id * CB_DEV - CB_DEV // 2)) % coarse_total
    opposite = np.array([1, 0, 3, 2, 5, 4], dtype=np.int32)
    facing = extended.reshape(2 * CB_DEV, channels, 6, FACE)[:, :, opposite, :]
    selector = (
        offset[:, :, None] == jnp.arange(2 * CB_DEV, dtype=jnp.int32)[None, None, :]
    ).astype(jnp.float32)
    incoming = jnp.einsum("bke,eckf->bckf", selector, facing, precision=lax.Precision.HIGHEST)
    layer_table = jnp.asarray(layer_matrix(E))
    spread = jnp.einsum(
        "bcf,fv->bcv",
        incoming.reshape(CB_DEV, channels, 6 * FACE),
        layer_table,
        precision=lax.Precision.HIGHEST,
    )
    own_part = padded[:, :, :V] + spread
    coarse_grad = lax.psum_scatter(own_part, "tile", scatter_dimension=2, tiled=True)
    return (fine_grad, coarse_grad)


LANES = 128
KERNEL_VMEM = 16 * 1024 * 1024


def plane_weights(brick_edge):
    table = np.zeros((2, brick_edge, brick_edge + 2), np.float32)
    for half in range(2):
        for cell in range(brick_edge):
            at = half * brick_edge + cell
            table[half, cell, at // 2 + 1] += 0.75
            table[half, cell, at // 2 - 1 + 2 * (at % 2) + 1] += 0.25
    return table


def plane_matrices(brick_edge):
    weight = plane_weights(brick_edge)
    square = brick_edge * brick_edge
    full = np.einsum("aym,bzn->abyzmn", weight, weight).reshape(4 * square, brick_edge + 2, brick_edge + 2)
    out = np.zeros((4, 4 * square, 2 * LANES), np.float32)
    last = brick_edge - 1
    for m2 in range(-1, brick_edge + 1):
        for m3 in range(-1, brick_edge + 1):
            column = full[:, m2 + 1, m3 + 1]
            out_y = m2 < 0 or m2 > last
            out_z = m3 < 0 or m3 > last
            cell = min(max(m2, 0), last) * brick_edge + min(max(m3, 0), last)
            for odd in range(2):
                if out_y == out_z:
                    out[odd, :, odd * square + cell] += column
                elif out_y:
                    face = 0 if m2 < 0 else 1
                    out[odd, :, LANES + (odd * 4 + face) * brick_edge + m3] += column
                else:
                    face = 2 if m3 < 0 else 3
                    out[odd, :, LANES + (odd * 4 + face) * brick_edge + m2] += column
            for side in range(2):
                if out_y or out_z:
                    out[2 + side, :, side * square + cell] += column
                else:
                    out[2 + side, :, LANES + square + cell] += column
    return out


def expand_tables(brick_edge):
    square = brick_edge * brick_edge
    last = brick_edge - 1
    out = np.zeros((2, LANES, LANES), np.float32)
    for side in range(2):
        for odd in range(2):
            for at in range(brick_edge):
                base = odd * 4 * brick_edge + at
                out[side, base, odd * square + last * brick_edge + at] = 1
                out[side, base + brick_edge, odd * square + at] = 1
                out[side, base + 2 * brick_edge, odd * square + at * brick_edge + last] = 1
                out[side, base + 3 * brick_edge, odd * square + at * brick_edge] = 1
        for cell in range(square):
            out[side, square + cell, side * square + cell] = 1
    return out


def split_two(value):
    high = value.astype(jnp.bfloat16)
    low = (value - high.astype(jnp.float32)).astype(jnp.bfloat16)
    return high, low


def contract_last(left, right):
    return lax.dot_general(left, right, (((1,), (1,)), ((), ())), preferred_element_type=jnp.float32)


def pack_kernel(group_len, dests, brick_hbm, slot_hbm, grad_hbm, plane_hbm, out_ref, plane_ref, brick_ref, slot_ref, grad_ref, high_ref, sems):
    channels = grad_hbm.shape[0]
    blocks = brick_ref.shape[0]
    square = E * E
    copies = [
        pltpu.make_async_copy(brick_hbm, brick_ref, sems.at[0]),
        pltpu.make_async_copy(slot_hbm, slot_ref, sems.at[1]),
        pltpu.make_async_copy(grad_hbm, grad_ref, sems.at[2]),
        pltpu.make_async_copy(plane_hbm, plane_ref, sems.at[3]),
    ]
    for copy in copies:
        copy.start()
    at_row = lax.broadcasted_iota(jnp.int32, (LANES, 2 * LANES), 0)
    at_lane = lax.broadcasted_iota(jnp.int32, (LANES, 2 * LANES), 1)
    tri = jnp.where((at_row < at_lane) | (at_lane >= LANES), 1.0, 0.0).astype(jnp.bfloat16)
    copies[0].wait()
    copies[1].wait()
    brick = brick_ref[...]
    slot = slot_ref[...]
    bucket = brick // group_len
    local = brick - bucket * group_len
    plane = slot // square
    cell = slot - plane * square
    bucket_f = bucket.astype(jnp.float32)
    dest_ids = lax.broadcasted_iota(jnp.int32, (dests, LANES), 0).astype(jnp.float32)
    hots = [
        jnp.where(jnp.broadcast_to(bucket_f[i : i + 1], (dests, LANES)) == dest_ids, 1.0, 0.0)
        for i in range(blocks)
    ]
    counts = jnp.dot(
        jnp.concatenate(hots, axis=0).astype(jnp.bfloat16), tri, preferred_element_type=jnp.float32
    )
    before = jnp.zeros((dests, LANES), jnp.float32)
    ranks = []
    for i in range(blocks):
        part = counts[i * dests : (i + 1) * dests]
        ranks.append(jnp.sum(hots[i] * (part[:, :LANES] + before), axis=0, keepdims=True))
        before = before + part[:, LANES:]
    rank = jnp.concatenate(ranks, axis=1)

    rows = lax.broadcasted_iota(jnp.int32, (4, LANES), 0)
    local_f = (local + 1).astype(jnp.float32)
    plane_f = plane.astype(jnp.float32)
    cell_f = cell.astype(jnp.float32)
    for i in range(blocks):
        code = jnp.where(
            rows == 0,
            local_f[i : i + 1],
            jnp.where(rows == 1, plane_f[i : i + 1], jnp.where(rows == 2, cell_f[i : i + 1], 0.0)),
        )
        high_ref[channels - 16 : channels - 12, i * LANES : (i + 1) * LANES] = code.astype(jnp.bfloat16)
    copies[2].wait()
    high_ref[: channels - 16, :] = grad_ref[16:channels, :]
    low = grad_ref[:16, :]
    high = high_ref[...]
    bucket16 = jnp.concatenate(
        [jnp.broadcast_to(bucket_f[i : i + 1], (16, LANES)) for i in range(blocks)], axis=1
    ).astype(jnp.bfloat16)
    zero = jnp.zeros_like(low)
    low_rows = []
    high_rows = []
    for dest in range(dests):
        mask = bucket16 == jnp.bfloat16(dest)
        low_rows.append(jnp.where(mask, low, zero))
        high_rows.append(jnp.where(mask, high, zero))
    rank_ids = lax.broadcasted_iota(jnp.int32, (LANES, rank.shape[1]), 0).astype(jnp.float32)
    half = LANES // 2
    hot_low = jnp.where(rank_ids == rank, 1.0, 0.0).astype(jnp.bfloat16)
    hot_high = jnp.where(rank_ids == rank + half, 1.0, 0.0).astype(jnp.bfloat16)
    placed = contract_last(jnp.concatenate(low_rows, axis=0), hot_low)
    placed = placed + contract_last(jnp.concatenate(high_rows, axis=0), hot_high)
    out_ref[...] = placed.astype(jnp.bfloat16).reshape(dests, 16, LANES)
    copies[3].wait()


def grid_kernel(channels, arrived_ref, plane_ref, fine_ref, own_ref, skin_ref, quarter_ref):
    tile_id = lax.axis_index("tile")
    sources = arrived_ref.shape[0]
    half = LANES // 2
    lows = []
    highs = []
    for p in range(sources // 2):
        first = arrived_ref[p]
        second = arrived_ref[p + sources // 2]
        lows.append(jnp.concatenate([first[:, :half], second[:, :half]], axis=1))
        highs.append(jnp.concatenate([first[:, half:], second[:, half:]], axis=1))
    low = jnp.concatenate(lows, axis=1)
    high = jnp.concatenate(highs, axis=1)
    total = low.shape[1]
    codes = high.astype(jnp.float32)
    at = channels - 16
    brick16 = jnp.broadcast_to(codes[at : at + 1], (16, total)).astype(jnp.bfloat16)
    plane16 = jnp.broadcast_to(codes[at + 1 : at + 2], (16, total)).astype(jnp.bfloat16)
    cell16 = jnp.broadcast_to(codes[at + 2 : at + 3], (16, total)).astype(jnp.bfloat16)
    zero = jnp.zeros_like(low)
    one = jnp.ones_like(low)
    left = []
    for child in range(8):
        mask = brick16 == jnp.bfloat16(child + 1)
        left.append(jnp.where(mask, low, zero))
        left.append(jnp.where(mask, high, zero))
    row_ids = lax.broadcasted_iota(jnp.int32, (16, total), 0).astype(jnp.float32)
    cells = [
        jnp.where(cell16 == (row_ids + 16.0 * g).astype(jnp.bfloat16), one, zero) for g in range(E * E // 16)
    ]
    right = []
    for plane in range(E):
        mask = plane16 == jnp.bfloat16(plane)
        for g in range(E * E // 16):
            right.append(jnp.where(mask, cells[g], zero))
    fine = contract_last(jnp.concatenate(left, axis=0), jnp.concatenate(right, axis=0))
    parts = [fine[32 * child : 32 * child + 32] for child in range(8)]
    fine_ref[...] = fine

    lane = lax.broadcasted_iota(jnp.int32, (32, LANES), 1)
    first_half = lane < half
    blank = jnp.zeros((32, LANES), jnp.float32)

    def slab(child, m):
        return parts[child][:, m * LANES : (m + 1) * LANES] if 0 <= m < E // 2 else blank

    def along_x(child, m):
        value = 0.25 * jnp.where(first_half, slab(child, m + 1), slab(child, m - 1))
        return value + 0.75 * slab(child, m) if 0 <= m < E // 2 else value

    def layer(m):
        columns = []
        for kyz in range(4):
            if m <= E // 2 and m >= E // 2 - 1:
                columns.append(along_x(kyz, m) + along_x(4 + kyz, m - E // 2))
            elif m < E // 2:
                columns.append(along_x(kyz, m))
            else:
                columns.append(along_x(4 + kyz, m - E // 2))
        return jnp.concatenate(columns, axis=1)

    def matrix(which):
        pieces = []
        for kyz in range(4):
            piece = plane_ref[which, kyz * half : (kyz + 1) * half, :]
            pieces += [piece, piece]
        return jnp.concatenate(pieces, axis=0)

    def apply(stack, table):
        high_part, low_part = split_two(stack)
        return jnp.dot(high_part, table, preferred_element_type=jnp.float32) + jnp.dot(
            low_part, table, preferred_element_type=jnp.float32
        )

    even = jnp.concatenate([layer(2 * q) for q in range(4)], axis=0)
    odd = jnp.concatenate([layer(2 * q + 1) for q in range(4)], axis=0)
    inner = apply(even, matrix(0)) + apply(odd, matrix(1))
    below = apply(layer(-1), matrix(2))
    above = apply(layer(E), matrix(3))
    for q in range(4):
        own = inner[32 * q : 32 * q + 32, :LANES]
        skin = inner[32 * q : 32 * q + 32, LANES:]
        if q == 0:
            own = own + below[:, :LANES]
            skin = skin + above[:, LANES:]
        if q == 3:
            own = own + above[:, :LANES]
            skin = skin + below[:, LANES:]
        quarter_ref[q, 0] = own
        quarter_ref[q, 1] = skin
    for delta in range(4):
        own_ref[delta] = quarter_ref[tile_id ^ delta, 0][:channels]
        skin_ref[delta] = quarter_ref[tile_id ^ delta, 1][:channels]


def turn_kernel(channels, coarse_total, rows_ref, near_ref, fine_ref, source_ref, turn_ref):
    first = lax.axis_index("brick") * CB_DEV - CB_DEV // 2
    lane = lax.broadcasted_iota(jnp.int32, (8, LANES), 1)
    group = jnp.where(lane < LANES // 2, (lane // E) % 4, 4)
    x_face = jnp.where(lax.axis_index("tile") < 2, 0, 1)
    for i in range(CB_DEV):
        near = [(near_ref[i, face] - first + coarse_total) % coarse_total for face in (3, 2, 5, 4, x_face)]
        source = jnp.where(group == 0, near[0], near[1])
        for k in range(2, 5):
            source = jnp.where(group == k, near[k], source)
        source_ref[i] = source
    for i in range(V // LANES):
        for child in range(8):
            turn_ref[i, pl.ds(child, channels, stride=8), :] = rows_ref[
                32 * child : 32 * child + channels, i * LANES : (i + 1) * LANES
            ]
        fine_ref[:, i * LANES : (i + 1) * LANES] = turn_ref[i]


def combine_kernel(channels, source_ref, own_ref, skin_ref, far_ref, one_ref, two_ref, three_ref,
                   table_ref, out_ref, hold_ref):
    tile_id = lax.axis_index("tile")
    hold_ref[tile_id, 0] = own_ref[0]
    hold_ref[tile_id, 1] = skin_ref[0]
    hold_ref[tile_id, 2] = far_ref[0]
    for delta, ref in ((1, one_ref), (2, two_ref), (3, three_ref)):
        hold_ref[tile_id ^ delta] = ref[...]
    skins = [hold_ref[2, 2], hold_ref[3, 2]]
    skins += [hold_ref[j, 1] for j in range(4)]
    skins += [hold_ref[0, 2], hold_ref[1, 2]]
    gathered = []
    for i in range(4):
        source = jnp.broadcast_to(source_ref[i, :1], (channels, LANES))
        first = 0 if i < 2 else 4
        value = jnp.zeros((channels, LANES), jnp.float32)
        for e in range(first, first + 4):
            value = jnp.where(source == e, skins[e], value)
        gathered.append(value)
    table = table_ref[tile_id // 2]
    for i in range(4):
        high_part, low_part = split_two(gathered[i])
        moved = jnp.dot(high_part, table, preferred_element_type=jnp.float32) + jnp.dot(
            low_part, table, preferred_element_type=jnp.float32
        )
        out_ref[pl.ds(i, channels, stride=4), :] = hold_ref[i, 0] + moved


def family_body(sample_grad, sample_brick, sample_slot, neighbour):
    tile_count = lax.axis_size("tile")
    owners = lax.axis_size("brick")
    channels, samples = sample_grad.shape
    dests = owners * tile_count
    group_len = FB_DEV // tile_count
    vmem = pl.BlockSpec(memory_space=pltpu.VMEM)
    packed, planes = pl.pallas_call(
        functools.partial(pack_kernel, group_len, dests),
        out_shape=(
            jax.ShapeDtypeStruct((dests, 16, LANES), jnp.bfloat16),
            jax.ShapeDtypeStruct((4, 4 * E * E, 2 * LANES), jnp.bfloat16),
        ),
        in_specs=[pl.BlockSpec(memory_space=pltpu.HBM)] * 4,
        out_specs=(vmem, vmem),
        scratch_shapes=[
            pltpu.VMEM((samples // LANES, LANES), jnp.int32),
            pltpu.VMEM((samples // LANES, LANES), jnp.int32),
            pltpu.VMEM((channels, samples), jnp.bfloat16),
            pltpu.VMEM((16, samples), jnp.bfloat16),
            pltpu.SemaphoreType.DMA((4,)),
        ],
        compiler_params=pltpu.CompilerParams(vmem_limit_bytes=KERNEL_VMEM),
        name="pack",
    )(
        pltpu.with_memory_space_constraint(sample_brick.reshape(samples // LANES, LANES), pltpu.HBM),
        pltpu.with_memory_space_constraint(sample_slot.reshape(samples // LANES, LANES), pltpu.HBM),
        pltpu.with_memory_space_constraint(sample_grad, pltpu.HBM),
        pltpu.with_memory_space_constraint(jnp.asarray(plane_matrices(E), jnp.bfloat16), pltpu.HBM),
    )
    arrived = lax.all_to_all(packed, ("brick", "tile"), 0, 0, tiled=True)
    quarter = jax.ShapeDtypeStruct((4, channels, LANES), jnp.float32)
    rows, own, skin = pl.pallas_call(
        functools.partial(grid_kernel, channels),
        out_shape=(jax.ShapeDtypeStruct((8 * 32, V), jnp.float32), quarter, quarter),
        in_specs=[vmem, vmem],
        out_specs=(vmem,) * 3,
        scratch_shapes=[pltpu.VMEM((4, 2, 32, LANES), jnp.float32)],
        compiler_params=pltpu.CompilerParams(vmem_limit_bytes=KERNEL_VMEM),
        name="grid",
    )(arrived, planes)
    pairs = []
    for b in range(owners):
        for t in range(tile_count):
            step = 1 if t >= tile_count // 2 else -1
            pairs.append((b * tile_count + t, (b + step) % owners * tile_count + t))
    far = lax.ppermute(skin, ("brick", "tile"), pairs)
    fine, source = pl.pallas_call(
        functools.partial(turn_kernel, channels, CB_DEV * owners),
        out_shape=(
            jax.ShapeDtypeStruct((channels * 8, V), jnp.float32),
            jax.ShapeDtypeStruct((CB_DEV, 8, LANES), jnp.int32),
        ),
        in_specs=[vmem, pl.BlockSpec(memory_space=pltpu.SMEM)],
        out_specs=(vmem, vmem),
        scratch_shapes=[pltpu.VMEM((V // LANES, channels * 8, LANES), jnp.float32)],
        compiler_params=pltpu.CompilerParams(vmem_limit_bytes=KERNEL_VMEM),
        name="turn",
    )(rows, neighbour)
    arrivals = {}
    for delta in (3, 2, 1):
        message = jnp.stack([own[delta], skin[delta], far[delta]])
        arrivals[delta] = lax.ppermute(message, "tile", [(t, t ^ delta) for t in range(tile_count)])
    coarse = pl.pallas_call(
        functools.partial(combine_kernel, channels),
        out_shape=jax.ShapeDtypeStruct((channels * CB_DEV, LANES), jnp.float32),
        in_specs=[vmem] * 8,
        out_specs=vmem,
        scratch_shapes=[pltpu.VMEM((4, 3, channels, LANES), jnp.float32)],
        compiler_params=pltpu.CompilerParams(vmem_limit_bytes=KERNEL_VMEM),
        name="combine",
    )(source, own, skin, far, arrivals[1], arrivals[2], arrivals[3], jnp.asarray(expand_tables(E), jnp.bfloat16))
    fine_grad = fine.reshape(channels, 8, V).transpose(1, 0, 2)
    coarse_grad = coarse.reshape(channels, CB_DEV, LANES).transpose(1, 0, 2)
    return fine_grad, coarse_grad


def solution(mesh):
    in_specs = (
        P(None, ("brick", "tile")),
        P(("brick", "tile")),
        P(("brick", "tile")),
        P("brick", None),
    )
    out_specs = (P(("brick", "tile"), None, None), P("brick", None, "tile"))

    def step(sample_grad, sample_brick, sample_slot, neighbour):
        owners, tile_count = mesh.shape["brick"], mesh.shape["tile"]
        samples = sample_grad.shape[1] // (owners * tile_count)
        whole_family = FB_DEV == 8 * tile_count == 2 * 4 * CB_DEV and tile_count == CB_DEV
        full_messages = 2 * samples == (LANES // 2) * owners * tile_count and samples % LANES == 0
        fits = whole_family and full_messages and sample_grad.shape[0] == 28 and owners > 2
        if not fits:
            mapped = jax.shard_map(body, mesh=mesh, in_specs=in_specs, out_specs=out_specs, check_vma=False)
        else:
            mapped = jax.shard_map(family_body, mesh=mesh, in_specs=in_specs, out_specs=out_specs, check_vma=False)
        return mapped(sample_grad, sample_brick, sample_slot, neighbour)

    return step
```

```python
import functools

import jax
import jax.numpy as jnp
import numpy as np
from jax import lax
from jax.experimental import pallas as pl
from jax.experimental.pallas import tpu as pltpu
from jax.sharding import PartitionSpec as P


E = 8
V = 512
FACE = 64
CB_DEV = 4
FB_DEV = 32


row_block = 256


def extended_2(block, sides, width):
    for axis, dim in sides:
        count = lax.axis_size(axis)
        forward = [(i, i + 1) for i in range(count - 1)]
        forward.append((count - 1, 0))
        backward = [(target, source) for source, target in forward]
        low = lax.ppermute(
            lax.slice_in_dim(block, block.shape[dim] - width, None, axis=dim), axis, forward
        )
        high = lax.ppermute(lax.slice_in_dim(block, 0, width, axis=dim), axis, backward)
        block = jnp.concatenate([low, block, high], axis=dim)
    return block


def corners(fine_pos):
    is_even = fine_pos % 2 == 0
    lower_at = jnp.where(is_even, fine_pos // 2, fine_pos // 2 + 1)
    lower_w = jnp.where(is_even, 0.25, 0.75).astype(jnp.float32)
    return ((lower_at, lower_w), (lower_at + 1, 1.0 - lower_w))


def fold_column(pos_a, pos_b, pos_c, brick_edge):
    out_a = (pos_a == 0) | (pos_a == brick_edge + 1)
    out_b = (pos_b == 0) | (pos_b == brick_edge + 1)
    out_c = (pos_c == 0) | (pos_c == brick_edge + 1)
    outside = out_a.astype(jnp.int32) + out_b.astype(jnp.int32) + out_c.astype(jnp.int32)
    clamp_a = jnp.clip(pos_a, 1, brick_edge) - 1
    clamp_b = jnp.clip(pos_b, 1, brick_edge) - 1
    clamp_c = jnp.clip(pos_c, 1, brick_edge) - 1
    inner_col = clamp_a * brick_edge * brick_edge + clamp_b * brick_edge + clamp_c
    face_cells = brick_edge * brick_edge
    face_base = brick_edge**3
    face_a = (
        face_base
        + jnp.where(pos_a == 0, 0, 1) * face_cells
        + (pos_b - 1) * brick_edge
        + (pos_c - 1)
    )
    face_b = (
        face_base
        + (2 + jnp.where(pos_b == 0, 0, 1)) * face_cells
        + (pos_a - 1) * brick_edge
        + (pos_c - 1)
    )
    face_c = (
        face_base
        + (4 + jnp.where(pos_c == 0, 0, 1)) * face_cells
        + (pos_a - 1) * brick_edge
        + (pos_b - 1)
    )
    single = outside == 1
    return jnp.where(
        single & out_a,
        face_a,
        jnp.where(single & out_b, face_b, jnp.where(single & out_c, face_c, inner_col)),
    )


def child_matrix(child_id, row_count, brick_edge):
    slot_ids = jnp.arange(row_count, dtype=jnp.int32)
    coord_x = slot_ids // (brick_edge * brick_edge)
    coord_y = slot_ids // brick_edge % brick_edge
    coord_z = slot_ids % brick_edge
    fine_x = (child_id >> 2 & 1) * brick_edge + coord_x
    fine_y = (child_id >> 1 & 1) * brick_edge + coord_y
    fine_z = (child_id & 1) * brick_edge + coord_z
    column_total = brick_edge**3 + 6 * brick_edge * brick_edge
    column_ids = jnp.arange(column_total, dtype=jnp.int32)
    matrix = jnp.zeros((row_count, column_total), jnp.float32)
    for pos_a, weight_a in corners(fine_x):
        for pos_b, weight_b in corners(fine_y):
            for pos_c, weight_c in corners(fine_z):
                column = fold_column(pos_a, pos_b, pos_c, brick_edge)
                weight = weight_a * weight_b * weight_c
                matrix = matrix + jnp.where(
                    column[:, None] == column_ids[None, :], weight[:, None], 0.0
                )
    return matrix


def layer_matrix(brick_edge):
    grid_p, grid_q = np.meshgrid(np.arange(brick_edge), np.arange(brick_edge), indexing="ij")
    grid_p = grid_p.reshape(-1)
    grid_q = grid_q.reshape(-1)
    square = brick_edge * brick_edge
    last = brick_edge - 1
    layers = [
        grid_p * brick_edge + grid_q,
        last * square + grid_p * brick_edge + grid_q,
        grid_p * square + grid_q,
        grid_p * square + last * brick_edge + grid_q,
        grid_p * square + grid_q * brick_edge,
        grid_p * square + grid_q * brick_edge + last,
    ]
    cells = np.concatenate(layers)
    table = np.zeros((cells.shape[0], brick_edge**3), dtype=np.float32)
    table[np.arange(cells.shape[0]), cells] = 1.0
    return table


def rank_within(bucket_key):
    count = bucket_key.shape[0]
    order = jnp.arange(count, dtype=jnp.int32)
    earlier = (bucket_key[:, None] == bucket_key[None, :]) & (order[None, :] < order[:, None])
    return jnp.sum(earlier.astype(jnp.int32), axis=1)


def pack_rows(sample_grad, slot_code, bucket_at, slot_total):
    channels = sample_grad.shape[0]
    high_part = (slot_code // 128).astype(jnp.bfloat16)
    low_part = (slot_code % 128).astype(jnp.bfloat16)
    stacked = jnp.concatenate([sample_grad, high_part[None, :], low_part[None, :]], axis=0)
    hits = bucket_at[:, None] == jnp.arange(slot_total, dtype=jnp.int32)[None, :]
    placed = jnp.dot(stacked, hits.astype(jnp.bfloat16), preferred_element_type=jnp.float32)
    filled = jnp.any(hits, axis=0)
    high_row = jnp.where(filled, placed[channels], -1.0)
    moved = jnp.concatenate([placed[:channels], high_row[None, :], placed[channels + 1 :]], axis=0)
    return moved.astype(jnp.bfloat16)


def unpack_rows(arrived, channels):
    grad_rows = arrived[:channels]
    code_rows = arrived[channels].astype(jnp.int32) * 128 + arrived[channels + 1].astype(jnp.int32)
    return (grad_rows, code_rows)


def accumulate(grad_rows, code_rows, brick_count, slot_count):
    channels = grad_rows.shape[0]
    block_total = code_rows.shape[0] // row_block

    def add_block(block_id, running):
        start_row = block_id * row_block
        grad_part = lax.dynamic_slice_in_dim(grad_rows, start_row, row_block, 1)
        code_part = lax.dynamic_slice_in_dim(code_rows, start_row, row_block, 0)
        brick_part = jnp.where(code_part >= 0, code_part // slot_count, -1)
        slot_part = code_part % slot_count
        brick_hot = brick_part[None, :] == jnp.arange(brick_count, dtype=jnp.int32)[:, None]
        masked = jnp.where(brick_hot[:, None, :], grad_part[None, :, :], 0)
        slot_hot = (slot_part[:, None] == jnp.arange(slot_count, dtype=jnp.int32)[None, :]).astype(
            jnp.bfloat16
        )
        product = jnp.dot(
            masked.reshape(brick_count * channels, row_block),
            slot_hot,
            preferred_element_type=jnp.float32,
        )
        return running + product

    running = lax.fori_loop(
        0, block_total, add_block, jnp.zeros((brick_count * channels, slot_count), jnp.float32)
    )
    return running.reshape(brick_count, channels, slot_count)


def body(sample_grad, sample_brick, sample_slot, neighbour):
    tile_count = lax.axis_size("tile")
    owners = lax.axis_size("brick")
    tile_id = lax.axis_index("tile")
    brick_id = lax.axis_index("brick")
    samples = sample_brick.shape[0]
    channels = sample_grad.shape[0]
    capacity = 2 * samples // owners
    group_len = FB_DEV // tile_count
    group_cap = capacity // tile_count
    owner_of = sample_brick // FB_DEV
    local_brick = sample_brick - owner_of * FB_DEV
    group_of = local_brick // group_len
    bucket_key = owner_of * tile_count + group_of
    slot_code = (local_brick - group_of * group_len) * V + sample_slot
    bucket_at = bucket_key * group_cap + rank_within(bucket_key)
    packed = pack_rows(sample_grad, slot_code, bucket_at, owners * tile_count * group_cap)
    arrived = lax.all_to_all(
        lax.all_to_all(
            packed.reshape(channels + 2, owners, tile_count, group_cap),
            "brick",
            split_axis=1,
            concat_axis=1,
            tiled=True,
        ),
        "tile",
        split_axis=2,
        concat_axis=2,
        tiled=True,
    )
    grad_rows, code_rows = unpack_rows(
        arrived.reshape(channels + 2, owners * tile_count * group_cap), channels
    )
    fine_grad = accumulate(grad_rows, code_rows, group_len, V)
    family_count = max(group_len // 8, 1)
    first_fine = tile_id * group_len
    holder = jnp.zeros((family_count * 8, channels, V), jnp.float32)
    holder = lax.dynamic_update_slice_in_dim(holder, fine_grad, first_fine % (family_count * 8), 0)
    families = holder.reshape(family_count, 8, channels, V)
    part_padded = jnp.zeros((family_count, channels, V + 6 * FACE), jnp.float32)
    for child_id in range(8):
        matrix = child_matrix(child_id, V, E)
        part_padded = part_padded + jnp.einsum(
            "bcv,vo->bco", families[:, child_id], matrix, precision=lax.Precision.HIGHEST
        )
    padded = jnp.zeros((CB_DEV, channels, V + 6 * FACE), jnp.float32)
    padded = lax.dynamic_update_slice_in_dim(padded, part_padded, first_fine // 8, 0)
    face_skins = padded[:, :, V:]
    extended = extended_2(face_skins, (("brick", 0),), CB_DEV // 2)
    coarse_total = CB_DEV * owners
    offset = (neighbour - (brick_id * CB_DEV - CB_DEV // 2)) % coarse_total
    opposite = np.array([1, 0, 3, 2, 5, 4], dtype=np.int32)
    facing = extended.reshape(2 * CB_DEV, channels, 6, FACE)[:, :, opposite, :]
    selector = (
        offset[:, :, None] == jnp.arange(2 * CB_DEV, dtype=jnp.int32)[None, None, :]
    ).astype(jnp.float32)
    incoming = jnp.einsum("bke,eckf->bckf", selector, facing, precision=lax.Precision.HIGHEST)
    layer_table = jnp.asarray(layer_matrix(E))
    spread = jnp.einsum(
        "bcf,fv->bcv",
        incoming.reshape(CB_DEV, channels, 6 * FACE),
        layer_table,
        precision=lax.Precision.HIGHEST,
    )
    own_part = padded[:, :, :V] + spread
    coarse_grad = lax.psum_scatter(own_part, "tile", scatter_dimension=2, tiled=True)
    return (fine_grad, coarse_grad)


LANES = 128
KERNEL_VMEM = 16 * 1024 * 1024


def expand_tables(brick_edge):
    square = brick_edge * brick_edge
    last = brick_edge - 1
    out = np.zeros((2, LANES, LANES), np.float32)
    for side in range(2):
        for odd in range(2):
            for at in range(brick_edge):
                base = odd * 4 * brick_edge + at
                out[side, base, odd * square + last * brick_edge + at] = 1
                out[side, base + brick_edge, odd * square + at] = 1
                out[side, base + 2 * brick_edge, odd * square + at * brick_edge + last] = 1
                out[side, base + 3 * brick_edge, odd * square + at * brick_edge] = 1
        for cell in range(square):
            out[side, square + cell, side * square + cell] = 1
    return out


def split_two(value):
    high = value.astype(jnp.bfloat16)
    low = (value - high.astype(jnp.float32)).astype(jnp.bfloat16)
    return high, low


def contract_last(left, right):
    return lax.dot_general(left, right, (((1,), (1,)), ((), ())), preferred_element_type=jnp.float32)


def pack_kernel(group_len, partners, brick_hbm, slot_hbm, grad_hbm, out_ref, brick_ref, slot_ref, grad_ref, high_ref, sems):
    channels = grad_hbm.shape[0]
    blocks = brick_ref.shape[0]
    dests = len(partners)
    copies = [
        pltpu.make_async_copy(brick_hbm, brick_ref, sems.at[0]),
        pltpu.make_async_copy(slot_hbm, slot_ref, sems.at[1]),
        pltpu.make_async_copy(grad_hbm, grad_ref, sems.at[2]),
    ]
    for copy in copies:
        copy.start()
    at_row = lax.broadcasted_iota(jnp.int32, (LANES, 2 * LANES), 0)
    at_lane = lax.broadcasted_iota(jnp.int32, (LANES, 2 * LANES), 1)
    tri = jnp.where((at_row < at_lane) | (at_lane >= LANES), 1.0, 0.0).astype(jnp.bfloat16)
    copies[0].wait()
    copies[1].wait()
    brick = brick_ref[...]
    slot = slot_ref[...]
    bucket = brick // group_len
    local = brick - bucket * group_len
    coord_x = (local // 4) * E + slot // (E * E)
    coord_y = (local // 2 % 2) * E + slot // E % E
    coord_z = (local % 2) * E + slot % E
    bucket_f = bucket.astype(jnp.float32)
    dest_ids = lax.broadcasted_iota(jnp.int32, (dests, LANES), 0).astype(jnp.float32)
    hots = [
        jnp.where(jnp.broadcast_to(bucket_f[i : i + 1], (dests, LANES)) == dest_ids, 1.0, 0.0)
        for i in range(blocks)
    ]
    counts = jnp.dot(
        jnp.concatenate(hots, axis=0).astype(jnp.bfloat16), tri, preferred_element_type=jnp.float32
    )
    before = jnp.zeros((dests, LANES), jnp.float32)
    ranks = []
    for i in range(blocks):
        part = counts[i * dests : (i + 1) * dests]
        ranks.append(jnp.sum(hots[i] * (part[:, :LANES] + before), axis=0, keepdims=True))
        before = before + part[:, LANES:]
    rank = jnp.concatenate(ranks, axis=1)

    rows = lax.broadcasted_iota(jnp.int32, (4, LANES), 0)
    x_f = coord_x.astype(jnp.float32)
    y_f = coord_y.astype(jnp.float32)
    z_f = coord_z.astype(jnp.float32)
    for i in range(blocks):
        code = jnp.where(
            rows == 0,
            x_f[i : i + 1],
            jnp.where(rows == 1, y_f[i : i + 1], jnp.where(rows == 2, z_f[i : i + 1], 0.0)),
        )
        high_ref[channels - 16 : channels - 12, i * LANES : (i + 1) * LANES] = code.astype(jnp.bfloat16)
    copies[2].wait()
    high_ref[: channels - 16, :] = grad_ref[16:channels, :]
    low = grad_ref[:16, :]
    high = high_ref[...]
    bucket16 = jnp.concatenate(
        [jnp.broadcast_to(bucket_f[i : i + 1], (16, LANES)) for i in range(blocks)], axis=1
    ).astype(jnp.bfloat16)
    zero = jnp.zeros_like(low)
    low_rows = []
    high_rows = []
    for dest in range(dests):
        mask = bucket16 == jnp.bfloat16(dest)
        low_rows.append(jnp.where(mask, low, zero))
        high_rows.append(jnp.where(mask, high, zero))
    rank_ids = lax.broadcasted_iota(jnp.int32, (LANES, rank.shape[1]), 0).astype(jnp.float32)
    half = LANES // 2
    hot_low = jnp.where(rank_ids == rank, 1.0, 0.0).astype(jnp.bfloat16)
    hot_high = jnp.where(rank_ids == rank + half, 1.0, 0.0).astype(jnp.bfloat16)
    placed = contract_last(jnp.concatenate(low_rows, axis=0), hot_low)
    placed = placed + contract_last(jnp.concatenate(high_rows, axis=0), hot_high)
    placed = placed.astype(jnp.bfloat16).reshape(dests, 16, LANES)
    for dest in range(dests):
        out_ref[dest, 0] = placed[dest]
        out_ref[dest, 1] = placed[partners[dest]]


def unpack(arrived_ref, which, channels):
    half = LANES // 2
    pairs = arrived_ref.shape[0] // 2
    lows = []
    highs = []
    for p in range(pairs):
        first = arrived_ref[p, which]
        second = arrived_ref[p + pairs, which]
        lows.append(jnp.concatenate([first[:, :half], second[:, :half]], axis=1))
        highs.append(jnp.concatenate([first[:, half:], second[:, half:]], axis=1))
    low = jnp.concatenate(lows, axis=1)
    high = jnp.concatenate(highs, axis=1)
    codes = high.astype(jnp.float32)
    at = channels - 16
    coords = [
        jnp.broadcast_to(codes[at + k : at + k + 1], (16, low.shape[1])).astype(jnp.bfloat16) for k in range(3)
    ]
    return low, high, coords


def tent(halved, cell):
    return jnp.maximum(jnp.bfloat16(1.0) - jnp.abs(halved - (cell + jnp.bfloat16(0.25))), jnp.bfloat16(0.0))


def sample_weights(coords, with_own):
    x, y, z = coords
    shape = x.shape
    quarter = jnp.bfloat16(0.25)
    half = jnp.bfloat16(0.5)
    zero = jnp.zeros(shape, jnp.bfloat16)
    last = 2 * E - 1
    row = lax.broadcasted_iota(jnp.int32, shape, 0)
    upper = row >= E
    along = jnp.where(upper, row - E, row).astype(jnp.float32).astype(jnp.bfloat16)
    upper_f = jnp.where(upper, 1.0, 0.0).astype(jnp.bfloat16)
    ends = upper_f * jnp.bfloat16(last)
    x_half, y_half, z_half = x * half, y * half, z * half
    z_in = tent(z_half, along)
    y_in = tent(y_half, along)
    y_pair = [tent(y_half, upper_f + jnp.bfloat16(2 * g)) for g in range(E // 2)]
    x_in = [tent(x_half, jnp.bfloat16(m)) for m in range(E)]
    x_low = jnp.where(x == jnp.bfloat16(0), quarter, zero)
    x_high = jnp.where(x == jnp.bfloat16(last), quarter, zero)
    plane = [y_pair[g] * z_in for g in range(E // 2)]
    own = []
    if with_own:
        far = jnp.bfloat16(-1)
        z_ends = jnp.where(along == jnp.bfloat16(0), jnp.bfloat16(0), far)
        z_ends = jnp.where(along == jnp.bfloat16(E - 1), jnp.bfloat16(last), z_ends)
        z_out = jnp.where(z == z_ends, quarter, zero)
        y_first = jnp.where(y == jnp.where(upper_f == jnp.bfloat16(0), jnp.bfloat16(0), far), quarter, zero)
        y_last = jnp.where(y == jnp.where(upper_f == jnp.bfloat16(1), jnp.bfloat16(last), far), quarter, zero)
        z_both = z_in + z_out
        inner = list(plane)
        outer = [y_pair[g] * z_out for g in range(E // 2)]
        for g, y_out in ((0, y_first), (E // 2 - 1, y_last)):
            inner[g] = inner[g] + y_out * z_out
            outer[g] = outer[g] + y_out * z_both
        for m in range(E):
            for g in range(E // 2):
                value = x_in[m] * inner[g]
                if m == 0:
                    value = value + x_low * outer[g]
                if m == E - 1:
                    value = value + x_high * outer[g]
                own.append(value)
    y_face = jnp.where(y == ends, quarter, zero) * z_in
    z_face = jnp.where(z == ends, quarter, zero) * y_in
    skins = []
    for m in range(E):
        skins += [x_in[m] * y_face, x_in[m] * z_face]
    skins += [x_low * plane[g] for g in range(E // 2)]
    skins += [x_high * plane[g] for g in range(E // 2)]
    return own, skins


def skin_quarters(skins):
    half = LANES // 2
    lane = lax.broadcasted_iota(jnp.int32, (skins.shape[0], LANES), 1)
    left = lane < half
    parts = [skins[:, i * LANES : (i + 1) * LANES] for i in range(3)]
    turned = [jnp.concatenate([part[:, half:], part[:, :half]], axis=1) for part in parts]
    return [
        jnp.where(left, parts[0], parts[2]),
        jnp.where(left, turned[0], 0.0),
        jnp.where(left, parts[1], 0.0),
        jnp.where(left, turned[1], turned[2]),
    ]


def coarse_kernel(channels, arrived_ref, *refs):
    out_refs, quarter_ref = refs[:4], refs[4]
    tile_id = lax.axis_index("tile")
    for which in range(2):
        low, high, coords = unpack(arrived_ref, which, channels)
        values = jnp.concatenate([low, high], axis=0)
        own, skins = sample_weights(coords, which == 0)
        product = contract_last(values, jnp.concatenate(own + skins, axis=0))
        base = 16 * len(own)
        for q, skin in enumerate(skin_quarters(product[:, base:])):
            if which == 0:
                quarter_ref[q, 0] = product[:, q * LANES : (q + 1) * LANES]
            quarter_ref[q, 1 + which] = skin
    for delta in range(4):
        for part in range(3):
            out_refs[delta][part] = quarter_ref[tile_id ^ delta, part][:channels]


def fine_kernel(channels, coarse_total, arrived_ref, near_ref, fine_ref, source_ref, turn_ref):
    first = lax.axis_index("brick") * CB_DEV - CB_DEV // 2
    lane = lax.broadcasted_iota(jnp.int32, (8, LANES), 1)
    group = jnp.where(lane < LANES // 2, (lane // E) % 4, 4)
    x_face = jnp.where(lax.axis_index("tile") < 2, 0, 1)
    for i in range(CB_DEV):
        near = [(near_ref[i, face] - first + coarse_total) % coarse_total for face in (3, 2, 5, 4, x_face)]
        source = jnp.where(group == 0, near[0], near[1])
        for k in range(2, 5):
            source = jnp.where(group == k, near[k], source)
        source_ref[i] = source
    low, high, coords = unpack(arrived_ref, 0, channels)
    zero = jnp.zeros_like(low)
    one = jnp.ones_like(low)
    edge = jnp.bfloat16(E)
    halves = [jnp.where(c >= edge, one, zero) for c in coords]
    inside = [c - edge * h for c, h in zip(coords, halves)]
    child_at = halves[0] * jnp.bfloat16(4) + halves[1] * jnp.bfloat16(2) + halves[2]
    cell_at = inside[1] * edge + inside[2]
    left = []
    for child in range(8):
        mask = child_at == jnp.bfloat16(child)
        left.append(jnp.where(mask, low, zero))
        left.append(jnp.where(mask, high, zero))
    row_ids = lax.broadcasted_iota(jnp.int32, low.shape, 0).astype(jnp.float32)
    cells = [
        jnp.where(cell_at == (row_ids + 16.0 * g).astype(jnp.bfloat16), one, zero) for g in range(E * E // 16)
    ]
    right = []
    for plane in range(E):
        mask = inside[0] == jnp.bfloat16(plane)
        for g in range(E * E // 16):
            right.append(jnp.where(mask, cells[g], zero))
    fine = contract_last(jnp.concatenate(left, axis=0), jnp.concatenate(right, axis=0))
    for i in range(V // LANES):
        for child in range(8):
            turn_ref[i, pl.ds(child, channels, stride=8), :] = fine[
                32 * child : 32 * child + channels, i * LANES : (i + 1) * LANES
            ]
        fine_ref[:, i * LANES : (i + 1) * LANES] = turn_ref[i]


def combine_kernel(channels, source_ref, zero_ref, one_ref, two_ref, three_ref,
                   table_ref, out_ref, hold_ref):
    tile_id = lax.axis_index("tile")
    for delta, ref in enumerate((zero_ref, one_ref, two_ref, three_ref)):
        hold_ref[tile_id ^ delta] = ref[...]
    skins = [hold_ref[2, 2], hold_ref[3, 2]]
    skins += [hold_ref[j, 1] for j in range(4)]
    skins += [hold_ref[0, 2], hold_ref[1, 2]]
    gathered = []
    for i in range(4):
        source = jnp.broadcast_to(source_ref[i, :1], (channels, LANES))
        first = 0 if i < 2 else 4
        value = jnp.zeros((channels, LANES), jnp.float32)
        for e in range(first, first + 4):
            value = jnp.where(source == e, skins[e], value)
        gathered.append(value)
    table = table_ref[tile_id // 2]
    for i in range(4):
        high_part, low_part = split_two(gathered[i])
        moved = jnp.dot(high_part, table, preferred_element_type=jnp.float32) + jnp.dot(
            low_part, table, preferred_element_type=jnp.float32
        )
        out_ref[pl.ds(i, channels, stride=4), :] = hold_ref[i, 0] + moved


def family_body(sample_grad, sample_brick, sample_slot, neighbour):
    tile_count = lax.axis_size("tile")
    owners = lax.axis_size("brick")
    channels, samples = sample_grad.shape
    dests = owners * tile_count
    group_len = FB_DEV // tile_count
    vmem = pl.BlockSpec(memory_space=pltpu.VMEM)
    hbm = pl.BlockSpec(memory_space=pltpu.HBM)
    limit = pltpu.CompilerParams(vmem_limit_bytes=KERNEL_VMEM)
    partners = []
    for b in range(owners):
        for t in range(tile_count):
            step = -1 if t >= tile_count // 2 else 1
            partners.append((b + step) % owners * tile_count + t)
    inputs = (
        sample_brick.reshape(samples // LANES, LANES),
        sample_slot.reshape(samples // LANES, LANES),
        sample_grad,
    )
    packed = pl.pallas_call(
        functools.partial(pack_kernel, group_len, tuple(partners)),
        out_shape=jax.ShapeDtypeStruct((dests, 2, 16, LANES), jnp.bfloat16),
        in_specs=[hbm] * 3,
        out_specs=vmem,
        scratch_shapes=[
            pltpu.VMEM((samples // LANES, LANES), jnp.int32),
            pltpu.VMEM((samples // LANES, LANES), jnp.int32),
            pltpu.VMEM((channels, samples), jnp.bfloat16),
            pltpu.VMEM((16, samples), jnp.bfloat16),
            pltpu.SemaphoreType.DMA((3,)),
        ],
        compiler_params=limit,
        name="pack",
    )(*[pltpu.with_memory_space_constraint(value, pltpu.HBM) for value in inputs])
    arrived = lax.all_to_all(packed, ("brick", "tile"), 0, 0, tiled=True)
    message = jax.ShapeDtypeStruct((3, channels, LANES), jnp.float32)
    messages = pl.pallas_call(
        functools.partial(coarse_kernel, channels),
        out_shape=(message,) * 4,
        in_specs=[vmem],
        out_specs=(vmem,) * 4,
        scratch_shapes=[pltpu.VMEM((4, 3, 32, LANES), jnp.float32)],
        compiler_params=limit,
        name="coarse",
    )(arrived)
    arrivals = {}
    for delta in (3, 1, 2):
        arrivals[delta] = lax.ppermute(messages[delta], "tile", [(t, t ^ delta) for t in range(tile_count)])
    fine, source = pl.pallas_call(
        functools.partial(fine_kernel, channels, CB_DEV * owners),
        out_shape=(
            jax.ShapeDtypeStruct((channels * 8, V), jnp.float32),
            jax.ShapeDtypeStruct((CB_DEV, 8, LANES), jnp.int32),
        ),
        in_specs=[vmem, pl.BlockSpec(memory_space=pltpu.SMEM)],
        out_specs=(vmem, vmem),
        scratch_shapes=[pltpu.VMEM((V // LANES, channels * 8, LANES), jnp.float32)],
        compiler_params=limit,
        name="fine",
    )(arrived, neighbour)
    coarse = pl.pallas_call(
        functools.partial(combine_kernel, channels),
        out_shape=jax.ShapeDtypeStruct((channels * CB_DEV, LANES), jnp.float32),
        in_specs=[vmem] * 6,
        out_specs=vmem,
        scratch_shapes=[pltpu.VMEM((4, 3, channels, LANES), jnp.float32)],
        compiler_params=limit,
        name="combine",
    )(source, messages[0], arrivals[1], arrivals[2], arrivals[3], jnp.asarray(expand_tables(E), jnp.bfloat16))
    fine_grad = fine.reshape(channels, 8, V).transpose(1, 0, 2)
    coarse_grad = coarse.reshape(channels, CB_DEV, LANES).transpose(1, 0, 2)
    return fine_grad, coarse_grad


def solution(mesh):
    in_specs = (
        P(None, ("brick", "tile")),
        P(("brick", "tile")),
        P(("brick", "tile")),
        P("brick", None),
    )
    out_specs = (P(("brick", "tile"), None, None), P("brick", None, "tile"))

    def step(sample_grad, sample_brick, sample_slot, neighbour):
        owners, tile_count = mesh.shape["brick"], mesh.shape["tile"]
        samples = sample_grad.shape[1] // (owners * tile_count)
        whole_family = FB_DEV == 8 * tile_count == 2 * 4 * CB_DEV and tile_count == CB_DEV
        full_messages = 2 * samples == (LANES // 2) * owners * tile_count and samples % LANES == 0
        fits = whole_family and full_messages and sample_grad.shape[0] == 28 and owners > 2
        if not fits:
            mapped = jax.shard_map(body, mesh=mesh, in_specs=in_specs, out_specs=out_specs, check_vma=False)
        else:
            mapped = jax.shard_map(family_body, mesh=mesh, in_specs=in_specs, out_specs=out_specs, check_vma=False)
        return mapped(sample_grad, sample_brick, sample_slot, neighbour)

    return step
```

```python
import functools

import jax
import jax.numpy as jnp
import numpy as np
from jax import lax
from jax.experimental import pallas as pl
from jax.experimental.pallas import tpu as pltpu
from jax.sharding import PartitionSpec as P


E = 8
V = 512
FACE = 64
CB_DEV = 4
FB_DEV = 32


row_block = 256


def extended_2(block, sides, width):
    for axis, dim in sides:
        count = lax.axis_size(axis)
        forward = [(i, i + 1) for i in range(count - 1)]
        forward.append((count - 1, 0))
        backward = [(target, source) for source, target in forward]
        low = lax.ppermute(
            lax.slice_in_dim(block, block.shape[dim] - width, None, axis=dim), axis, forward
        )
        high = lax.ppermute(lax.slice_in_dim(block, 0, width, axis=dim), axis, backward)
        block = jnp.concatenate([low, block, high], axis=dim)
    return block


def corners(fine_pos):
    is_even = fine_pos % 2 == 0
    lower_at = jnp.where(is_even, fine_pos // 2, fine_pos // 2 + 1)
    lower_w = jnp.where(is_even, 0.25, 0.75).astype(jnp.float32)
    return ((lower_at, lower_w), (lower_at + 1, 1.0 - lower_w))


def fold_column(pos_a, pos_b, pos_c, brick_edge):
    out_a = (pos_a == 0) | (pos_a == brick_edge + 1)
    out_b = (pos_b == 0) | (pos_b == brick_edge + 1)
    out_c = (pos_c == 0) | (pos_c == brick_edge + 1)
    outside = out_a.astype(jnp.int32) + out_b.astype(jnp.int32) + out_c.astype(jnp.int32)
    clamp_a = jnp.clip(pos_a, 1, brick_edge) - 1
    clamp_b = jnp.clip(pos_b, 1, brick_edge) - 1
    clamp_c = jnp.clip(pos_c, 1, brick_edge) - 1
    inner_col = clamp_a * brick_edge * brick_edge + clamp_b * brick_edge + clamp_c
    face_cells = brick_edge * brick_edge
    face_base = brick_edge**3
    face_a = (
        face_base
        + jnp.where(pos_a == 0, 0, 1) * face_cells
        + (pos_b - 1) * brick_edge
        + (pos_c - 1)
    )
    face_b = (
        face_base
        + (2 + jnp.where(pos_b == 0, 0, 1)) * face_cells
        + (pos_a - 1) * brick_edge
        + (pos_c - 1)
    )
    face_c = (
        face_base
        + (4 + jnp.where(pos_c == 0, 0, 1)) * face_cells
        + (pos_a - 1) * brick_edge
        + (pos_b - 1)
    )
    single = outside == 1
    return jnp.where(
        single & out_a,
        face_a,
        jnp.where(single & out_b, face_b, jnp.where(single & out_c, face_c, inner_col)),
    )


def child_matrix(child_id, row_count, brick_edge):
    slot_ids = jnp.arange(row_count, dtype=jnp.int32)
    coord_x = slot_ids // (brick_edge * brick_edge)
    coord_y = slot_ids // brick_edge % brick_edge
    coord_z = slot_ids % brick_edge
    fine_x = (child_id >> 2 & 1) * brick_edge + coord_x
    fine_y = (child_id >> 1 & 1) * brick_edge + coord_y
    fine_z = (child_id & 1) * brick_edge + coord_z
    column_total = brick_edge**3 + 6 * brick_edge * brick_edge
    column_ids = jnp.arange(column_total, dtype=jnp.int32)
    matrix = jnp.zeros((row_count, column_total), jnp.float32)
    for pos_a, weight_a in corners(fine_x):
        for pos_b, weight_b in corners(fine_y):
            for pos_c, weight_c in corners(fine_z):
                column = fold_column(pos_a, pos_b, pos_c, brick_edge)
                weight = weight_a * weight_b * weight_c
                matrix = matrix + jnp.where(
                    column[:, None] == column_ids[None, :], weight[:, None], 0.0
                )
    return matrix


def layer_matrix(brick_edge):
    grid_p, grid_q = np.meshgrid(np.arange(brick_edge), np.arange(brick_edge), indexing="ij")
    grid_p = grid_p.reshape(-1)
    grid_q = grid_q.reshape(-1)
    square = brick_edge * brick_edge
    last = brick_edge - 1
    layers = [
        grid_p * brick_edge + grid_q,
        last * square + grid_p * brick_edge + grid_q,
        grid_p * square + grid_q,
        grid_p * square + last * brick_edge + grid_q,
        grid_p * square + grid_q * brick_edge,
        grid_p * square + grid_q * brick_edge + last,
    ]
    cells = np.concatenate(layers)
    table = np.zeros((cells.shape[0], brick_edge**3), dtype=np.float32)
    table[np.arange(cells.shape[0]), cells] = 1.0
    return table


def rank_within(bucket_key):
    count = bucket_key.shape[0]
    order = jnp.arange(count, dtype=jnp.int32)
    earlier = (bucket_key[:, None] == bucket_key[None, :]) & (order[None, :] < order[:, None])
    return jnp.sum(earlier.astype(jnp.int32), axis=1)


def pack_rows(sample_grad, slot_code, bucket_at, slot_total):
    channels = sample_grad.shape[0]
    high_part = (slot_code // 128).astype(jnp.bfloat16)
    low_part = (slot_code % 128).astype(jnp.bfloat16)
    stacked = jnp.concatenate([sample_grad, high_part[None, :], low_part[None, :]], axis=0)
    hits = bucket_at[:, None] == jnp.arange(slot_total, dtype=jnp.int32)[None, :]
    placed = jnp.dot(stacked, hits.astype(jnp.bfloat16), preferred_element_type=jnp.float32)
    filled = jnp.any(hits, axis=0)
    high_row = jnp.where(filled, placed[channels], -1.0)
    moved = jnp.concatenate([placed[:channels], high_row[None, :], placed[channels + 1 :]], axis=0)
    return moved.astype(jnp.bfloat16)


def unpack_rows(arrived, channels):
    grad_rows = arrived[:channels]
    code_rows = arrived[channels].astype(jnp.int32) * 128 + arrived[channels + 1].astype(jnp.int32)
    return (grad_rows, code_rows)


def accumulate(grad_rows, code_rows, brick_count, slot_count):
    channels = grad_rows.shape[0]
    block_total = code_rows.shape[0] // row_block

    def add_block(block_id, running):
        start_row = block_id * row_block
        grad_part = lax.dynamic_slice_in_dim(grad_rows, start_row, row_block, 1)
        code_part = lax.dynamic_slice_in_dim(code_rows, start_row, row_block, 0)
        brick_part = jnp.where(code_part >= 0, code_part // slot_count, -1)
        slot_part = code_part % slot_count
        brick_hot = brick_part[None, :] == jnp.arange(brick_count, dtype=jnp.int32)[:, None]
        masked = jnp.where(brick_hot[:, None, :], grad_part[None, :, :], 0)
        slot_hot = (slot_part[:, None] == jnp.arange(slot_count, dtype=jnp.int32)[None, :]).astype(
            jnp.bfloat16
        )
        product = jnp.dot(
            masked.reshape(brick_count * channels, row_block),
            slot_hot,
            preferred_element_type=jnp.float32,
        )
        return running + product

    running = lax.fori_loop(
        0, block_total, add_block, jnp.zeros((brick_count * channels, slot_count), jnp.float32)
    )
    return running.reshape(brick_count, channels, slot_count)


def body(sample_grad, sample_brick, sample_slot, neighbour):
    tile_count = lax.axis_size("tile")
    owners = lax.axis_size("brick")
    tile_id = lax.axis_index("tile")
    brick_id = lax.axis_index("brick")
    samples = sample_brick.shape[0]
    channels = sample_grad.shape[0]
    capacity = 2 * samples // owners
    group_len = FB_DEV // tile_count
    group_cap = capacity // tile_count
    owner_of = sample_brick // FB_DEV
    local_brick = sample_brick - owner_of * FB_DEV
    group_of = local_brick // group_len
    bucket_key = owner_of * tile_count + group_of
    slot_code = (local_brick - group_of * group_len) * V + sample_slot
    bucket_at = bucket_key * group_cap + rank_within(bucket_key)
    packed = pack_rows(sample_grad, slot_code, bucket_at, owners * tile_count * group_cap)
    arrived = lax.all_to_all(
        lax.all_to_all(
            packed.reshape(channels + 2, owners, tile_count, group_cap),
            "brick",
            split_axis=1,
            concat_axis=1,
            tiled=True,
        ),
        "tile",
        split_axis=2,
        concat_axis=2,
        tiled=True,
    )
    grad_rows, code_rows = unpack_rows(
        arrived.reshape(channels + 2, owners * tile_count * group_cap), channels
    )
    fine_grad = accumulate(grad_rows, code_rows, group_len, V)
    family_count = max(group_len // 8, 1)
    first_fine = tile_id * group_len
    holder = jnp.zeros((family_count * 8, channels, V), jnp.float32)
    holder = lax.dynamic_update_slice_in_dim(holder, fine_grad, first_fine % (family_count * 8), 0)
    families = holder.reshape(family_count, 8, channels, V)
    part_padded = jnp.zeros((family_count, channels, V + 6 * FACE), jnp.float32)
    for child_id in range(8):
        matrix = child_matrix(child_id, V, E)
        part_padded = part_padded + jnp.einsum(
            "bcv,vo->bco", families[:, child_id], matrix, precision=lax.Precision.HIGHEST
        )
    padded = jnp.zeros((CB_DEV, channels, V + 6 * FACE), jnp.float32)
    padded = lax.dynamic_update_slice_in_dim(padded, part_padded, first_fine // 8, 0)
    face_skins = padded[:, :, V:]
    extended = extended_2(face_skins, (("brick", 0),), CB_DEV // 2)
    coarse_total = CB_DEV * owners
    offset = (neighbour - (brick_id * CB_DEV - CB_DEV // 2)) % coarse_total
    opposite = np.array([1, 0, 3, 2, 5, 4], dtype=np.int32)
    facing = extended.reshape(2 * CB_DEV, channels, 6, FACE)[:, :, opposite, :]
    selector = (
        offset[:, :, None] == jnp.arange(2 * CB_DEV, dtype=jnp.int32)[None, None, :]
    ).astype(jnp.float32)
    incoming = jnp.einsum("bke,eckf->bckf", selector, facing, precision=lax.Precision.HIGHEST)
    layer_table = jnp.asarray(layer_matrix(E))
    spread = jnp.einsum(
        "bcf,fv->bcv",
        incoming.reshape(CB_DEV, channels, 6 * FACE),
        layer_table,
        precision=lax.Precision.HIGHEST,
    )
    own_part = padded[:, :, :V] + spread
    coarse_grad = lax.psum_scatter(own_part, "tile", scatter_dimension=2, tiled=True)
    return (fine_grad, coarse_grad)


LANES = 128
KERNEL_VMEM = 16 * 1024 * 1024


def expand_tables(brick_edge):
    square = brick_edge * brick_edge
    last = brick_edge - 1
    out = np.zeros((2, LANES, LANES), np.float32)
    for side in range(2):
        for odd in range(2):
            for at in range(brick_edge):
                base = odd * brick_edge + at
                out[side, base, odd * square + last * brick_edge + at] = 1
                out[side, base + 2 * brick_edge, odd * square + at] = 1
                out[side, base + 4 * brick_edge, odd * square + at * brick_edge + last] = 1
                out[side, base + 6 * brick_edge, odd * square + at * brick_edge] = 1
        for cell in range(square):
            out[side, square + cell, side * square + cell] = 1
    return out


def split_two(value):
    high = value.astype(jnp.bfloat16)
    low = (value - high.astype(jnp.float32)).astype(jnp.bfloat16)
    return high, low


def contract_last(left, right):
    return lax.dot_general(left, right, (((1,), (1,)), ((), ())), preferred_element_type=jnp.float32)


def pack_kernel(group_len, tile_count, partners, brick_hbm, slot_hbm, grad_hbm, out_ref, brick_ref, slot_ref, grad_ref, high_ref, sems):
    channels = grad_hbm.shape[0]
    blocks = brick_ref.shape[0]
    dests = len(partners)
    copies = [
        pltpu.make_async_copy(brick_hbm, brick_ref, sems.at[0]),
        pltpu.make_async_copy(slot_hbm, slot_ref, sems.at[1]),
        pltpu.make_async_copy(grad_hbm, grad_ref, sems.at[2]),
    ]
    for copy in copies:
        copy.start()
    at_row = lax.broadcasted_iota(jnp.int32, (LANES, 2 * LANES), 0)
    at_lane = lax.broadcasted_iota(jnp.int32, (LANES, 2 * LANES), 1)
    tri = jnp.where((at_row < at_lane) | (at_lane >= LANES), 1.0, 0.0).astype(jnp.bfloat16)
    copies[0].wait()
    copies[1].wait()
    brick = brick_ref[...]
    slot = slot_ref[...]
    bucket = brick // group_len
    local = brick - bucket * group_len
    coord_x = (local // 4) * E + slot // (E * E)
    coord_y = (local // 2 % 2) * E + slot // E % E
    coord_z = (local % 2) * E + slot % E
    bucket_f = bucket.astype(jnp.float32)
    dest_ids = lax.broadcasted_iota(jnp.int32, (dests, LANES), 0).astype(jnp.float32)
    hots = [
        jnp.where(jnp.broadcast_to(bucket_f[i : i + 1], (dests, LANES)) == dest_ids, 1.0, 0.0)
        for i in range(blocks)
    ]
    counts = jnp.dot(
        jnp.concatenate(hots, axis=0).astype(jnp.bfloat16), tri, preferred_element_type=jnp.float32
    )
    before = jnp.zeros((dests, LANES), jnp.float32)
    ranks = []
    for i in range(blocks):
        part = counts[i * dests : (i + 1) * dests]
        ranks.append(jnp.sum(hots[i] * (part[:, :LANES] + before), axis=0, keepdims=True))
        before = before + part[:, LANES:]
    rank = jnp.concatenate(ranks, axis=1)

    rows = lax.broadcasted_iota(jnp.int32, (4, LANES), 0)
    x_f = coord_x.astype(jnp.float32)
    y_f = coord_y.astype(jnp.float32)
    z_f = coord_z.astype(jnp.float32)
    for i in range(blocks):
        code = jnp.where(
            rows == 0,
            x_f[i : i + 1],
            jnp.where(rows == 1, y_f[i : i + 1], jnp.where(rows == 2, z_f[i : i + 1], 0.0)),
        )
        high_ref[channels - 16 : channels - 12, i * LANES : (i + 1) * LANES] = code.astype(jnp.bfloat16)
    copies[2].wait()
    high_ref[: channels - 16, :] = grad_ref[16:channels, :]
    low = grad_ref[:16, :]
    high = high_ref[...]

    def spread(value):
        return jnp.concatenate(
            [jnp.broadcast_to(value[i : i + 1], (16, LANES)) for i in range(blocks)], axis=1
        ).astype(jnp.bfloat16)

    owner16 = spread((bucket // tile_count).astype(jnp.float32))
    tile16 = spread((bucket % tile_count).astype(jnp.float32))
    zero = jnp.zeros_like(low)
    left = []
    for owner in range(dests // tile_count):
        mask = owner16 == jnp.bfloat16(owner)
        left += [jnp.where(mask, low, zero), jnp.where(mask, high, zero)]
    half = LANES // 2
    rank16 = jnp.broadcast_to(rank, (16, rank.shape[1])).astype(jnp.bfloat16)
    row_ids = lax.broadcasted_iota(jnp.int32, rank16.shape, 0).astype(jnp.float32)
    ones = jnp.ones_like(low)
    hot = [
        jnp.where(rank16 == (row_ids + 16.0 * g).astype(jnp.bfloat16), ones, zero) for g in range(half // 16)
    ]
    right = []
    for tile in range(tile_count):
        mask = tile16 == jnp.bfloat16(tile)
        right += [jnp.where(mask, value, zero) for value in hot]
    placed = contract_last(jnp.concatenate(left, axis=0), jnp.concatenate(right, axis=0)).astype(jnp.bfloat16)
    tiles = []
    for owner in range(dests // tile_count):
        for pair in range(tile_count // 2):
            low_part = placed[32 * owner : 32 * owner + 16, pair * LANES : (pair + 1) * LANES]
            high_part = placed[32 * owner + 16 : 32 * owner + 32, pair * LANES : (pair + 1) * LANES]
            tiles.append(jnp.concatenate([low_part[:, :half], high_part[:, :half]], axis=1))
            tiles.append(jnp.concatenate([low_part[:, half:], high_part[:, half:]], axis=1))
    for dest in range(dests):
        out_ref[dest, 0] = tiles[dest]
        out_ref[dest, 1] = tiles[partners[dest]]


def unpack(arrived_ref, which, channels):
    half = LANES // 2
    pairs = arrived_ref.shape[0] // 2
    lows = []
    highs = []
    for p in range(pairs):
        first = arrived_ref[p, which]
        second = arrived_ref[p + pairs, which]
        lows.append(jnp.concatenate([first[:, :half], second[:, :half]], axis=1))
        highs.append(jnp.concatenate([first[:, half:], second[:, half:]], axis=1))
    low = jnp.concatenate(lows, axis=1)
    high = jnp.concatenate(highs, axis=1)
    codes = high.astype(jnp.float32)
    at = channels - 16
    coords = [
        jnp.broadcast_to(codes[at + k : at + k + 1], (16, low.shape[1])).astype(jnp.bfloat16) for k in range(3)
    ]
    return low, high, coords


def pack_pair(first, second):
    return jnp.concatenate([first, second], axis=0).astype(jnp.bfloat16)


def block_axes(code, axis_ref):
    row = lax.broadcasted_iota(jnp.int32, (8, LANES), 0).astype(jnp.float32)
    axis_ref[0] = code
    coords = [axis_ref[0, pl.ds(at, 8, stride=0), :] for at in (4, 5, 6)]
    rows = [jnp.maximum(1.0 - jnp.abs(c * 0.5 - (row + 0.25)), 0.0) for c in coords]
    return row, coords, rows


def paired(axis_ref, at, rows):
    axis_ref[at] = rows
    lines = [axis_ref[at, pl.ds(m, 8, stride=0), :] for m in range(E)]
    return [pack_pair(lines[2 * g], lines[2 * g + 1]) for g in range(E // 2)]


def select_rows(hits, low, high):
    zero = jnp.zeros_like(low)
    rows = []
    for hit in hits:
        rows += [jnp.where(hit, low, zero), jnp.where(hit, high, zero)]
    return rows


def own_block(code, axis_ref, low, high):
    row, (x, y, z), (_, y_rows, z_rows) = block_axes(code, axis_ref)
    last = 2.0 * E - 1.0
    blank = jnp.zeros((8, LANES), jnp.float32)
    y_pair = paired(axis_ref, 2, y_rows)
    z_in = pack_pair(z_rows, z_rows)
    y_low = jnp.where(y == 0.0, 0.25, 0.0)
    y_high = jnp.where(y == last, 0.25, 0.0)
    z_low = jnp.where(z == 0.0, 0.25, 0.0)
    z_high = jnp.where(z == last, 0.25, 0.0)
    z_out = jnp.where(row == 0.0, z_low, jnp.where(row == E - 1.0, z_high, blank))
    z_out = pack_pair(z_out, z_out)
    z_both = z_in + z_out
    plane = [y_pair[g] * z_in for g in range(E // 2)]
    inner = list(plane)
    outer = [y_pair[g] * z_out for g in range(E // 2)]
    for g, y_out in ((0, pack_pair(y_low, blank)), (E // 2 - 1, pack_pair(blank, y_high))):
        inner[g] = inner[g] + y_out * z_out
        outer[g] = outer[g] + y_out * z_both
    faces = [y_low * z_rows, y_high * z_rows, z_low * y_rows, z_high * y_rows]
    x16 = pack_pair(x, x)
    left = select_rows([x16 == jnp.bfloat16(at) for at in range(2 * E)], low, high)
    return left, inner + [pack_pair(face, blank) for face in faces], outer + plane


def skin_block(code, axis_ref, low, high):
    _, coords, (x_rows, y_rows, z_rows) = block_axes(code, axis_ref)
    last = 2 * E - 1
    x_pair = paired(axis_ref, 1, x_rows)
    y_pair = paired(axis_ref, 2, y_rows)
    z_in = pack_pair(z_rows, z_rows)
    y_in = pack_pair(y_rows, y_rows)
    x16, y16, z16 = [pack_pair(c, c) for c in coords]
    hits = [c == jnp.bfloat16(end) for c in (y16, z16, x16) for end in (0, last)]
    left = select_rows(hits, low, high)
    right = [value * z_in for value in x_pair] + [value * y_in for value in x_pair]
    return left, right + [value * z_in for value in y_pair]


def lay_out(blocks):
    return jnp.concatenate(
        [jnp.concatenate([block[i] for block in blocks], axis=1) for i in range(len(blocks[0]))], axis=0
    )


def own_quarters(product, folds):
    half = LANES // 2
    lane = lax.broadcasted_iota(jnp.int32, (32, LANES), 1)
    left = lane < half
    at_x = [product[32 * at : 32 * at + 32] for at in range(2 * E)]
    first, second = 0.25 * folds[:32], 0.25 * folds[32:]
    layers = []
    for m in range(E):
        value = 0.75 * (at_x[2 * m] + at_x[2 * m + 1])
        if m == 0:
            value = value + 0.25 * at_x[2] + jnp.where(left, first, 0.0)
        elif m == E - 1:
            value = value + 0.25 * at_x[2 * m - 1] + jnp.where(left, second, 0.0)
        else:
            value = value + 0.25 * (at_x[2 * m - 1] + at_x[2 * m + 2])
        layers.append(value)
    quarters = []
    for q in range(E // 2):
        even, odd = layers[2 * q], layers[2 * q + 1]
        faces = pltpu.roll(even, half, 1) + pltpu.roll(jnp.where(left, 0.0, odd), half + E, 1)
        beyond = second if q == 0 else first if q == E // 2 - 1 else jnp.zeros_like(even)
        quarters.append((jnp.where(left, even, pltpu.roll(odd, half, 1)), jnp.where(left, faces, beyond)))
    return quarters


def skin_quarters(product):
    half = LANES // 2
    lane = lax.broadcasted_iota(jnp.int32, (32, LANES), 1)
    sides = [0.25 * product[32 * f : 32 * f + 32, :LANES] for f in range(4)]
    ends = []
    for f in (4, 5):
        end = 0.25 * product[32 * f : 32 * f + 32, LANES:]
        ends.append(jnp.concatenate([end, end], axis=1))
    quarters = []
    for q in range(E // 2):
        beyond = ends[1] if q == 0 else ends[0] if q == E // 2 - 1 else jnp.zeros_like(sides[0])
        value = beyond
        for f in range(4):
            shift = (2 * E * f - 2 * E * q - (half if f >= 2 else 0)) % LANES
            moved = pltpu.roll(sides[f], shift, 1) if shift else sides[f]
            value = jnp.where((lane >= 2 * E * f) & (lane < 2 * E * (f + 1)), moved, value)
        quarters.append(value)
    return quarters


def coarse_kernel(channels, arrived_ref, *refs):
    out_refs, quarter_ref, axis_ref = refs[:4], refs[4], refs[5]
    tile_id = lax.axis_index("tile")
    half = LANES // 2
    pairs = arrived_ref.shape[0] // 2

    def blocks(which, make):
        made = []
        for p in range(pairs):
            first = arrived_ref[p, which]
            second = arrived_ref[p + pairs, which]
            low = jnp.concatenate([first[:, :half], second[:, :half]], axis=1)
            high = jnp.concatenate([first[:, half:], second[:, half:]], axis=1)
            made.append(make(high.astype(jnp.float32)[8:], axis_ref.at[which, p], low, high))
        return [[block[i] for block in made] for i in range(len(made[0]))]

    left, right, folds = blocks(0, own_block)
    product = contract_last(lay_out(left), lay_out(right))
    ends = [block[:2] + block[-2:] for block in left]
    folded = contract_last(lay_out(ends), lay_out(folds))
    for q, (own, skin) in enumerate(own_quarters(product, folded)):
        quarter_ref[q, 0] = own
        quarter_ref[q, 1] = skin
    left, right = blocks(1, skin_block)
    for q, skin in enumerate(skin_quarters(contract_last(lay_out(left), lay_out(right)))):
        quarter_ref[q, 2] = skin
    for delta in range(4):
        for part in range(3):
            out_refs[delta][part] = quarter_ref[tile_id ^ delta, part][:channels]


def fine_kernel(channels, coarse_total, arrived_ref, near_ref, fine_ref, source_ref, turn_ref):
    first = lax.axis_index("brick") * CB_DEV - CB_DEV // 2
    lane = lax.broadcasted_iota(jnp.int32, (8, LANES), 1)
    group = jnp.minimum(lane // (2 * E), 4)
    x_face = jnp.where(lax.axis_index("tile") < 2, 0, 1)
    for i in range(CB_DEV):
        near = [(near_ref[i, face] - first + coarse_total) % coarse_total for face in (3, 2, 5, 4, x_face)]
        source = jnp.where(group == 0, near[0], near[1])
        for k in range(2, 5):
            source = jnp.where(group == k, near[k], source)
        source_ref[i] = source
    low, high, coords = unpack(arrived_ref, 0, channels)
    zero = jnp.zeros_like(low)
    one = jnp.ones_like(low)
    edge = jnp.bfloat16(E)
    halves = [jnp.where(c >= edge, one, zero) for c in coords]
    inside = [c - edge * h for c, h in zip(coords, halves)]
    child_at = halves[0] * jnp.bfloat16(4) + halves[1] * jnp.bfloat16(2) + halves[2]
    cell_at = inside[1] * edge + inside[2]
    left = []
    for child in range(8):
        mask = child_at == jnp.bfloat16(child)
        left.append(jnp.where(mask, low, zero))
        left.append(jnp.where(mask, high, zero))
    row_ids = lax.broadcasted_iota(jnp.int32, low.shape, 0).astype(jnp.float32)
    cells = [
        jnp.where(cell_at == (row_ids + 16.0 * g).astype(jnp.bfloat16), one, zero) for g in range(E * E // 16)
    ]
    right = []
    for plane in range(E):
        mask = inside[0] == jnp.bfloat16(plane)
        for g in range(E * E // 16):
            right.append(jnp.where(mask, cells[g], zero))
    fine = contract_last(jnp.concatenate(left, axis=0), jnp.concatenate(right, axis=0))
    for i in range(V // LANES):
        for child in range(8):
            turn_ref[i, pl.ds(child, channels, stride=8), :] = fine[
                32 * child : 32 * child + channels, i * LANES : (i + 1) * LANES
            ]
        fine_ref[:, i * LANES : (i + 1) * LANES] = turn_ref[i]


def combine_kernel(channels, source_ref, zero_ref, one_ref, two_ref, three_ref,
                   table_ref, out_ref, hold_ref):
    tile_id = lax.axis_index("tile")
    for delta, ref in enumerate((zero_ref, one_ref, two_ref, three_ref)):
        hold_ref[tile_id ^ delta] = ref[...]
    skins = [hold_ref[2, 2], hold_ref[3, 2]]
    skins += [hold_ref[j, 1] for j in range(4)]
    skins += [hold_ref[0, 2], hold_ref[1, 2]]
    gathered = []
    for i in range(4):
        source = jnp.broadcast_to(source_ref[i, :1], (channels, LANES))
        first = 0 if i < 2 else 4
        value = jnp.zeros((channels, LANES), jnp.float32)
        for e in range(first, first + 4):
            value = jnp.where(source == e, skins[e], value)
        gathered.append(value)
    table = table_ref[tile_id // 2]
    for i in range(4):
        high_part, low_part = split_two(gathered[i])
        moved = jnp.dot(high_part, table, preferred_element_type=jnp.float32) + jnp.dot(
            low_part, table, preferred_element_type=jnp.float32
        )
        out_ref[pl.ds(i, channels, stride=4), :] = hold_ref[i, 0] + moved


def family_body(sample_grad, sample_brick, sample_slot, neighbour):
    tile_count = lax.axis_size("tile")
    owners = lax.axis_size("brick")
    channels, samples = sample_grad.shape
    dests = owners * tile_count
    group_len = FB_DEV // tile_count
    vmem = pl.BlockSpec(memory_space=pltpu.VMEM)
    hbm = pl.BlockSpec(memory_space=pltpu.HBM)
    limit = pltpu.CompilerParams(vmem_limit_bytes=KERNEL_VMEM)
    partners = []
    for b in range(owners):
        for t in range(tile_count):
            step = -1 if t >= tile_count // 2 else 1
            partners.append((b + step) % owners * tile_count + t)
    inputs = (
        sample_brick.reshape(samples // LANES, LANES),
        sample_slot.reshape(samples // LANES, LANES),
        sample_grad,
    )
    packed = pl.pallas_call(
        functools.partial(pack_kernel, group_len, tile_count, tuple(partners)),
        out_shape=jax.ShapeDtypeStruct((dests, 2, 16, LANES), jnp.bfloat16),
        in_specs=[hbm] * 3,
        out_specs=vmem,
        scratch_shapes=[
            pltpu.VMEM((samples // LANES, LANES), jnp.int32),
            pltpu.VMEM((samples // LANES, LANES), jnp.int32),
            pltpu.VMEM((channels, samples), jnp.bfloat16),
            pltpu.VMEM((16, samples), jnp.bfloat16),
            pltpu.SemaphoreType.DMA((3,)),
        ],
        compiler_params=limit,
        name="pack",
    )(*[pltpu.with_memory_space_constraint(value, pltpu.HBM) for value in inputs])
    arrived = lax.all_to_all(packed, ("brick", "tile"), 0, 0, tiled=True)
    message = jax.ShapeDtypeStruct((3, channels, LANES), jnp.float32)
    messages = pl.pallas_call(
        functools.partial(coarse_kernel, channels),
        out_shape=(message,) * 4,
        in_specs=[vmem],
        out_specs=(vmem,) * 4,
        scratch_shapes=[
            pltpu.VMEM((4, 3, 32, LANES), jnp.float32),
            pltpu.VMEM((2, dests // 2, 3, 8, LANES), jnp.float32),
        ],
        compiler_params=limit,
        name="coarse",
    )(arrived)
    arrivals = {}
    for delta in (3, 1, 2):
        arrivals[delta] = lax.ppermute(messages[delta], "tile", [(t, t ^ delta) for t in range(tile_count)])
    fine, source = pl.pallas_call(
        functools.partial(fine_kernel, channels, CB_DEV * owners),
        out_shape=(
            jax.ShapeDtypeStruct((channels * 8, V), jnp.float32),
            jax.ShapeDtypeStruct((CB_DEV, 8, LANES), jnp.int32),
        ),
        in_specs=[vmem, pl.BlockSpec(memory_space=pltpu.SMEM)],
        out_specs=(vmem, vmem),
        scratch_shapes=[pltpu.VMEM((V // LANES, channels * 8, LANES), jnp.float32)],
        compiler_params=limit,
        name="fine",
    )(arrived, neighbour)
    coarse = pl.pallas_call(
        functools.partial(combine_kernel, channels),
        out_shape=jax.ShapeDtypeStruct((channels * CB_DEV, LANES), jnp.float32),
        in_specs=[vmem] * 6,
        out_specs=vmem,
        scratch_shapes=[pltpu.VMEM((4, 3, channels, LANES), jnp.float32)],
        compiler_params=limit,
        name="combine",
    )(source, messages[0], arrivals[1], arrivals[2], arrivals[3], jnp.asarray(expand_tables(E), jnp.bfloat16))
    fine_grad = fine.reshape(channels, 8, V).transpose(1, 0, 2)
    coarse_grad = coarse.reshape(channels, CB_DEV, LANES).transpose(1, 0, 2)
    return fine_grad, coarse_grad


def solution(mesh):
    in_specs = (
        P(None, ("brick", "tile")),
        P(("brick", "tile")),
        P(("brick", "tile")),
        P("brick", None),
    )
    out_specs = (P(("brick", "tile"), None, None), P("brick", None, "tile"))

    def step(sample_grad, sample_brick, sample_slot, neighbour):
        owners, tile_count = mesh.shape["brick"], mesh.shape["tile"]
        samples = sample_grad.shape[1] // (owners * tile_count)
        whole_family = FB_DEV == 8 * tile_count == 2 * 4 * CB_DEV and tile_count == CB_DEV
        full_messages = 2 * samples == (LANES // 2) * owners * tile_count and samples % LANES == 0
        fits = whole_family and full_messages and sample_grad.shape[0] == 28 and owners > 2
        if not fits:
            mapped = jax.shard_map(body, mesh=mesh, in_specs=in_specs, out_specs=out_specs, check_vma=False)
        else:
            mapped = jax.shard_map(family_body, mesh=mesh, in_specs=in_specs, out_specs=out_specs, check_vma=False)
        return mapped(sample_grad, sample_brick, sample_slot, neighbour)

    return step
```

```python
import functools

import jax
import jax.numpy as jnp
import numpy as np
from jax import lax
from jax.experimental import pallas as pl
from jax.experimental.pallas import tpu as pltpu
from jax.sharding import PartitionSpec as P


E = 8
V = 512
FACE = 64
CB_DEV = 4
FB_DEV = 32


row_block = 256


def extended_2(block, sides, width):
    for axis, dim in sides:
        count = lax.axis_size(axis)
        forward = [(i, i + 1) for i in range(count - 1)]
        forward.append((count - 1, 0))
        backward = [(target, source) for source, target in forward]
        low = lax.ppermute(
            lax.slice_in_dim(block, block.shape[dim] - width, None, axis=dim), axis, forward
        )
        high = lax.ppermute(lax.slice_in_dim(block, 0, width, axis=dim), axis, backward)
        block = jnp.concatenate([low, block, high], axis=dim)
    return block


def corners(fine_pos):
    is_even = fine_pos % 2 == 0
    lower_at = jnp.where(is_even, fine_pos // 2, fine_pos // 2 + 1)
    lower_w = jnp.where(is_even, 0.25, 0.75).astype(jnp.float32)
    return ((lower_at, lower_w), (lower_at + 1, 1.0 - lower_w))


def fold_column(pos_a, pos_b, pos_c, brick_edge):
    out_a = (pos_a == 0) | (pos_a == brick_edge + 1)
    out_b = (pos_b == 0) | (pos_b == brick_edge + 1)
    out_c = (pos_c == 0) | (pos_c == brick_edge + 1)
    outside = out_a.astype(jnp.int32) + out_b.astype(jnp.int32) + out_c.astype(jnp.int32)
    clamp_a = jnp.clip(pos_a, 1, brick_edge) - 1
    clamp_b = jnp.clip(pos_b, 1, brick_edge) - 1
    clamp_c = jnp.clip(pos_c, 1, brick_edge) - 1
    inner_col = clamp_a * brick_edge * brick_edge + clamp_b * brick_edge + clamp_c
    face_cells = brick_edge * brick_edge
    face_base = brick_edge**3
    face_a = (
        face_base
        + jnp.where(pos_a == 0, 0, 1) * face_cells
        + (pos_b - 1) * brick_edge
        + (pos_c - 1)
    )
    face_b = (
        face_base
        + (2 + jnp.where(pos_b == 0, 0, 1)) * face_cells
        + (pos_a - 1) * brick_edge
        + (pos_c - 1)
    )
    face_c = (
        face_base
        + (4 + jnp.where(pos_c == 0, 0, 1)) * face_cells
        + (pos_a - 1) * brick_edge
        + (pos_b - 1)
    )
    single = outside == 1
    return jnp.where(
        single & out_a,
        face_a,
        jnp.where(single & out_b, face_b, jnp.where(single & out_c, face_c, inner_col)),
    )


def child_matrix(child_id, row_count, brick_edge):
    slot_ids = jnp.arange(row_count, dtype=jnp.int32)
    coord_x = slot_ids // (brick_edge * brick_edge)
    coord_y = slot_ids // brick_edge % brick_edge
    coord_z = slot_ids % brick_edge
    fine_x = (child_id >> 2 & 1) * brick_edge + coord_x
    fine_y = (child_id >> 1 & 1) * brick_edge + coord_y
    fine_z = (child_id & 1) * brick_edge + coord_z
    column_total = brick_edge**3 + 6 * brick_edge * brick_edge
    column_ids = jnp.arange(column_total, dtype=jnp.int32)
    matrix = jnp.zeros((row_count, column_total), jnp.float32)
    for pos_a, weight_a in corners(fine_x):
        for pos_b, weight_b in corners(fine_y):
            for pos_c, weight_c in corners(fine_z):
                column = fold_column(pos_a, pos_b, pos_c, brick_edge)
                weight = weight_a * weight_b * weight_c
                matrix = matrix + jnp.where(
                    column[:, None] == column_ids[None, :], weight[:, None], 0.0
                )
    return matrix


def layer_matrix(brick_edge):
    grid_p, grid_q = np.meshgrid(np.arange(brick_edge), np.arange(brick_edge), indexing="ij")
    grid_p = grid_p.reshape(-1)
    grid_q = grid_q.reshape(-1)
    square = brick_edge * brick_edge
    last = brick_edge - 1
    layers = [
        grid_p * brick_edge + grid_q,
        last * square + grid_p * brick_edge + grid_q,
        grid_p * square + grid_q,
        grid_p * square + last * brick_edge + grid_q,
        grid_p * square + grid_q * brick_edge,
        grid_p * square + grid_q * brick_edge + last,
    ]
    cells = np.concatenate(layers)
    table = np.zeros((cells.shape[0], brick_edge**3), dtype=np.float32)
    table[np.arange(cells.shape[0]), cells] = 1.0
    return table


def rank_within(bucket_key):
    count = bucket_key.shape[0]
    order = jnp.arange(count, dtype=jnp.int32)
    earlier = (bucket_key[:, None] == bucket_key[None, :]) & (order[None, :] < order[:, None])
    return jnp.sum(earlier.astype(jnp.int32), axis=1)


def pack_rows(sample_grad, slot_code, bucket_at, slot_total):
    channels = sample_grad.shape[0]
    high_part = (slot_code // 128).astype(jnp.bfloat16)
    low_part = (slot_code % 128).astype(jnp.bfloat16)
    stacked = jnp.concatenate([sample_grad, high_part[None, :], low_part[None, :]], axis=0)
    hits = bucket_at[:, None] == jnp.arange(slot_total, dtype=jnp.int32)[None, :]
    placed = jnp.dot(stacked, hits.astype(jnp.bfloat16), preferred_element_type=jnp.float32)
    filled = jnp.any(hits, axis=0)
    high_row = jnp.where(filled, placed[channels], -1.0)
    moved = jnp.concatenate([placed[:channels], high_row[None, :], placed[channels + 1 :]], axis=0)
    return moved.astype(jnp.bfloat16)


def unpack_rows(arrived, channels):
    grad_rows = arrived[:channels]
    code_rows = arrived[channels].astype(jnp.int32) * 128 + arrived[channels + 1].astype(jnp.int32)
    return (grad_rows, code_rows)


def accumulate(grad_rows, code_rows, brick_count, slot_count):
    channels = grad_rows.shape[0]
    block_total = code_rows.shape[0] // row_block

    def add_block(block_id, running):
        start_row = block_id * row_block
        grad_part = lax.dynamic_slice_in_dim(grad_rows, start_row, row_block, 1)
        code_part = lax.dynamic_slice_in_dim(code_rows, start_row, row_block, 0)
        brick_part = jnp.where(code_part >= 0, code_part // slot_count, -1)
        slot_part = code_part % slot_count
        brick_hot = brick_part[None, :] == jnp.arange(brick_count, dtype=jnp.int32)[:, None]
        masked = jnp.where(brick_hot[:, None, :], grad_part[None, :, :], 0)
        slot_hot = (slot_part[:, None] == jnp.arange(slot_count, dtype=jnp.int32)[None, :]).astype(
            jnp.bfloat16
        )
        product = jnp.dot(
            masked.reshape(brick_count * channels, row_block),
            slot_hot,
            preferred_element_type=jnp.float32,
        )
        return running + product

    running = lax.fori_loop(
        0, block_total, add_block, jnp.zeros((brick_count * channels, slot_count), jnp.float32)
    )
    return running.reshape(brick_count, channels, slot_count)


def body(sample_grad, sample_brick, sample_slot, neighbour):
    tile_count = lax.axis_size("tile")
    owners = lax.axis_size("brick")
    tile_id = lax.axis_index("tile")
    brick_id = lax.axis_index("brick")
    samples = sample_brick.shape[0]
    channels = sample_grad.shape[0]
    capacity = 2 * samples // owners
    group_len = FB_DEV // tile_count
    group_cap = capacity // tile_count
    owner_of = sample_brick // FB_DEV
    local_brick = sample_brick - owner_of * FB_DEV
    group_of = local_brick // group_len
    bucket_key = owner_of * tile_count + group_of
    slot_code = (local_brick - group_of * group_len) * V + sample_slot
    bucket_at = bucket_key * group_cap + rank_within(bucket_key)
    packed = pack_rows(sample_grad, slot_code, bucket_at, owners * tile_count * group_cap)
    arrived = lax.all_to_all(
        lax.all_to_all(
            packed.reshape(channels + 2, owners, tile_count, group_cap),
            "brick",
            split_axis=1,
            concat_axis=1,
            tiled=True,
        ),
        "tile",
        split_axis=2,
        concat_axis=2,
        tiled=True,
    )
    grad_rows, code_rows = unpack_rows(
        arrived.reshape(channels + 2, owners * tile_count * group_cap), channels
    )
    fine_grad = accumulate(grad_rows, code_rows, group_len, V)
    family_count = max(group_len // 8, 1)
    first_fine = tile_id * group_len
    holder = jnp.zeros((family_count * 8, channels, V), jnp.float32)
    holder = lax.dynamic_update_slice_in_dim(holder, fine_grad, first_fine % (family_count * 8), 0)
    families = holder.reshape(family_count, 8, channels, V)
    part_padded = jnp.zeros((family_count, channels, V + 6 * FACE), jnp.float32)
    for child_id in range(8):
        matrix = child_matrix(child_id, V, E)
        part_padded = part_padded + jnp.einsum(
            "bcv,vo->bco", families[:, child_id], matrix, precision=lax.Precision.HIGHEST
        )
    padded = jnp.zeros((CB_DEV, channels, V + 6 * FACE), jnp.float32)
    padded = lax.dynamic_update_slice_in_dim(padded, part_padded, first_fine // 8, 0)
    face_skins = padded[:, :, V:]
    extended = extended_2(face_skins, (("brick", 0),), CB_DEV // 2)
    coarse_total = CB_DEV * owners
    offset = (neighbour - (brick_id * CB_DEV - CB_DEV // 2)) % coarse_total
    opposite = np.array([1, 0, 3, 2, 5, 4], dtype=np.int32)
    facing = extended.reshape(2 * CB_DEV, channels, 6, FACE)[:, :, opposite, :]
    selector = (
        offset[:, :, None] == jnp.arange(2 * CB_DEV, dtype=jnp.int32)[None, None, :]
    ).astype(jnp.float32)
    incoming = jnp.einsum("bke,eckf->bckf", selector, facing, precision=lax.Precision.HIGHEST)
    layer_table = jnp.asarray(layer_matrix(E))
    spread = jnp.einsum(
        "bcf,fv->bcv",
        incoming.reshape(CB_DEV, channels, 6 * FACE),
        layer_table,
        precision=lax.Precision.HIGHEST,
    )
    own_part = padded[:, :, :V] + spread
    coarse_grad = lax.psum_scatter(own_part, "tile", scatter_dimension=2, tiled=True)
    return (fine_grad, coarse_grad)


LANES = 128
KERNEL_VMEM = 16 * 1024 * 1024


def expand_tables(brick_edge):
    square = brick_edge * brick_edge
    last = brick_edge - 1
    out = np.zeros((2, LANES, LANES), np.float32)
    for side in range(2):
        for odd in range(2):
            for at in range(brick_edge):
                base = odd * 4 * brick_edge + at
                out[side, base, odd * square + last * brick_edge + at] = 1
                out[side, base + brick_edge, odd * square + at] = 1
                out[side, base + 2 * brick_edge, odd * square + at * brick_edge + last] = 1
                out[side, base + 3 * brick_edge, odd * square + at * brick_edge] = 1
        for cell in range(square):
            out[side, square + cell, side * square + cell] = 1
    return out


def fold_table(brick_edge):
    square = brick_edge * brick_edge
    last = brick_edge - 1
    base = square
    out = np.zeros((LANES, 2 * LANES), np.float32)
    for at in range(brick_edge):
        targets = [(at, at), (brick_edge + at, last * brick_edge + at)]
        if 0 < at < last:
            targets += [(2 * brick_edge + at, at * brick_edge), (3 * brick_edge + at, at * brick_edge + last)]
        else:
            out[base + 2 * brick_edge + at, LANES + square + at * brick_edge] = -1
            out[base + 3 * brick_edge + at, LANES + square + at * brick_edge + last] = -1
        for source, cell in targets:
            out[base + source, cell] = 1
            out[base + source, square + cell] = 1
    return out


def split_two(value):
    high = value.astype(jnp.bfloat16)
    low = (value - high.astype(jnp.float32)).astype(jnp.bfloat16)
    return high, low


def contract_last(left, right):
    return lax.dot_general(left, right, (((1,), (1,)), ((), ())), preferred_element_type=jnp.float32)


def pack_kernel(group_len, tile_count, partners, brick_hbm, slot_hbm, grad_hbm, out_ref, brick_ref, slot_ref, grad_ref, high_ref, sems):
    channels = grad_hbm.shape[0]
    blocks = brick_ref.shape[0]
    dests = len(partners)
    copies = [
        pltpu.make_async_copy(brick_hbm, brick_ref, sems.at[0]),
        pltpu.make_async_copy(slot_hbm, slot_ref, sems.at[1]),
        pltpu.make_async_copy(grad_hbm, grad_ref, sems.at[2]),
    ]
    for copy in copies:
        copy.start()
    at_row = lax.broadcasted_iota(jnp.int32, (LANES, 2 * LANES), 0)
    at_lane = lax.broadcasted_iota(jnp.int32, (LANES, 2 * LANES), 1)
    tri = jnp.where((at_row < at_lane) | (at_lane >= LANES), 1.0, 0.0).astype(jnp.bfloat16)
    copies[0].wait()
    copies[1].wait()
    brick = brick_ref[...]
    slot = slot_ref[...]
    bucket = brick // group_len
    local = brick - bucket * group_len
    coord_x = (local // 4) * E + slot // (E * E)
    coord_y = (local // 2 % 2) * E + slot // E % E
    coord_z = (local % 2) * E + slot % E
    bucket_f = bucket.astype(jnp.float32)
    dest_ids = lax.broadcasted_iota(jnp.int32, (dests, LANES), 0).astype(jnp.float32)
    hots = [
        jnp.where(jnp.broadcast_to(bucket_f[i : i + 1], (dests, LANES)) == dest_ids, 1.0, 0.0)
        for i in range(blocks)
    ]
    counts = jnp.dot(
        jnp.concatenate(hots, axis=0).astype(jnp.bfloat16), tri, preferred_element_type=jnp.float32
    )
    before = jnp.zeros((dests, LANES), jnp.float32)
    ranks = []
    for i in range(blocks):
        part = counts[i * dests : (i + 1) * dests]
        ranks.append(jnp.sum(hots[i] * (part[:, :LANES] + before), axis=0, keepdims=True))
        before = before + part[:, LANES:]
    rank = jnp.concatenate(ranks, axis=1)

    rows = lax.broadcasted_iota(jnp.int32, (4, LANES), 0)
    x_f = coord_x.astype(jnp.float32)
    y_f = coord_y.astype(jnp.float32)
    z_f = coord_z.astype(jnp.float32)
    for i in range(blocks):
        code = jnp.where(
            rows == 0,
            x_f[i : i + 1],
            jnp.where(rows == 1, y_f[i : i + 1], jnp.where(rows == 2, z_f[i : i + 1], 0.0)),
        )
        high_ref[channels - 16 : channels - 12, i * LANES : (i + 1) * LANES] = code.astype(jnp.bfloat16)
    copies[2].wait()
    high_ref[: channels - 16, :] = grad_ref[16:channels, :]
    low = grad_ref[:16, :]
    high = high_ref[...]

    def spread(value):
        return jnp.concatenate(
            [jnp.broadcast_to(value[i : i + 1], (16, LANES)) for i in range(blocks)], axis=1
        ).astype(jnp.bfloat16)

    owner16 = spread((bucket // tile_count).astype(jnp.float32))
    tile16 = spread((bucket % tile_count).astype(jnp.float32))
    zero = jnp.zeros_like(low)
    left = []
    for owner in range(dests // tile_count):
        mask = owner16 == jnp.bfloat16(owner)
        left += [jnp.where(mask, low, zero), jnp.where(mask, high, zero)]
    half = LANES // 2
    rank16 = jnp.broadcast_to(rank, (16, rank.shape[1])).astype(jnp.bfloat16)
    row_ids = lax.broadcasted_iota(jnp.int32, rank16.shape, 0).astype(jnp.float32)
    ones = jnp.ones_like(low)
    hot = [
        jnp.where(rank16 == (row_ids + 16.0 * g).astype(jnp.bfloat16), ones, zero) for g in range(half // 16)
    ]
    right = []
    for tile in range(tile_count):
        mask = tile16 == jnp.bfloat16(tile)
        right += [jnp.where(mask, value, zero) for value in hot]
    placed = contract_last(jnp.concatenate(left, axis=0), jnp.concatenate(right, axis=0)).astype(jnp.bfloat16)
    tiles = []
    for owner in range(dests // tile_count):
        for pair in range(tile_count // 2):
            low_part = placed[32 * owner : 32 * owner + 16, pair * LANES : (pair + 1) * LANES]
            high_part = placed[32 * owner + 16 : 32 * owner + 32, pair * LANES : (pair + 1) * LANES]
            tiles.append(jnp.concatenate([low_part[:, :half], high_part[:, :half]], axis=1))
            tiles.append(jnp.concatenate([low_part[:, half:], high_part[:, half:]], axis=1))
    for dest in range(dests):
        out_ref[dest, 0] = tiles[dest]
        out_ref[dest, 1] = tiles[partners[dest]]


def unpack(arrived_ref, which, channels):
    half = LANES // 2
    pairs = arrived_ref.shape[0] // 2
    lows = []
    highs = []
    for p in range(pairs):
        first = arrived_ref[p, which]
        second = arrived_ref[p + pairs, which]
        lows.append(jnp.concatenate([first[:, :half], second[:, :half]], axis=1))
        highs.append(jnp.concatenate([first[:, half:], second[:, half:]], axis=1))
    low = jnp.concatenate(lows, axis=1)
    high = jnp.concatenate(highs, axis=1)
    codes = high.astype(jnp.float32)
    at = channels - 16
    coords = [
        jnp.broadcast_to(codes[at + k : at + k + 1], (16, low.shape[1])).astype(jnp.bfloat16) for k in range(3)
    ]
    return low, high, coords


def pack_pair(first, second):
    return jnp.concatenate([first, second], axis=0).astype(jnp.bfloat16)


def block_axes(code, axis_ref):
    row = lax.broadcasted_iota(jnp.int32, (8, LANES), 0).astype(jnp.float32)
    axis_ref[0] = code
    coords = [axis_ref[0, pl.ds(at, 8, stride=0), :] for at in (4, 5, 6)]
    rows = [jnp.maximum(1.0 - jnp.abs(c * 0.5 - (row + 0.25)), 0.0) for c in coords]
    return row, coords, rows


def lines_of(axis_ref, at, rows):
    axis_ref[at] = rows
    return [axis_ref[at, pl.ds(m, 8, stride=0), :] for m in range(E)]


def select_rows(hits, low, high):
    zero = jnp.zeros_like(low)
    rows = []
    for hit in hits:
        rows += [jnp.where(hit, low, zero), jnp.where(hit, high, zero)]
    return rows


def own_block(code, axis_ref, low, high):
    row, (x, y, z), (_, y_rows, z_rows) = block_axes(code, axis_ref)
    last = 2.0 * E - 1.0
    blank = jnp.zeros((8, LANES), jnp.float32)
    y_lines = lines_of(axis_ref, 2, y_rows)
    y_pair = [pack_pair(y_lines[2 * g], y_lines[2 * g + 1]) for g in range(E // 2)]
    z_in = pack_pair(z_rows, z_rows)
    y_low = jnp.where(y == 0.0, 0.25, 0.0)
    y_high = jnp.where(y == last, 0.25, 0.0)
    z_low = jnp.where(z == 0.0, 0.25, 0.0)
    z_high = jnp.where(z == last, 0.25, 0.0)
    z_out = jnp.where(row == 0.0, z_low, jnp.where(row == E - 1.0, z_high, blank))
    y_edge = jnp.where(row == 0.0, y_low, jnp.where(row == E - 1.0, y_high, y_rows))
    z_both = z_rows + z_out
    inner = [value * z_in for value in y_pair]
    inner[0] = inner[0] + pack_pair(y_low * z_out, blank)
    inner[-1] = inner[-1] + pack_pair(blank, y_high * z_out)
    faces = [pack_pair(y_low * z_rows, y_high * z_rows), pack_pair(z_low * y_rows, z_high * y_rows)]
    edges = [
        pack_pair(y_lines[0] * z_out + y_low * z_both, y_lines[E - 1] * z_out + y_high * z_both),
        pack_pair(y_edge * z_low, y_edge * z_high),
    ]
    whole = x.astype(jnp.int32)
    pair_of = (whole >> 1).astype(jnp.float32)
    odd = (whole & 1).astype(jnp.float32)
    odd16 = pack_pair(odd, odd)
    even16 = jnp.bfloat16(1.0) - odd16
    ends = jnp.where((x == 0.0) | (x == last), 1.0, 0.0)
    ends16 = pack_pair(ends, ends)
    pair16 = pack_pair(pair_of, pair_of)
    left = select_rows([pair16 == jnp.bfloat16(at) for at in range(E)], low, high)
    right = [value * even16 for value in inner] + [value * odd16 for value in inner]
    right += [value * even16 for value in faces] + [value * odd16 for value in faces]
    return left, right + [value * ends16 for value in edges]


def skin_block(code, axis_ref, low, high):
    _, coords, (x_rows, y_rows, z_rows) = block_axes(code, axis_ref)
    last = 2 * E - 1
    x_lines = lines_of(axis_ref, 1, x_rows)
    y_lines = lines_of(axis_ref, 2, y_rows)
    x_order = list(range(0, E, 2)) + list(range(1, E, 2))
    x_pair = [pack_pair(x_lines[x_order[2 * g]], x_lines[x_order[2 * g + 1]]) for g in range(E // 2)]
    y_pair = [pack_pair(y_lines[2 * g], y_lines[2 * g + 1]) for g in range(E // 2)]
    z_in = pack_pair(z_rows, z_rows)
    y_in = pack_pair(y_rows, y_rows)
    x16, y16, z16 = [pack_pair(c, c) for c in coords]
    hits = [c == jnp.bfloat16(end) for c in (y16, z16, x16) for end in (0, last)]
    left = select_rows(hits, low, high)
    right = [value * z_in for value in x_pair] + [value * y_in for value in x_pair]
    return left, right + [value * z_in for value in y_pair]


def lay_out(blocks):
    return jnp.concatenate(
        [jnp.concatenate([block[i] for block in blocks], axis=1) for i in range(len(blocks[0]))], axis=0
    )


def own_quarters(product, table):
    half = LANES // 2
    width = half // 2
    lane = lax.broadcasted_iota(jnp.int32, (32, LANES), 1)
    left = lane < half
    blank = jnp.zeros((32, LANES - product.shape[1] % LANES), jnp.float32)
    cells = [product[32 * i : 32 * i + 32, :LANES] for i in range(E)]
    faces = [jnp.concatenate([product[32 * i : 32 * i + 32, LANES:], blank], axis=1) for i in range(E)]
    high_part, low_part = split_two(jnp.concatenate([faces[0], faces[-1]], axis=0))
    folds = jnp.dot(high_part, table, preferred_element_type=jnp.float32)
    folds = 0.25 * (folds + jnp.dot(low_part, table, preferred_element_type=jnp.float32))
    cells_turned = [pltpu.roll(value, half, 1) for value in cells]
    faces_turned = [pltpu.roll(value, LANES - width, 1) for value in faces]

    def mixed(m, even, odd):
        near = [odd[m - 1]] if m > 0 else []
        near += [even[m + 1]] if m < E - 1 else []
        return 0.75 * (even[m] + odd[m]) + 0.25 * (near[0] if len(near) == 1 else near[0] + near[1])

    quarters = []
    for q in range(E // 2):
        first = mixed(2 * q, cells, cells_turned)
        second = mixed(2 * q + 1, cells_turned, cells)
        beyond = jnp.zeros_like(first)
        if q == 0:
            first = first + folds[:32, :LANES]
            beyond = 0.25 * cells[-1] + folds[32:, LANES:]
        if q == E // 2 - 1:
            second = second + folds[32:, :LANES]
            beyond = 0.25 * cells_turned[0] + folds[:32, LANES:]
        side = pltpu.roll(mixed(2 * q + 1, faces, faces_turned), width, 1)
        skin = jnp.where(lane < width, mixed(2 * q, faces, faces_turned), jnp.where(left, side, beyond))
        quarters.append((jnp.where(left, first, second), skin))
    return quarters


def skin_quarters(product):
    half = LANES // 2
    lane = lax.broadcasted_iota(jnp.int32, (32, LANES), 1)
    face_of = jnp.where(lane < half, (lane // E) % 4, 4)
    sides = [0.25 * product[32 * f : 32 * f + 32, :LANES] for f in range(4)]
    ends = []
    for f in (4, 5):
        end = 0.25 * product[32 * f : 32 * f + 32, LANES:]
        ends.append(jnp.concatenate([end, end], axis=1))
    quarters = []
    for q in range(E // 2):
        value = ends[1] if q == 0 else ends[0] if q == E // 2 - 1 else jnp.zeros_like(sides[0])
        for f in range(4):
            shift = (E * (f - q) - (half if f >= 2 else 0)) % LANES
            moved = pltpu.roll(sides[f], shift, 1) if shift else sides[f]
            value = jnp.where(face_of == f, moved, value)
        quarters.append(value)
    return quarters


def coarse_kernel(channels, arrived_ref, table_hbm, *refs):
    out_refs, (quarter_ref, axis_ref, table_ref, sem) = refs[:4], refs[4:]
    table_copy = pltpu.make_async_copy(table_hbm, table_ref, sem)
    table_copy.start()
    tile_id = lax.axis_index("tile")
    half = LANES // 2
    pairs = arrived_ref.shape[0] // 2

    def blocks(which, make):
        made = []
        for p in range(pairs):
            first = arrived_ref[p, which]
            second = arrived_ref[p + pairs, which]
            low = jnp.concatenate([first[:, :half], second[:, :half]], axis=1)
            high = jnp.concatenate([first[:, half:], second[:, half:]], axis=1)
            made.append(make(high.astype(jnp.float32)[8:], axis_ref.at[which, p], low, high))
        return [[block[i] for block in made] for i in range(len(made[0]))]

    def in_halves(left, right):
        middle = pairs // 2
        return contract_last(lay_out(left[:middle]), lay_out(right[:middle])) + contract_last(
            lay_out(left[middle:]), lay_out(right[middle:])
        )

    skin_product = in_halves(*blocks(1, skin_block))
    own_product = in_halves(*blocks(0, own_block))
    for q, skin in enumerate(skin_quarters(skin_product)):
        quarter_ref[q, 2] = skin
    table_copy.wait()
    for q, (own, skin) in enumerate(own_quarters(own_product, table_ref[...])):
        quarter_ref[q, 0] = own
        quarter_ref[q, 1] = skin
    for delta in range(4):
        for part in range(3):
            out_refs[delta][part] = quarter_ref[tile_id ^ delta, part][:channels]


def fine_kernel(channels, coarse_total, arrived_ref, near_ref, fine_ref, source_ref, turn_ref):
    first = lax.axis_index("brick") * CB_DEV - CB_DEV // 2
    lane = lax.broadcasted_iota(jnp.int32, (8, LANES), 1)
    group = jnp.where(lane < LANES // 2, (lane // E) % 4, 4)
    x_face = jnp.where(lax.axis_index("tile") < 2, 0, 1)
    for i in range(CB_DEV):
        near = [(near_ref[i, face] - first + coarse_total) % coarse_total for face in (3, 2, 5, 4, x_face)]
        source = jnp.where(group == 0, near[0], near[1])
        for k in range(2, 5):
            source = jnp.where(group == k, near[k], source)
        source_ref[i] = source
    low, high, coords = unpack(arrived_ref, 0, channels)
    zero = jnp.zeros_like(low)
    one = jnp.ones_like(low)
    edge = jnp.bfloat16(E)
    halves = [jnp.where(c >= edge, one, zero) for c in coords]
    inside = [c - edge * h for c, h in zip(coords, halves)]
    child_at = halves[0] * jnp.bfloat16(4) + halves[1] * jnp.bfloat16(2) + halves[2]
    cell_at = inside[1] * edge + inside[2]
    left = []
    for child in range(8):
        mask = child_at == jnp.bfloat16(child)
        left.append(jnp.where(mask, low, zero))
        left.append(jnp.where(mask, high, zero))
    row_ids = lax.broadcasted_iota(jnp.int32, low.shape, 0).astype(jnp.float32)
    cells = [
        jnp.where(cell_at == (row_ids + 16.0 * g).astype(jnp.bfloat16), one, zero) for g in range(E * E // 16)
    ]
    right = []
    for plane in range(E):
        mask = inside[0] == jnp.bfloat16(plane)
        for g in range(E * E // 16):
            right.append(jnp.where(mask, cells[g], zero))
    fine = contract_last(jnp.concatenate(left, axis=0), jnp.concatenate(right, axis=0))
    for i in range(V // LANES):
        for child in range(8):
            turn_ref[i, pl.ds(child, channels, stride=8), :] = fine[
                32 * child : 32 * child + channels, i * LANES : (i + 1) * LANES
            ]
        fine_ref[:, i * LANES : (i + 1) * LANES] = turn_ref[i]


def combine_kernel(channels, source_ref, zero_ref, one_ref, two_ref, three_ref,
                   table_ref, out_ref, hold_ref):
    tile_id = lax.axis_index("tile")
    for delta, ref in enumerate((zero_ref, one_ref, two_ref, three_ref)):
        hold_ref[tile_id ^ delta] = ref[...]
    skins = [hold_ref[2, 2], hold_ref[3, 2]]
    skins += [hold_ref[j, 1] for j in range(4)]
    skins += [hold_ref[0, 2], hold_ref[1, 2]]
    gathered = []
    for i in range(4):
        source = jnp.broadcast_to(source_ref[i, :1], (channels, LANES))
        first = 0 if i < 2 else 4
        value = jnp.zeros((channels, LANES), jnp.float32)
        for e in range(first, first + 4):
            value = jnp.where(source == e, skins[e], value)
        gathered.append(value)
    table = table_ref[tile_id // 2]
    for i in range(4):
        high_part, low_part = split_two(gathered[i])
        moved = jnp.dot(high_part, table, preferred_element_type=jnp.float32) + jnp.dot(
            low_part, table, preferred_element_type=jnp.float32
        )
        out_ref[pl.ds(i, channels, stride=4), :] = hold_ref[i, 0] + moved


def family_body(sample_grad, sample_brick, sample_slot, neighbour):
    tile_count = lax.axis_size("tile")
    owners = lax.axis_size("brick")
    channels, samples = sample_grad.shape
    dests = owners * tile_count
    group_len = FB_DEV // tile_count
    vmem = pl.BlockSpec(memory_space=pltpu.VMEM)
    hbm = pl.BlockSpec(memory_space=pltpu.HBM)
    limit = pltpu.CompilerParams(vmem_limit_bytes=KERNEL_VMEM)
    partners = []
    for b in range(owners):
        for t in range(tile_count):
            step = -1 if t >= tile_count // 2 else 1
            partners.append((b + step) % owners * tile_count + t)
    inputs = (
        sample_brick.reshape(samples // LANES, LANES),
        sample_slot.reshape(samples // LANES, LANES),
        sample_grad,
    )
    packed = pl.pallas_call(
        functools.partial(pack_kernel, group_len, tile_count, tuple(partners)),
        out_shape=jax.ShapeDtypeStruct((dests, 2, 16, LANES), jnp.bfloat16),
        in_specs=[hbm] * 3,
        out_specs=vmem,
        scratch_shapes=[
            pltpu.VMEM((samples // LANES, LANES), jnp.int32),
            pltpu.VMEM((samples // LANES, LANES), jnp.int32),
            pltpu.VMEM((channels, samples), jnp.bfloat16),
            pltpu.VMEM((16, samples), jnp.bfloat16),
            pltpu.SemaphoreType.DMA((3,)),
        ],
        compiler_params=limit,
        name="pack",
    )(*[pltpu.with_memory_space_constraint(value, pltpu.HBM) for value in inputs])
    arrived = lax.all_to_all(packed, ("brick", "tile"), 0, 0, tiled=True)
    message = jax.ShapeDtypeStruct((3, channels, LANES), jnp.float32)
    messages = pl.pallas_call(
        functools.partial(coarse_kernel, channels),
        out_shape=(message,) * 4,
        in_specs=[vmem, hbm],
        out_specs=(vmem,) * 4,
        scratch_shapes=[
            pltpu.VMEM((4, 3, 32, LANES), jnp.float32),
            pltpu.VMEM((2, dests // 2, 3, 8, LANES), jnp.float32),
            pltpu.VMEM((LANES, 2 * LANES), jnp.bfloat16),
            pltpu.SemaphoreType.DMA,
        ],
        compiler_params=limit,
        name="coarse",
    )(arrived, pltpu.with_memory_space_constraint(jnp.asarray(fold_table(E), jnp.bfloat16), pltpu.HBM))
    arrivals = {}
    for delta in (3, 1, 2):
        arrivals[delta] = lax.ppermute(messages[delta], "tile", [(t, t ^ delta) for t in range(tile_count)])
    fine, source = pl.pallas_call(
        functools.partial(fine_kernel, channels, CB_DEV * owners),
        out_shape=(
            jax.ShapeDtypeStruct((channels * 8, V), jnp.float32),
            jax.ShapeDtypeStruct((CB_DEV, 8, LANES), jnp.int32),
        ),
        in_specs=[vmem, pl.BlockSpec(memory_space=pltpu.SMEM)],
        out_specs=(vmem, vmem),
        scratch_shapes=[pltpu.VMEM((V // LANES, channels * 8, LANES), jnp.float32)],
        compiler_params=limit,
        name="fine",
    )(arrived, neighbour)
    coarse = pl.pallas_call(
        functools.partial(combine_kernel, channels),
        out_shape=jax.ShapeDtypeStruct((channels * CB_DEV, LANES), jnp.float32),
        in_specs=[vmem] * 6,
        out_specs=vmem,
        scratch_shapes=[pltpu.VMEM((4, 3, channels, LANES), jnp.float32)],
        compiler_params=limit,
        name="combine",
    )(source, messages[0], arrivals[1], arrivals[2], arrivals[3], jnp.asarray(expand_tables(E), jnp.bfloat16))
    fine_grad = fine.reshape(channels, 8, V).transpose(1, 0, 2)
    coarse_grad = coarse.reshape(channels, CB_DEV, LANES).transpose(1, 0, 2)
    return fine_grad, coarse_grad


def solution(mesh):
    in_specs = (
        P(None, ("brick", "tile")),
        P(("brick", "tile")),
        P(("brick", "tile")),
        P("brick", None),
    )
    out_specs = (P(("brick", "tile"), None, None), P("brick", None, "tile"))

    def step(sample_grad, sample_brick, sample_slot, neighbour):
        owners, tile_count = mesh.shape["brick"], mesh.shape["tile"]
        samples = sample_grad.shape[1] // (owners * tile_count)
        whole_family = FB_DEV == 8 * tile_count == 2 * 4 * CB_DEV and tile_count == CB_DEV
        full_messages = 2 * samples == (LANES // 2) * owners * tile_count and samples % LANES == 0
        fits = whole_family and full_messages and sample_grad.shape[0] == 28 and owners > 2
        if not fits:
            mapped = jax.shard_map(body, mesh=mesh, in_specs=in_specs, out_specs=out_specs, check_vma=False)
        else:
            mapped = jax.shard_map(family_body, mesh=mesh, in_specs=in_specs, out_specs=out_specs, check_vma=False)
        return mapped(sample_grad, sample_brick, sample_slot, neighbour)

    return step
```

```python
import functools

import jax
import jax.numpy as jnp
import numpy as np
from jax import lax
from jax.experimental import pallas as pl
from jax.experimental.pallas import tpu as pltpu
from jax.sharding import PartitionSpec as P


E = 8
V = 512
FACE = 64
CB_DEV = 4
FB_DEV = 32


row_block = 256


def extended_2(block, sides, width):
    for axis, dim in sides:
        count = lax.axis_size(axis)
        forward = [(i, i + 1) for i in range(count - 1)]
        forward.append((count - 1, 0))
        backward = [(target, source) for source, target in forward]
        low = lax.ppermute(
            lax.slice_in_dim(block, block.shape[dim] - width, None, axis=dim), axis, forward
        )
        high = lax.ppermute(lax.slice_in_dim(block, 0, width, axis=dim), axis, backward)
        block = jnp.concatenate([low, block, high], axis=dim)
    return block


def corners(fine_pos):
    is_even = fine_pos % 2 == 0
    lower_at = jnp.where(is_even, fine_pos // 2, fine_pos // 2 + 1)
    lower_w = jnp.where(is_even, 0.25, 0.75).astype(jnp.float32)
    return ((lower_at, lower_w), (lower_at + 1, 1.0 - lower_w))


def fold_column(pos_a, pos_b, pos_c, brick_edge):
    out_a = (pos_a == 0) | (pos_a == brick_edge + 1)
    out_b = (pos_b == 0) | (pos_b == brick_edge + 1)
    out_c = (pos_c == 0) | (pos_c == brick_edge + 1)
    outside = out_a.astype(jnp.int32) + out_b.astype(jnp.int32) + out_c.astype(jnp.int32)
    clamp_a = jnp.clip(pos_a, 1, brick_edge) - 1
    clamp_b = jnp.clip(pos_b, 1, brick_edge) - 1
    clamp_c = jnp.clip(pos_c, 1, brick_edge) - 1
    inner_col = clamp_a * brick_edge * brick_edge + clamp_b * brick_edge + clamp_c
    face_cells = brick_edge * brick_edge
    face_base = brick_edge**3
    face_a = (
        face_base
        + jnp.where(pos_a == 0, 0, 1) * face_cells
        + (pos_b - 1) * brick_edge
        + (pos_c - 1)
    )
    face_b = (
        face_base
        + (2 + jnp.where(pos_b == 0, 0, 1)) * face_cells
        + (pos_a - 1) * brick_edge
        + (pos_c - 1)
    )
    face_c = (
        face_base
        + (4 + jnp.where(pos_c == 0, 0, 1)) * face_cells
        + (pos_a - 1) * brick_edge
        + (pos_b - 1)
    )
    single = outside == 1
    return jnp.where(
        single & out_a,
        face_a,
        jnp.where(single & out_b, face_b, jnp.where(single & out_c, face_c, inner_col)),
    )


def child_matrix(child_id, row_count, brick_edge):
    slot_ids = jnp.arange(row_count, dtype=jnp.int32)
    coord_x = slot_ids // (brick_edge * brick_edge)
    coord_y = slot_ids // brick_edge % brick_edge
    coord_z = slot_ids % brick_edge
    fine_x = (child_id >> 2 & 1) * brick_edge + coord_x
    fine_y = (child_id >> 1 & 1) * brick_edge + coord_y
    fine_z = (child_id & 1) * brick_edge + coord_z
    column_total = brick_edge**3 + 6 * brick_edge * brick_edge
    column_ids = jnp.arange(column_total, dtype=jnp.int32)
    matrix = jnp.zeros((row_count, column_total), jnp.float32)
    for pos_a, weight_a in corners(fine_x):
        for pos_b, weight_b in corners(fine_y):
            for pos_c, weight_c in corners(fine_z):
                column = fold_column(pos_a, pos_b, pos_c, brick_edge)
                weight = weight_a * weight_b * weight_c
                matrix = matrix + jnp.where(
                    column[:, None] == column_ids[None, :], weight[:, None], 0.0
                )
    return matrix


def layer_matrix(brick_edge):
    grid_p, grid_q = np.meshgrid(np.arange(brick_edge), np.arange(brick_edge), indexing="ij")
    grid_p = grid_p.reshape(-1)
    grid_q = grid_q.reshape(-1)
    square = brick_edge * brick_edge
    last = brick_edge - 1
    layers = [
        grid_p * brick_edge + grid_q,
        last * square + grid_p * brick_edge + grid_q,
        grid_p * square + grid_q,
        grid_p * square + last * brick_edge + grid_q,
        grid_p * square + grid_q * brick_edge,
        grid_p * square + grid_q * brick_edge + last,
    ]
    cells = np.concatenate(layers)
    table = np.zeros((cells.shape[0], brick_edge**3), dtype=np.float32)
    table[np.arange(cells.shape[0]), cells] = 1.0
    return table


def rank_within(bucket_key):
    count = bucket_key.shape[0]
    order = jnp.arange(count, dtype=jnp.int32)
    earlier = (bucket_key[:, None] == bucket_key[None, :]) & (order[None, :] < order[:, None])
    return jnp.sum(earlier.astype(jnp.int32), axis=1)


def pack_rows(sample_grad, slot_code, bucket_at, slot_total):
    channels = sample_grad.shape[0]
    high_part = (slot_code // 128).astype(jnp.bfloat16)
    low_part = (slot_code % 128).astype(jnp.bfloat16)
    stacked = jnp.concatenate([sample_grad, high_part[None, :], low_part[None, :]], axis=0)
    hits = bucket_at[:, None] == jnp.arange(slot_total, dtype=jnp.int32)[None, :]
    placed = jnp.dot(stacked, hits.astype(jnp.bfloat16), preferred_element_type=jnp.float32)
    filled = jnp.any(hits, axis=0)
    high_row = jnp.where(filled, placed[channels], -1.0)
    moved = jnp.concatenate([placed[:channels], high_row[None, :], placed[channels + 1 :]], axis=0)
    return moved.astype(jnp.bfloat16)


def unpack_rows(arrived, channels):
    grad_rows = arrived[:channels]
    code_rows = arrived[channels].astype(jnp.int32) * 128 + arrived[channels + 1].astype(jnp.int32)
    return (grad_rows, code_rows)


def accumulate(grad_rows, code_rows, brick_count, slot_count):
    channels = grad_rows.shape[0]
    block_total = code_rows.shape[0] // row_block

    def add_block(block_id, running):
        start_row = block_id * row_block
        grad_part = lax.dynamic_slice_in_dim(grad_rows, start_row, row_block, 1)
        code_part = lax.dynamic_slice_in_dim(code_rows, start_row, row_block, 0)
        brick_part = jnp.where(code_part >= 0, code_part // slot_count, -1)
        slot_part = code_part % slot_count
        brick_hot = brick_part[None, :] == jnp.arange(brick_count, dtype=jnp.int32)[:, None]
        masked = jnp.where(brick_hot[:, None, :], grad_part[None, :, :], 0)
        slot_hot = (slot_part[:, None] == jnp.arange(slot_count, dtype=jnp.int32)[None, :]).astype(
            jnp.bfloat16
        )
        product = jnp.dot(
            masked.reshape(brick_count * channels, row_block),
            slot_hot,
            preferred_element_type=jnp.float32,
        )
        return running + product

    running = lax.fori_loop(
        0, block_total, add_block, jnp.zeros((brick_count * channels, slot_count), jnp.float32)
    )
    return running.reshape(brick_count, channels, slot_count)


def body(sample_grad, sample_brick, sample_slot, neighbour):
    tile_count = lax.axis_size("tile")
    owners = lax.axis_size("brick")
    tile_id = lax.axis_index("tile")
    brick_id = lax.axis_index("brick")
    samples = sample_brick.shape[0]
    channels = sample_grad.shape[0]
    capacity = 2 * samples // owners
    group_len = FB_DEV // tile_count
    group_cap = capacity // tile_count
    owner_of = sample_brick // FB_DEV
    local_brick = sample_brick - owner_of * FB_DEV
    group_of = local_brick // group_len
    bucket_key = owner_of * tile_count + group_of
    slot_code = (local_brick - group_of * group_len) * V + sample_slot
    bucket_at = bucket_key * group_cap + rank_within(bucket_key)
    packed = pack_rows(sample_grad, slot_code, bucket_at, owners * tile_count * group_cap)
    arrived = lax.all_to_all(
        lax.all_to_all(
            packed.reshape(channels + 2, owners, tile_count, group_cap),
            "brick",
            split_axis=1,
            concat_axis=1,
            tiled=True,
        ),
        "tile",
        split_axis=2,
        concat_axis=2,
        tiled=True,
    )
    grad_rows, code_rows = unpack_rows(
        arrived.reshape(channels + 2, owners * tile_count * group_cap), channels
    )
    fine_grad = accumulate(grad_rows, code_rows, group_len, V)
    family_count = max(group_len // 8, 1)
    first_fine = tile_id * group_len
    holder = jnp.zeros((family_count * 8, channels, V), jnp.float32)
    holder = lax.dynamic_update_slice_in_dim(holder, fine_grad, first_fine % (family_count * 8), 0)
    families = holder.reshape(family_count, 8, channels, V)
    part_padded = jnp.zeros((family_count, channels, V + 6 * FACE), jnp.float32)
    for child_id in range(8):
        matrix = child_matrix(child_id, V, E)
        part_padded = part_padded + jnp.einsum(
            "bcv,vo->bco", families[:, child_id], matrix, precision=lax.Precision.HIGHEST
        )
    padded = jnp.zeros((CB_DEV, channels, V + 6 * FACE), jnp.float32)
    padded = lax.dynamic_update_slice_in_dim(padded, part_padded, first_fine // 8, 0)
    face_skins = padded[:, :, V:]
    extended = extended_2(face_skins, (("brick", 0),), CB_DEV // 2)
    coarse_total = CB_DEV * owners
    offset = (neighbour - (brick_id * CB_DEV - CB_DEV // 2)) % coarse_total
    opposite = np.array([1, 0, 3, 2, 5, 4], dtype=np.int32)
    facing = extended.reshape(2 * CB_DEV, channels, 6, FACE)[:, :, opposite, :]
    selector = (
        offset[:, :, None] == jnp.arange(2 * CB_DEV, dtype=jnp.int32)[None, None, :]
    ).astype(jnp.float32)
    incoming = jnp.einsum("bke,eckf->bckf", selector, facing, precision=lax.Precision.HIGHEST)
    layer_table = jnp.asarray(layer_matrix(E))
    spread = jnp.einsum(
        "bcf,fv->bcv",
        incoming.reshape(CB_DEV, channels, 6 * FACE),
        layer_table,
        precision=lax.Precision.HIGHEST,
    )
    own_part = padded[:, :, :V] + spread
    coarse_grad = lax.psum_scatter(own_part, "tile", scatter_dimension=2, tiled=True)
    return (fine_grad, coarse_grad)


LANES = 128
KERNEL_VMEM = 16 * 1024 * 1024


def beyond_lane(cell):
    return cell + (32 if cell < 32 else 64)


def expand_tables(brick_edge):
    square = brick_edge * brick_edge
    last = brick_edge - 1
    out = np.zeros((2, LANES, LANES), np.float32)
    for side in range(2):
        for odd in range(2):
            for at in range(brick_edge):
                base = odd * square + at
                out[side, base, odd * square + last * brick_edge + at] = 1
                out[side, base + brick_edge, odd * square + at] = 1
                out[side, base + 2 * brick_edge, odd * square + at * brick_edge + last] = 1
                out[side, base + 3 * brick_edge, odd * square + at * brick_edge] = 1
        for cell in range(square):
            out[side, beyond_lane(cell), side * square + cell] = 1
    return out


def fold_table(brick_edge):
    square = brick_edge * brick_edge
    last = brick_edge - 1
    base = 4 * brick_edge
    out = np.zeros((LANES, 2 * LANES), np.float32)
    for at in range(brick_edge):
        targets = [(at, at), (brick_edge + at, last * brick_edge + at)]
        if 0 < at < last:
            targets += [(2 * brick_edge + at, at * brick_edge), (3 * brick_edge + at, at * brick_edge + last)]
        else:
            out[base + 2 * brick_edge + at, LANES + beyond_lane(at * brick_edge)] = -1
            out[base + 3 * brick_edge + at, LANES + beyond_lane(at * brick_edge + last)] = -1
        for source, cell in targets:
            out[base + source, cell] = 1
            out[base + source, square + cell] = 1
    return out


def split_two(value):
    high = value.astype(jnp.bfloat16)
    low = (value - high.astype(jnp.float32)).astype(jnp.bfloat16)
    return high, low


def contract_last(left, right):
    return lax.dot_general(left, right, (((1,), (1,)), ((), ())), preferred_element_type=jnp.float32)


def pack_kernel(group_len, tile_count, partners, brick_hbm, slot_hbm, grad_hbm, out_ref, brick_ref, slot_ref, grad_ref, high_ref, sems):
    channels = grad_hbm.shape[0]
    blocks = brick_ref.shape[0]
    dests = len(partners)
    copies = [
        pltpu.make_async_copy(brick_hbm, brick_ref, sems.at[0]),
        pltpu.make_async_copy(slot_hbm, slot_ref, sems.at[1]),
        pltpu.make_async_copy(grad_hbm, grad_ref, sems.at[2]),
    ]
    for copy in copies:
        copy.start()
    at_row = lax.broadcasted_iota(jnp.int32, (LANES, 2 * LANES), 0)
    at_lane = lax.broadcasted_iota(jnp.int32, (LANES, 2 * LANES), 1)
    tri = jnp.where((at_row < at_lane) | (at_lane >= LANES), 1.0, 0.0).astype(jnp.bfloat16)
    copies[0].wait()
    copies[1].wait()
    brick = brick_ref[...]
    slot = slot_ref[...]
    bucket = brick // group_len
    local = brick - bucket * group_len
    coord_x = (local // 4) * E + slot // (E * E)
    coord_y = (local // 2 % 2) * E + slot // E % E
    coord_z = (local % 2) * E + slot % E
    bucket_f = bucket.astype(jnp.float32)
    dest_ids = lax.broadcasted_iota(jnp.int32, (dests, LANES), 0).astype(jnp.float32)
    hots = [
        jnp.where(jnp.broadcast_to(bucket_f[i : i + 1], (dests, LANES)) == dest_ids, 1.0, 0.0)
        for i in range(blocks)
    ]
    counts = jnp.dot(
        jnp.concatenate(hots, axis=0).astype(jnp.bfloat16), tri, preferred_element_type=jnp.float32
    )
    before = jnp.zeros((dests, LANES), jnp.float32)
    ranks = []
    for i in range(blocks):
        part = counts[i * dests : (i + 1) * dests]
        ranks.append(jnp.sum(hots[i] * (part[:, :LANES] + before), axis=0, keepdims=True))
        before = before + part[:, LANES:]
    rank = jnp.concatenate(ranks, axis=1)

    rows = lax.broadcasted_iota(jnp.int32, (4, LANES), 0)
    x_f = coord_x.astype(jnp.float32)
    y_f = coord_y.astype(jnp.float32)
    z_f = coord_z.astype(jnp.float32)
    for i in range(blocks):
        code = jnp.where(
            rows == 0,
            x_f[i : i + 1],
            jnp.where(rows == 1, y_f[i : i + 1], jnp.where(rows == 2, z_f[i : i + 1], 0.0)),
        )
        high_ref[channels - 16 : channels - 12, i * LANES : (i + 1) * LANES] = code.astype(jnp.bfloat16)
    copies[2].wait()
    high_ref[: channels - 16, :] = grad_ref[16:channels, :]
    low = grad_ref[:16, :]
    high = high_ref[...]

    def spread(value):
        return jnp.concatenate(
            [jnp.broadcast_to(value[i : i + 1], (16, LANES)) for i in range(blocks)], axis=1
        ).astype(jnp.bfloat16)

    owner16 = spread((bucket // tile_count).astype(jnp.float32))
    tile16 = spread((bucket % tile_count).astype(jnp.float32))
    zero = jnp.zeros_like(low)
    left = []
    for owner in range(dests // tile_count):
        mask = owner16 == jnp.bfloat16(owner)
        left += [jnp.where(mask, low, zero), jnp.where(mask, high, zero)]
    half = LANES // 2
    rank16 = jnp.broadcast_to(rank, (16, rank.shape[1])).astype(jnp.bfloat16)
    row_ids = lax.broadcasted_iota(jnp.int32, rank16.shape, 0).astype(jnp.float32)
    ones = jnp.ones_like(low)
    hot = [
        jnp.where(rank16 == (row_ids + 16.0 * g).astype(jnp.bfloat16), ones, zero) for g in range(half // 16)
    ]
    right = []
    for tile in range(tile_count):
        mask = tile16 == jnp.bfloat16(tile)
        right += [jnp.where(mask, value, zero) for value in hot]
    placed = contract_last(jnp.concatenate(left, axis=0), jnp.concatenate(right, axis=0)).astype(jnp.bfloat16)
    tiles = []
    for owner in range(dests // tile_count):
        for pair in range(tile_count // 2):
            low_part = placed[32 * owner : 32 * owner + 16, pair * LANES : (pair + 1) * LANES]
            high_part = placed[32 * owner + 16 : 32 * owner + 32, pair * LANES : (pair + 1) * LANES]
            tiles.append(jnp.concatenate([low_part[:, :half], high_part[:, :half]], axis=1))
            tiles.append(jnp.concatenate([low_part[:, half:], high_part[:, half:]], axis=1))
    for dest in range(dests):
        out_ref[dest, 0] = tiles[dest]
        out_ref[dest, 1] = tiles[partners[dest]]


def unpack(arrived_ref, which, channels):
    half = LANES // 2
    pairs = arrived_ref.shape[0] // 2
    lows = []
    highs = []
    for p in range(pairs):
        first = arrived_ref[p, which]
        second = arrived_ref[p + pairs, which]
        lows.append(jnp.concatenate([first[:, :half], second[:, :half]], axis=1))
        highs.append(jnp.concatenate([first[:, half:], second[:, half:]], axis=1))
    low = jnp.concatenate(lows, axis=1)
    high = jnp.concatenate(highs, axis=1)
    codes = high.astype(jnp.float32)
    at = channels - 16
    coords = [
        jnp.broadcast_to(codes[at + k : at + k + 1], (16, low.shape[1])).astype(jnp.bfloat16) for k in range(3)
    ]
    return low, high, coords


def pack_pair(first, second):
    return jnp.concatenate([first, second], axis=0).astype(jnp.bfloat16)


def block_axes(code, axis_ref):
    row = lax.broadcasted_iota(jnp.int32, (8, LANES), 0).astype(jnp.float32)
    axis_ref[0] = code
    coords = [axis_ref[0, pl.ds(at, 8, stride=0), :] for at in (4, 5, 6)]
    rows = [jnp.maximum(1.0 - jnp.abs(c * 0.5 - (row + 0.25)), 0.0) for c in coords]
    return row, coords, rows


def lines_of(axis_ref, at, rows):
    axis_ref[at] = rows
    return [axis_ref[at, pl.ds(m, 8, stride=0), :] for m in range(E)]


def select_rows(hits, low, high):
    zero = jnp.zeros_like(low)
    rows = []
    for hit in hits:
        rows += [jnp.where(hit, low, zero), jnp.where(hit, high, zero)]
    return rows


def own_block(code, axis_ref, low, high):
    row, (x, y, z), (_, y_rows, z_rows) = block_axes(code, axis_ref)
    last = 2.0 * E - 1.0
    blank = jnp.zeros((8, LANES), jnp.float32)
    y_lines = lines_of(axis_ref, 2, y_rows)
    y_pair = [pack_pair(y_lines[2 * g], y_lines[2 * g + 1]) for g in range(E // 2)]
    z_in = pack_pair(z_rows, z_rows)
    y_low = jnp.where(y == 0.0, 0.25, 0.0)
    y_high = jnp.where(y == last, 0.25, 0.0)
    z_low = jnp.where(z == 0.0, 0.25, 0.0)
    z_high = jnp.where(z == last, 0.25, 0.0)
    z_out = jnp.where(row == 0.0, z_low, jnp.where(row == E - 1.0, z_high, blank))
    y_edge = jnp.where(row == 0.0, y_low, jnp.where(row == E - 1.0, y_high, y_rows))
    z_both = z_rows + z_out
    inner = [value * z_in for value in y_pair]
    inner[0] = inner[0] + pack_pair(y_low * z_out, blank)
    inner[-1] = inner[-1] + pack_pair(blank, y_high * z_out)
    faces = [pack_pair(y_low * z_rows, y_high * z_rows), pack_pair(z_low * y_rows, z_high * y_rows)]
    edges = [
        pack_pair(y_lines[0] * z_out + y_low * z_both, y_lines[E - 1] * z_out + y_high * z_both),
        pack_pair(y_edge * z_low, y_edge * z_high),
    ]
    whole = x.astype(jnp.int32)
    pair_of = (whole >> 1).astype(jnp.float32)
    odd = (whole & 1).astype(jnp.float32)
    odd16 = pack_pair(odd, odd)
    even16 = jnp.bfloat16(1.0) - odd16
    ends = jnp.where((x == 0.0) | (x == last), 1.0, 0.0)
    ends16 = pack_pair(ends, ends)
    pair16 = pack_pair(pair_of, pair_of)
    left = select_rows([pair16 == jnp.bfloat16(at) for at in range(E)], low, high)
    right = [value * even16 for value in inner] + [value * odd16 for value in inner]
    right += [value * even16 for value in faces] + [value * ends16 for value in edges]
    return left, right + [value * odd16 for value in faces]


def skin_block(code, axis_ref, low, high):
    _, coords, (x_rows, y_rows, z_rows) = block_axes(code, axis_ref)
    last = 2 * E - 1
    x_lines = lines_of(axis_ref, 1, x_rows)
    y_lines = lines_of(axis_ref, 2, y_rows)
    x_order = list(range(0, E, 2)) + list(range(1, E, 2))
    x_pair = [pack_pair(x_lines[x_order[2 * g]], x_lines[x_order[2 * g + 1]]) for g in range(E // 2)]
    y_pair = [pack_pair(y_lines[2 * g], y_lines[2 * g + 1]) for g in range(E // 2)]
    z_in = pack_pair(z_rows, z_rows)
    y_in = pack_pair(y_rows, y_rows)
    x16, y16, z16 = [pack_pair(c, c) for c in coords]
    hits = [c == jnp.bfloat16(end) for c in (y16, z16, x16) for end in (0, last)]
    left = select_rows(hits, low, high)
    right = []
    for part in (x_pair[: E // 4], x_pair[E // 4 :]):
        right += [value * z_in for value in part] + [value * y_in for value in part]
    return left, right + [value * z_in for value in y_pair]


def lay_out(blocks):
    return jnp.concatenate(
        [jnp.concatenate([block[i] for block in blocks], axis=1) for i in range(len(blocks[0]))], axis=0
    )


def own_quarters(product, table):
    half = LANES // 2
    lane = lax.broadcasted_iota(jnp.int32, (32, LANES), 1)
    left = lane < half
    spare = lane % half >= half // 2
    blank = jnp.zeros((32, LANES - product.shape[1] % LANES), jnp.float32)
    cells = [product[32 * i : 32 * i + 32, :LANES] for i in range(E)]
    faces = [jnp.concatenate([product[32 * i : 32 * i + 32, LANES:], blank], axis=1) for i in range(E)]
    high_part, low_part = split_two(jnp.concatenate([faces[0], faces[-1]], axis=0))
    folds = jnp.dot(high_part, table, preferred_element_type=jnp.float32)
    folds = 0.25 * (folds + jnp.dot(low_part, table, preferred_element_type=jnp.float32))

    def even_x(values, m):
        return 0.75 * values[m] + 0.25 * values[m + 1] if m < E - 1 else 0.75 * values[m]

    def odd_x(values, m):
        return 0.75 * values[m] + 0.25 * values[m - 1] if m > 0 else 0.75 * values[m]

    def layers(values, m):
        stay = jnp.where(left, even_x(values, m), odd_x(values, m + 1))
        cross = jnp.where(left, even_x(values, m + 1), odd_x(values, m))
        return stay + pltpu.roll(cross, half, 1)

    quarters = []
    for q in range(E // 2):
        own = layers(cells, 2 * q)
        skin = layers(faces, 2 * q)
        beyond = jnp.zeros_like(own)
        if q == 0:
            own = own + jnp.where(left, folds[:32, :LANES], 0.0)
            moved = jnp.where(left, pltpu.roll(cells[-1], LANES - half // 2, 1), cells[-1])
            beyond = 0.25 * moved + folds[32:, LANES:]
        if q == E // 2 - 1:
            own = own + jnp.where(left, 0.0, folds[32:, :LANES])
            moved = jnp.where(left, pltpu.roll(cells[0], half // 2, 1), pltpu.roll(cells[0], half, 1))
            beyond = 0.25 * moved + folds[:32, LANES:]
        quarters.append((own, jnp.where(spare, beyond, skin)))
    return quarters


def skin_quarters(product):
    half = LANES // 2
    lane = lax.broadcasted_iota(jnp.int32, (32, LANES), 1)
    left = lane < half
    face_of = jnp.where(lane % half < half // 2, (lane // E) % 4, 4)
    sides = [0.25 * product[32 * f : 32 * f + 32, :LANES] for f in range(4)]
    ends = []
    for f in (4, 5):
        end = 0.25 * product[32 * f : 32 * f + 32, LANES:]
        end = jnp.concatenate([end, end], axis=1)
        ends.append(jnp.where(left, pltpu.roll(end, half // 2, 1), end))
    quarters = []
    for q in range(E // 2):
        value = ends[1] if q == 0 else ends[0] if q == E // 2 - 1 else jnp.zeros_like(sides[0])
        for f in range(4):
            shift = (E * (f - q) - (half // 2 if f >= 2 else 0)) % LANES
            moved = pltpu.roll(sides[f], shift, 1) if shift else sides[f]
            value = jnp.where(face_of == f, moved, value)
        quarters.append(value)
    return quarters


def coarse_kernel(channels, arrived_ref, table_hbm, *refs):
    out_refs, (quarter_ref, axis_ref, table_ref, sem) = refs[:4], refs[4:]
    table_copy = pltpu.make_async_copy(table_hbm, table_ref, sem)
    table_copy.start()
    tile_id = lax.axis_index("tile")
    half = LANES // 2
    pairs = arrived_ref.shape[0] // 2

    def blocks(which, make):
        made = []
        for p in range(pairs):
            first = arrived_ref[p, which]
            second = arrived_ref[p + pairs, which]
            low = jnp.concatenate([first[:, :half], second[:, :half]], axis=1)
            high = jnp.concatenate([first[:, half:], second[:, half:]], axis=1)
            made.append(make(high.astype(jnp.float32)[8:], axis_ref.at[which, p], low, high))
        return [[block[i] for block in made] for i in range(len(made[0]))]

    def in_halves(left, right):
        middle = pairs // 2
        return contract_last(lay_out(left[:middle]), lay_out(right[:middle])) + contract_last(
            lay_out(left[middle:]), lay_out(right[middle:])
        )

    skin_product = in_halves(*blocks(1, skin_block))
    own_product = in_halves(*blocks(0, own_block))
    for q, skin in enumerate(skin_quarters(skin_product)):
        quarter_ref[q, 2] = skin
    table_copy.wait()
    for q, (own, skin) in enumerate(own_quarters(own_product, table_ref[...])):
        quarter_ref[q, 0] = own
        quarter_ref[q, 1] = skin
    for delta in range(4):
        for part in range(3):
            out_refs[delta][pl.ds(part, channels, stride=3), :] = quarter_ref[tile_id ^ delta, part][:channels]


def fine_kernel(channels, coarse_total, arrived_ref, near_ref, fine_ref, source_ref, turn_ref):
    first = lax.axis_index("brick") * CB_DEV - CB_DEV // 2
    lane = lax.broadcasted_iota(jnp.int32, (8, LANES), 1)
    group = jnp.where(lane % (LANES // 2) < 4 * E, (lane // E) % 4, 4)
    x_face = jnp.where(lax.axis_index("tile") < 2, 0, 1)
    for i in range(CB_DEV):
        near = [(near_ref[i, face] - first + coarse_total) % coarse_total for face in (3, 2, 5, 4, x_face)]
        source = jnp.where(group == 0, near[0], near[1])
        for k in range(2, 5):
            source = jnp.where(group == k, near[k], source)
        source_ref[i] = source
    low, high, coords = unpack(arrived_ref, 0, channels)
    zero = jnp.zeros_like(low)
    one = jnp.ones_like(low)
    edge = jnp.bfloat16(E)
    halves = [jnp.where(c >= edge, one, zero) for c in coords]
    inside = [c - edge * h for c, h in zip(coords, halves)]
    child_at = halves[0] * jnp.bfloat16(4) + halves[1] * jnp.bfloat16(2) + halves[2]
    cell_at = inside[1] * edge + inside[2]
    left = []
    for child in range(8):
        mask = child_at == jnp.bfloat16(child)
        left.append(jnp.where(mask, low, zero))
        left.append(jnp.where(mask, high, zero))
    row_ids = lax.broadcasted_iota(jnp.int32, low.shape, 0).astype(jnp.float32)
    cells = [
        jnp.where(cell_at == (row_ids + 16.0 * g).astype(jnp.bfloat16), one, zero) for g in range(E * E // 16)
    ]
    right = []
    for plane in range(E):
        mask = inside[0] == jnp.bfloat16(plane)
        for g in range(E * E // 16):
            right.append(jnp.where(mask, cells[g], zero))
    fine = contract_last(jnp.concatenate(left, axis=0), jnp.concatenate(right, axis=0))
    for i in range(V // LANES):
        for child in range(8):
            turn_ref[i, pl.ds(child, channels, stride=8), :] = fine[
                32 * child : 32 * child + channels, i * LANES : (i + 1) * LANES
            ]
        fine_ref[:, i * LANES : (i + 1) * LANES] = turn_ref[i]


def combine_kernel(channels, source_ref, zero_ref, one_ref, two_ref, three_ref,
                   table_ref, out_ref, hold_ref):
    tile_id = lax.axis_index("tile")
    for delta, ref in enumerate((zero_ref, one_ref, two_ref, three_ref)):
        hold_ref[tile_id ^ delta] = ref[...]

    def part(tile, which):
        return hold_ref[tile, pl.ds(which, channels, stride=3), :]

    skins = [part(2, 2), part(3, 2)] + [part(j, 1) for j in range(4)] + [part(0, 2), part(1, 2)]
    gathered = []
    for i in range(4):
        source = jnp.broadcast_to(source_ref[i, :1], (channels, LANES))
        first = 0 if i < 2 else 4
        value = jnp.zeros((channels, LANES), jnp.float32)
        for e in range(first, first + 4):
            value = jnp.where(source == e, skins[e], value)
        gathered.append(value)
    table = table_ref[tile_id // 2]
    for i in range(4):
        high_part, low_part = split_two(gathered[i])
        moved = jnp.dot(high_part, table, preferred_element_type=jnp.float32) + jnp.dot(
            low_part, table, preferred_element_type=jnp.float32
        )
        out_ref[pl.ds(i, channels, stride=4), :] = part(i, 0) + moved


def family_body(sample_grad, sample_brick, sample_slot, neighbour):
    tile_count = lax.axis_size("tile")
    owners = lax.axis_size("brick")
    channels, samples = sample_grad.shape
    dests = owners * tile_count
    group_len = FB_DEV // tile_count
    vmem = pl.BlockSpec(memory_space=pltpu.VMEM)
    hbm = pl.BlockSpec(memory_space=pltpu.HBM)
    limit = pltpu.CompilerParams(vmem_limit_bytes=KERNEL_VMEM)
    partners = []
    for b in range(owners):
        for t in range(tile_count):
            step = -1 if t >= tile_count // 2 else 1
            partners.append((b + step) % owners * tile_count + t)
    inputs = (
        sample_brick.reshape(samples // LANES, LANES),
        sample_slot.reshape(samples // LANES, LANES),
        sample_grad,
    )
    packed = pl.pallas_call(
        functools.partial(pack_kernel, group_len, tile_count, tuple(partners)),
        out_shape=jax.ShapeDtypeStruct((dests, 2, 16, LANES), jnp.bfloat16),
        in_specs=[hbm] * 3,
        out_specs=vmem,
        scratch_shapes=[
            pltpu.VMEM((samples // LANES, LANES), jnp.int32),
            pltpu.VMEM((samples // LANES, LANES), jnp.int32),
            pltpu.VMEM((channels, samples), jnp.bfloat16),
            pltpu.VMEM((16, samples), jnp.bfloat16),
            pltpu.SemaphoreType.DMA((3,)),
        ],
        compiler_params=limit,
        name="pack",
    )(*[pltpu.with_memory_space_constraint(value, pltpu.HBM) for value in inputs])
    arrived = lax.all_to_all(packed, ("brick", "tile"), 0, 0, tiled=True)
    message = jax.ShapeDtypeStruct((3 * channels, LANES), jnp.float32)
    messages = pl.pallas_call(
        functools.partial(coarse_kernel, channels),
        out_shape=(message,) * 4,
        in_specs=[vmem, hbm],
        out_specs=(vmem,) * 4,
        scratch_shapes=[
            pltpu.VMEM((4, 3, 32, LANES), jnp.float32),
            pltpu.VMEM((2, dests // 2, 3, 8, LANES), jnp.float32),
            pltpu.VMEM((LANES, 2 * LANES), jnp.bfloat16),
            pltpu.SemaphoreType.DMA,
        ],
        compiler_params=limit,
        name="coarse",
    )(arrived, pltpu.with_memory_space_constraint(jnp.asarray(fold_table(E), jnp.bfloat16), pltpu.HBM))
    arrivals = {}
    for delta in (3, 1, 2):
        arrivals[delta] = lax.ppermute(messages[delta], "tile", [(t, t ^ delta) for t in range(tile_count)])
    fine, source = pl.pallas_call(
        functools.partial(fine_kernel, channels, CB_DEV * owners),
        out_shape=(
            jax.ShapeDtypeStruct((channels * 8, V), jnp.float32),
            jax.ShapeDtypeStruct((CB_DEV, 8, LANES), jnp.int32),
        ),
        in_specs=[vmem, pl.BlockSpec(memory_space=pltpu.SMEM)],
        out_specs=(vmem, vmem),
        scratch_shapes=[pltpu.VMEM((V // LANES, channels * 8, LANES), jnp.float32)],
        compiler_params=limit,
        name="fine",
    )(arrived, neighbour)
    coarse = pl.pallas_call(
        functools.partial(combine_kernel, channels),
        out_shape=jax.ShapeDtypeStruct((channels * CB_DEV, LANES), jnp.float32),
        in_specs=[vmem] * 6,
        out_specs=vmem,
        scratch_shapes=[pltpu.VMEM((4, 3 * channels, LANES), jnp.float32)],
        compiler_params=limit,
        name="combine",
    )(source, messages[0], arrivals[1], arrivals[2], arrivals[3], jnp.asarray(expand_tables(E), jnp.bfloat16))
    fine_grad = fine.reshape(channels, 8, V).transpose(1, 0, 2)
    coarse_grad = coarse.reshape(channels, CB_DEV, LANES).transpose(1, 0, 2)
    return fine_grad, coarse_grad


def solution(mesh):
    in_specs = (
        P(None, ("brick", "tile")),
        P(("brick", "tile")),
        P(("brick", "tile")),
        P("brick", None),
    )
    out_specs = (P(("brick", "tile"), None, None), P("brick", None, "tile"))

    def step(sample_grad, sample_brick, sample_slot, neighbour):
        owners, tile_count = mesh.shape["brick"], mesh.shape["tile"]
        samples = sample_grad.shape[1] // (owners * tile_count)
        whole_family = FB_DEV == 8 * tile_count == 2 * 4 * CB_DEV and tile_count == CB_DEV
        full_messages = 2 * samples == (LANES // 2) * owners * tile_count and samples % LANES == 0
        fits = whole_family and full_messages and sample_grad.shape[0] == 28 and owners > 2
        if not fits:
            mapped = jax.shard_map(body, mesh=mesh, in_specs=in_specs, out_specs=out_specs, check_vma=False)
        else:
            mapped = jax.shard_map(family_body, mesh=mesh, in_specs=in_specs, out_specs=out_specs, check_vma=False)
        return mapped(sample_grad, sample_brick, sample_slot, neighbour)

    return step
```

```python
import functools

import jax
import jax.numpy as jnp
import numpy as np
from jax import lax
from jax.experimental import pallas as pl
from jax.experimental.pallas import tpu as pltpu
from jax.sharding import PartitionSpec as P


E = 8
V = 512
FACE = 64
CB_DEV = 4
FB_DEV = 32


row_block = 256


def extended_2(block, sides, width):
    for axis, dim in sides:
        count = lax.axis_size(axis)
        forward = [(i, i + 1) for i in range(count - 1)]
        forward.append((count - 1, 0))
        backward = [(target, source) for source, target in forward]
        low = lax.ppermute(
            lax.slice_in_dim(block, block.shape[dim] - width, None, axis=dim), axis, forward
        )
        high = lax.ppermute(lax.slice_in_dim(block, 0, width, axis=dim), axis, backward)
        block = jnp.concatenate([low, block, high], axis=dim)
    return block


def corners(fine_pos):
    is_even = fine_pos % 2 == 0
    lower_at = jnp.where(is_even, fine_pos // 2, fine_pos // 2 + 1)
    lower_w = jnp.where(is_even, 0.25, 0.75).astype(jnp.float32)
    return ((lower_at, lower_w), (lower_at + 1, 1.0 - lower_w))


def fold_column(pos_a, pos_b, pos_c, brick_edge):
    out_a = (pos_a == 0) | (pos_a == brick_edge + 1)
    out_b = (pos_b == 0) | (pos_b == brick_edge + 1)
    out_c = (pos_c == 0) | (pos_c == brick_edge + 1)
    outside = out_a.astype(jnp.int32) + out_b.astype(jnp.int32) + out_c.astype(jnp.int32)
    clamp_a = jnp.clip(pos_a, 1, brick_edge) - 1
    clamp_b = jnp.clip(pos_b, 1, brick_edge) - 1
    clamp_c = jnp.clip(pos_c, 1, brick_edge) - 1
    inner_col = clamp_a * brick_edge * brick_edge + clamp_b * brick_edge + clamp_c
    face_cells = brick_edge * brick_edge
    face_base = brick_edge**3
    face_a = (
        face_base
        + jnp.where(pos_a == 0, 0, 1) * face_cells
        + (pos_b - 1) * brick_edge
        + (pos_c - 1)
    )
    face_b = (
        face_base
        + (2 + jnp.where(pos_b == 0, 0, 1)) * face_cells
        + (pos_a - 1) * brick_edge
        + (pos_c - 1)
    )
    face_c = (
        face_base
        + (4 + jnp.where(pos_c == 0, 0, 1)) * face_cells
        + (pos_a - 1) * brick_edge
        + (pos_b - 1)
    )
    single = outside == 1
    return jnp.where(
        single & out_a,
        face_a,
        jnp.where(single & out_b, face_b, jnp.where(single & out_c, face_c, inner_col)),
    )


def child_matrix(child_id, row_count, brick_edge):
    slot_ids = jnp.arange(row_count, dtype=jnp.int32)
    coord_x = slot_ids // (brick_edge * brick_edge)
    coord_y = slot_ids // brick_edge % brick_edge
    coord_z = slot_ids % brick_edge
    fine_x = (child_id >> 2 & 1) * brick_edge + coord_x
    fine_y = (child_id >> 1 & 1) * brick_edge + coord_y
    fine_z = (child_id & 1) * brick_edge + coord_z
    column_total = brick_edge**3 + 6 * brick_edge * brick_edge
    column_ids = jnp.arange(column_total, dtype=jnp.int32)
    matrix = jnp.zeros((row_count, column_total), jnp.float32)
    for pos_a, weight_a in corners(fine_x):
        for pos_b, weight_b in corners(fine_y):
            for pos_c, weight_c in corners(fine_z):
                column = fold_column(pos_a, pos_b, pos_c, brick_edge)
                weight = weight_a * weight_b * weight_c
                matrix = matrix + jnp.where(
                    column[:, None] == column_ids[None, :], weight[:, None], 0.0
                )
    return matrix


def layer_matrix(brick_edge):
    grid_p, grid_q = np.meshgrid(np.arange(brick_edge), np.arange(brick_edge), indexing="ij")
    grid_p = grid_p.reshape(-1)
    grid_q = grid_q.reshape(-1)
    square = brick_edge * brick_edge
    last = brick_edge - 1
    layers = [
        grid_p * brick_edge + grid_q,
        last * square + grid_p * brick_edge + grid_q,
        grid_p * square + grid_q,
        grid_p * square + last * brick_edge + grid_q,
        grid_p * square + grid_q * brick_edge,
        grid_p * square + grid_q * brick_edge + last,
    ]
    cells = np.concatenate(layers)
    table = np.zeros((cells.shape[0], brick_edge**3), dtype=np.float32)
    table[np.arange(cells.shape[0]), cells] = 1.0
    return table


def rank_within(bucket_key):
    count = bucket_key.shape[0]
    order = jnp.arange(count, dtype=jnp.int32)
    earlier = (bucket_key[:, None] == bucket_key[None, :]) & (order[None, :] < order[:, None])
    return jnp.sum(earlier.astype(jnp.int32), axis=1)


def pack_rows(sample_grad, slot_code, bucket_at, slot_total):
    channels = sample_grad.shape[0]
    high_part = (slot_code // 128).astype(jnp.bfloat16)
    low_part = (slot_code % 128).astype(jnp.bfloat16)
    stacked = jnp.concatenate([sample_grad, high_part[None, :], low_part[None, :]], axis=0)
    hits = bucket_at[:, None] == jnp.arange(slot_total, dtype=jnp.int32)[None, :]
    placed = jnp.dot(stacked, hits.astype(jnp.bfloat16), preferred_element_type=jnp.float32)
    filled = jnp.any(hits, axis=0)
    high_row = jnp.where(filled, placed[channels], -1.0)
    moved = jnp.concatenate([placed[:channels], high_row[None, :], placed[channels + 1 :]], axis=0)
    return moved.astype(jnp.bfloat16)


def unpack_rows(arrived, channels):
    grad_rows = arrived[:channels]
    code_rows = arrived[channels].astype(jnp.int32) * 128 + arrived[channels + 1].astype(jnp.int32)
    return (grad_rows, code_rows)


def accumulate(grad_rows, code_rows, brick_count, slot_count):
    channels = grad_rows.shape[0]
    block_total = code_rows.shape[0] // row_block

    def add_block(block_id, running):
        start_row = block_id * row_block
        grad_part = lax.dynamic_slice_in_dim(grad_rows, start_row, row_block, 1)
        code_part = lax.dynamic_slice_in_dim(code_rows, start_row, row_block, 0)
        brick_part = jnp.where(code_part >= 0, code_part // slot_count, -1)
        slot_part = code_part % slot_count
        brick_hot = brick_part[None, :] == jnp.arange(brick_count, dtype=jnp.int32)[:, None]
        masked = jnp.where(brick_hot[:, None, :], grad_part[None, :, :], 0)
        slot_hot = (slot_part[:, None] == jnp.arange(slot_count, dtype=jnp.int32)[None, :]).astype(
            jnp.bfloat16
        )
        product = jnp.dot(
            masked.reshape(brick_count * channels, row_block),
            slot_hot,
            preferred_element_type=jnp.float32,
        )
        return running + product

    running = lax.fori_loop(
        0, block_total, add_block, jnp.zeros((brick_count * channels, slot_count), jnp.float32)
    )
    return running.reshape(brick_count, channels, slot_count)


def body(sample_grad, sample_brick, sample_slot, neighbour):
    tile_count = lax.axis_size("tile")
    owners = lax.axis_size("brick")
    tile_id = lax.axis_index("tile")
    brick_id = lax.axis_index("brick")
    samples = sample_brick.shape[0]
    channels = sample_grad.shape[0]
    capacity = 2 * samples // owners
    group_len = FB_DEV // tile_count
    group_cap = capacity // tile_count
    owner_of = sample_brick // FB_DEV
    local_brick = sample_brick - owner_of * FB_DEV
    group_of = local_brick // group_len
    bucket_key = owner_of * tile_count + group_of
    slot_code = (local_brick - group_of * group_len) * V + sample_slot
    bucket_at = bucket_key * group_cap + rank_within(bucket_key)
    packed = pack_rows(sample_grad, slot_code, bucket_at, owners * tile_count * group_cap)
    arrived = lax.all_to_all(
        lax.all_to_all(
            packed.reshape(channels + 2, owners, tile_count, group_cap),
            "brick",
            split_axis=1,
            concat_axis=1,
            tiled=True,
        ),
        "tile",
        split_axis=2,
        concat_axis=2,
        tiled=True,
    )
    grad_rows, code_rows = unpack_rows(
        arrived.reshape(channels + 2, owners * tile_count * group_cap), channels
    )
    fine_grad = accumulate(grad_rows, code_rows, group_len, V)
    family_count = max(group_len // 8, 1)
    first_fine = tile_id * group_len
    holder = jnp.zeros((family_count * 8, channels, V), jnp.float32)
    holder = lax.dynamic_update_slice_in_dim(holder, fine_grad, first_fine % (family_count * 8), 0)
    families = holder.reshape(family_count, 8, channels, V)
    part_padded = jnp.zeros((family_count, channels, V + 6 * FACE), jnp.float32)
    for child_id in range(8):
        matrix = child_matrix(child_id, V, E)
        part_padded = part_padded + jnp.einsum(
            "bcv,vo->bco", families[:, child_id], matrix, precision=lax.Precision.HIGHEST
        )
    padded = jnp.zeros((CB_DEV, channels, V + 6 * FACE), jnp.float32)
    padded = lax.dynamic_update_slice_in_dim(padded, part_padded, first_fine // 8, 0)
    face_skins = padded[:, :, V:]
    extended = extended_2(face_skins, (("brick", 0),), CB_DEV // 2)
    coarse_total = CB_DEV * owners
    offset = (neighbour - (brick_id * CB_DEV - CB_DEV // 2)) % coarse_total
    opposite = np.array([1, 0, 3, 2, 5, 4], dtype=np.int32)
    facing = extended.reshape(2 * CB_DEV, channels, 6, FACE)[:, :, opposite, :]
    selector = (
        offset[:, :, None] == jnp.arange(2 * CB_DEV, dtype=jnp.int32)[None, None, :]
    ).astype(jnp.float32)
    incoming = jnp.einsum("bke,eckf->bckf", selector, facing, precision=lax.Precision.HIGHEST)
    layer_table = jnp.asarray(layer_matrix(E))
    spread = jnp.einsum(
        "bcf,fv->bcv",
        incoming.reshape(CB_DEV, channels, 6 * FACE),
        layer_table,
        precision=lax.Precision.HIGHEST,
    )
    own_part = padded[:, :, :V] + spread
    coarse_grad = lax.psum_scatter(own_part, "tile", scatter_dimension=2, tiled=True)
    return (fine_grad, coarse_grad)


LANES = 128
KERNEL_VMEM = 16 * 1024 * 1024


def beyond_lane(cell):
    return cell + (32 if cell < 32 else 64)


def expand_tables(brick_edge):
    square = brick_edge * brick_edge
    last = brick_edge - 1
    out = np.zeros((2, LANES, LANES), np.float32)
    for side in range(2):
        for odd in range(2):
            for at in range(brick_edge):
                base = odd * square + at
                out[side, base, odd * square + last * brick_edge + at] = 1
                out[side, base + brick_edge, odd * square + at] = 1
                out[side, base + 2 * brick_edge, odd * square + at * brick_edge + last] = 1
                out[side, base + 3 * brick_edge, odd * square + at * brick_edge] = 1
        for cell in range(square):
            out[side, beyond_lane(cell), side * square + cell] = 1
    return out


def fold_table(brick_edge):
    square = brick_edge * brick_edge
    last = brick_edge - 1
    base = 4 * brick_edge
    out = np.zeros((LANES, 2 * LANES), np.float32)
    for at in range(brick_edge):
        targets = [(at, at), (brick_edge + at, last * brick_edge + at)]
        if 0 < at < last:
            targets += [(2 * brick_edge + at, at * brick_edge), (3 * brick_edge + at, at * brick_edge + last)]
        else:
            out[base + 2 * brick_edge + at, LANES + beyond_lane(at * brick_edge)] = -1
            out[base + 3 * brick_edge + at, LANES + beyond_lane(at * brick_edge + last)] = -1
        for source, cell in targets:
            out[base + source, cell] = 1
            out[base + source, square + cell] = 1
    return out


def split_two(value):
    high = value.astype(jnp.bfloat16)
    low = (value - high.astype(jnp.float32)).astype(jnp.bfloat16)
    return high, low


def contract_last(left, right):
    return lax.dot_general(left, right, (((1,), (1,)), ((), ())), preferred_element_type=jnp.float32)


def pack_kernel(group_len, tile_count, partners, brick_hbm, slot_hbm, grad_hbm, table_hbm, out_ref, table_ref, brick_ref, slot_ref, grad_ref, high_ref, sems):
    channels = grad_hbm.shape[0]
    blocks = brick_ref.shape[0]
    dests = len(partners)
    copies = [
        pltpu.make_async_copy(brick_hbm, brick_ref, sems.at[0]),
        pltpu.make_async_copy(slot_hbm, slot_ref, sems.at[1]),
        pltpu.make_async_copy(grad_hbm, grad_ref, sems.at[2]),
        pltpu.make_async_copy(table_hbm, table_ref, sems.at[3]),
    ]
    for copy in copies:
        copy.start()
    at_row = lax.broadcasted_iota(jnp.int32, (LANES, 2 * LANES), 0)
    at_lane = lax.broadcasted_iota(jnp.int32, (LANES, 2 * LANES), 1)
    tri = jnp.where((at_row < at_lane) | (at_lane >= LANES), 1.0, 0.0).astype(jnp.bfloat16)
    copies[0].wait()
    brick = brick_ref[...]
    bucket = brick // group_len
    local = brick - bucket * group_len
    bucket_f = bucket.astype(jnp.float32)
    dest_ids = lax.broadcasted_iota(jnp.int32, (dests, LANES), 0).astype(jnp.float32)
    hots = [
        jnp.where(jnp.broadcast_to(bucket_f[i : i + 1], (dests, LANES)) == dest_ids, 1.0, 0.0)
        for i in range(blocks)
    ]
    counts = jnp.dot(
        jnp.concatenate(hots, axis=0).astype(jnp.bfloat16), tri, preferred_element_type=jnp.float32
    )
    before = jnp.zeros((dests, LANES), jnp.float32)
    ranks = []
    for i in range(blocks):
        part = counts[i * dests : (i + 1) * dests]
        ranks.append(jnp.sum(hots[i] * (part[:, :LANES] + before), axis=0, keepdims=True))
        before = before + part[:, LANES:]
    rank = jnp.concatenate(ranks, axis=1)

    rows = lax.broadcasted_iota(jnp.int32, (4, LANES), 0)
    copies[1].wait()
    slot = slot_ref[...]
    coord_x = (local // 4) * E + slot // (E * E)
    coord_y = (local // 2 % 2) * E + slot // E % E
    coord_z = (local % 2) * E + slot % E
    x_f = coord_x.astype(jnp.float32)
    y_f = coord_y.astype(jnp.float32)
    z_f = coord_z.astype(jnp.float32)
    for i in range(blocks):
        code = jnp.where(
            rows == 0,
            x_f[i : i + 1],
            jnp.where(rows == 1, y_f[i : i + 1], jnp.where(rows == 2, z_f[i : i + 1], 0.0)),
        )
        high_ref[channels - 16 : channels - 12, i * LANES : (i + 1) * LANES] = code.astype(jnp.bfloat16)
    copies[2].wait()
    high_ref[: channels - 16, :] = grad_ref[16:channels, :]
    low = grad_ref[:16, :]
    high = high_ref[...]

    def spread(value):
        return jnp.concatenate(
            [jnp.broadcast_to(value[i : i + 1], (16, LANES)) for i in range(blocks)], axis=1
        ).astype(jnp.bfloat16)

    owner16 = spread((bucket // tile_count).astype(jnp.float32))
    tile16 = spread((bucket % tile_count).astype(jnp.float32))
    zero = jnp.zeros_like(low)
    left = []
    for owner in range(dests // tile_count):
        mask = owner16 == jnp.bfloat16(owner)
        left += [jnp.where(mask, low, zero), jnp.where(mask, high, zero)]
    half = LANES // 2
    rank16 = jnp.broadcast_to(rank, (16, rank.shape[1])).astype(jnp.bfloat16)
    row_ids = lax.broadcasted_iota(jnp.int32, rank16.shape, 0).astype(jnp.float32)
    ones = jnp.ones_like(low)
    hot = [
        jnp.where(rank16 == (row_ids + 16.0 * g).astype(jnp.bfloat16), ones, zero) for g in range(half // 16)
    ]
    right = []
    for tile in range(tile_count):
        mask = tile16 == jnp.bfloat16(tile)
        right += [jnp.where(mask, value, zero) for value in hot]
    placed = contract_last(jnp.concatenate(left, axis=0), jnp.concatenate(right, axis=0)).astype(jnp.bfloat16)
    tiles = []
    for owner in range(dests // tile_count):
        for pair in range(tile_count // 2):
            low_part = placed[32 * owner : 32 * owner + 16, pair * LANES : (pair + 1) * LANES]
            high_part = placed[32 * owner + 16 : 32 * owner + 32, pair * LANES : (pair + 1) * LANES]
            tiles.append(jnp.concatenate([low_part[:, :half], high_part[:, :half]], axis=1))
            tiles.append(jnp.concatenate([low_part[:, half:], high_part[:, half:]], axis=1))
    for dest in range(dests):
        out_ref[dest, 0] = tiles[dest]
        out_ref[dest, 1] = tiles[partners[dest]]
    copies[3].wait()


def unpack(arrived_ref, which, channels):
    half = LANES // 2
    pairs = arrived_ref.shape[0] // 2
    lows = []
    highs = []
    for p in range(pairs):
        first = arrived_ref[p, which]
        second = arrived_ref[p + pairs, which]
        lows.append(jnp.concatenate([first[:, :half], second[:, :half]], axis=1))
        highs.append(jnp.concatenate([first[:, half:], second[:, half:]], axis=1))
    low = jnp.concatenate(lows, axis=1)
    high = jnp.concatenate(highs, axis=1)
    codes = high.astype(jnp.float32)
    at = channels - 16
    coords = [
        jnp.broadcast_to(codes[at + k : at + k + 1], (16, low.shape[1])).astype(jnp.bfloat16) for k in range(3)
    ]
    return low, high, coords


def pack_pair(first, second):
    return jnp.concatenate([first, second], axis=0).astype(jnp.bfloat16)


def block_axes(code, axis_ref):
    row = lax.broadcasted_iota(jnp.int32, (8, LANES), 0).astype(jnp.float32)
    axis_ref[0] = code
    coords = [axis_ref[0, pl.ds(at, 8, stride=0), :] for at in (4, 5, 6)]
    rows = [jnp.maximum(1.0 - jnp.abs(c * 0.5 - (row + 0.25)), 0.0) for c in coords]
    return row, coords, rows


def lines_of(axis_ref, at, rows):
    axis_ref[at] = rows
    return [axis_ref[at, pl.ds(m, 8, stride=0), :] for m in range(E)]


def select_rows(hits, low, high):
    zero = jnp.zeros_like(low)
    rows = []
    for hit in hits:
        rows += [jnp.where(hit, low, zero), jnp.where(hit, high, zero)]
    return rows


def own_block(code, axis_ref, low, high):
    row, (x, y, z), (_, y_rows, z_rows) = block_axes(code, axis_ref)
    last = 2.0 * E - 1.0
    blank = jnp.zeros((8, LANES), jnp.float32)
    y_lines = lines_of(axis_ref, 2, y_rows)
    y_pair = [pack_pair(y_lines[2 * g], y_lines[2 * g + 1]) for g in range(E // 2)]
    z_in = pack_pair(z_rows, z_rows)
    y_low = jnp.where(y == 0.0, 0.25, 0.0)
    y_high = jnp.where(y == last, 0.25, 0.0)
    z_low = jnp.where(z == 0.0, 0.25, 0.0)
    z_high = jnp.where(z == last, 0.25, 0.0)
    z_out = jnp.where(row == 0.0, z_low, jnp.where(row == E - 1.0, z_high, blank))
    y_edge = jnp.where(row == 0.0, y_low, jnp.where(row == E - 1.0, y_high, y_rows))
    z_both = z_rows + z_out
    inner = [value * z_in for value in y_pair]
    inner[0] = inner[0] + pack_pair(y_low * z_out, blank)
    inner[-1] = inner[-1] + pack_pair(blank, y_high * z_out)
    faces = [pack_pair(y_low * z_rows, y_high * z_rows), pack_pair(z_low * y_rows, z_high * y_rows)]
    edges = [
        pack_pair(y_lines[0] * z_out + y_low * z_both, y_lines[E - 1] * z_out + y_high * z_both),
        pack_pair(y_edge * z_low, y_edge * z_high),
    ]
    whole = x.astype(jnp.int32)
    pair_of = (whole >> 1).astype(jnp.float32)
    odd = (whole & 1).astype(jnp.float32)
    odd16 = pack_pair(odd, odd)
    even16 = jnp.bfloat16(1.0) - odd16
    ends = jnp.where((x == 0.0) | (x == last), 1.0, 0.0)
    ends16 = pack_pair(ends, ends)
    pair16 = pack_pair(pair_of, pair_of)
    left = select_rows([pair16 == jnp.bfloat16(at) for at in range(E)], low, high)
    right = [value * even16 for value in inner] + [value * odd16 for value in inner]
    right += [value * even16 for value in faces] + [value * ends16 for value in edges]
    return left, right + [value * odd16 for value in faces]


def skin_block(code, axis_ref, low, high):
    _, coords, (x_rows, y_rows, z_rows) = block_axes(code, axis_ref)
    last = 2 * E - 1
    x_lines = lines_of(axis_ref, 1, x_rows)
    y_lines = lines_of(axis_ref, 2, y_rows)
    x_order = list(range(0, E, 2)) + list(range(1, E, 2))
    x_pair = [pack_pair(x_lines[x_order[2 * g]], x_lines[x_order[2 * g + 1]]) for g in range(E // 2)]
    y_pair = [pack_pair(y_lines[2 * g], y_lines[2 * g + 1]) for g in range(E // 2)]
    z_in = pack_pair(z_rows, z_rows)
    y_in = pack_pair(y_rows, y_rows)
    x16, y16, z16 = [pack_pair(c, c) for c in coords]
    hits = [c == jnp.bfloat16(end) for c in (y16, z16, x16) for end in (0, last)]
    left = select_rows(hits, low, high)
    right = []
    for part in (x_pair[: E // 4], x_pair[E // 4 :]):
        right += [value * z_in for value in part] + [value * y_in for value in part]
    return left, right + [value * z_in for value in y_pair]


def lay_out(blocks):
    return jnp.concatenate(
        [jnp.concatenate([block[i] for block in blocks], axis=1) for i in range(len(blocks[0]))], axis=0
    )


def own_quarters(product, table):
    half = LANES // 2
    lane = lax.broadcasted_iota(jnp.int32, (32, LANES), 1)
    left = lane < half
    spare = lane % half >= half // 2
    blank = jnp.zeros((32, LANES - product.shape[1] % LANES), jnp.float32)
    cells = [product[32 * i : 32 * i + 32, :LANES] for i in range(E)]
    faces = [jnp.concatenate([product[32 * i : 32 * i + 32, LANES:], blank], axis=1) for i in range(E)]
    high_part, low_part = split_two(jnp.concatenate([faces[0], faces[-1]], axis=0))
    folds = jnp.dot(high_part, table, preferred_element_type=jnp.float32)
    folds = folds + jnp.dot(low_part, table, preferred_element_type=jnp.float32)

    def even_x(values, m):
        return 3.0 * values[m] + values[m + 1] if m < E - 1 else 3.0 * values[m]

    def odd_x(values, m):
        return 3.0 * values[m] + values[m - 1] if m > 0 else 3.0 * values[m]

    def layers(values, m):
        stay = jnp.where(left, even_x(values, m), odd_x(values, m + 1))
        cross = jnp.where(left, even_x(values, m + 1), odd_x(values, m))
        return stay + pltpu.roll(cross, half, 1)

    quarters = []
    for q in range(E // 2):
        own = layers(cells, 2 * q)
        skin = layers(faces, 2 * q)
        beyond = jnp.zeros_like(own)
        if q == 0:
            own = own + jnp.where(left, folds[:32, :LANES], 0.0)
            moved = jnp.where(left, pltpu.roll(cells[-1], LANES - half // 2, 1), cells[-1])
            beyond = moved + folds[32:, LANES:]
        if q == E // 2 - 1:
            own = own + jnp.where(left, 0.0, folds[32:, :LANES])
            moved = jnp.where(left, pltpu.roll(cells[0], half // 2, 1), pltpu.roll(cells[0], half, 1))
            beyond = moved + folds[:32, LANES:]
        quarters.append((own, jnp.where(spare, beyond, skin)))
    return quarters


def skin_quarters(product):
    half = LANES // 2
    lane = lax.broadcasted_iota(jnp.int32, (32, LANES), 1)
    left = lane < half
    face_of = jnp.where(lane % half < half // 2, (lane // E) % 4, 4)
    sides = [product[32 * f : 32 * f + 32, :LANES] for f in range(4)]
    ends = []
    for f in (4, 5):
        end = product[32 * f : 32 * f + 32, LANES:]
        end = jnp.concatenate([end, end], axis=1)
        ends.append(jnp.where(left, pltpu.roll(end, half // 2, 1), end))
    quarters = []
    for q in range(E // 2):
        value = ends[1] if q == 0 else ends[0] if q == E // 2 - 1 else jnp.zeros_like(sides[0])
        for f in range(4):
            shift = (E * (f - q) - (half // 2 if f >= 2 else 0)) % LANES
            moved = pltpu.roll(sides[f], shift, 1) if shift else sides[f]
            value = jnp.where(face_of == f, moved, value)
        quarters.append(value)
    return quarters


def coarse_kernel(channels, arrived_ref, table_ref, *refs):
    out_refs, (quarter_ref, axis_ref) = refs[:4], refs[4:]
    tile_id = lax.axis_index("tile")
    half = LANES // 2
    pairs = arrived_ref.shape[0] // 2

    def blocks(which, make):
        made = []
        for p in range(pairs):
            first = arrived_ref[p, which]
            second = arrived_ref[p + pairs, which]
            low = jnp.concatenate([first[:, :half], second[:, :half]], axis=1)
            high = jnp.concatenate([first[:, half:], second[:, half:]], axis=1)
            made.append(make(high.astype(jnp.float32)[8:], axis_ref.at[which, p], low, high))
        return [[block[i] for block in made] for i in range(len(made[0]))]

    own_product = contract_last(*[lay_out(side) for side in blocks(0, own_block)])
    skin_product = contract_last(*[lay_out(side) for side in blocks(1, skin_block)])
    for q, (own, skin) in enumerate(own_quarters(0.25 * own_product, table_ref[...])):
        quarter_ref[q, 0] = own
        quarter_ref[q, 1] = skin
    for q, skin in enumerate(skin_quarters(0.25 * skin_product)):
        quarter_ref[q, 2] = skin
    for delta in range(4):
        for part in range(3):
            out_refs[delta][pl.ds(part, channels, stride=3), :] = quarter_ref[tile_id ^ delta, part][:channels]


def fine_kernel(channels, coarse_total, arrived_ref, near_ref, fine_ref, source_ref, turn_ref):
    first = lax.axis_index("brick") * CB_DEV - CB_DEV // 2
    lane = lax.broadcasted_iota(jnp.int32, (8, LANES), 1)
    group = jnp.where(lane % (LANES // 2) < 4 * E, (lane // E) % 4, 4)
    x_face = jnp.where(lax.axis_index("tile") < 2, 0, 1)
    for i in range(CB_DEV):
        near = [(near_ref[i, face] - first + coarse_total) % coarse_total for face in (3, 2, 5, 4, x_face)]
        source = jnp.where(group == 0, near[0], near[1])
        for k in range(2, 5):
            source = jnp.where(group == k, near[k], source)
        source_ref[i] = source
    low, high, coords = unpack(arrived_ref, 0, channels)
    zero = jnp.zeros_like(low)
    one = jnp.ones_like(low)
    edge = jnp.bfloat16(E)
    halves = [jnp.where(c >= edge, one, zero) for c in coords]
    inside = [c - edge * h for c, h in zip(coords, halves)]
    child_at = halves[0] * jnp.bfloat16(4) + halves[1] * jnp.bfloat16(2) + halves[2]
    cell_at = inside[1] * edge + inside[2]
    left = []
    for child in range(8):
        mask = child_at == jnp.bfloat16(child)
        left.append(jnp.where(mask, low, zero))
        left.append(jnp.where(mask, high, zero))
    row_ids = lax.broadcasted_iota(jnp.int32, low.shape, 0).astype(jnp.float32)
    cells = [
        jnp.where(cell_at == (row_ids + 16.0 * g).astype(jnp.bfloat16), one, zero) for g in range(E * E // 16)
    ]
    right = []
    for plane in range(E):
        mask = inside[0] == jnp.bfloat16(plane)
        for g in range(E * E // 16):
            right.append(jnp.where(mask, cells[g], zero))
    fine = contract_last(jnp.concatenate(left, axis=0), jnp.concatenate(right, axis=0))
    for i in range(V // LANES):
        for child in range(8):
            turn_ref[i, pl.ds(child, channels, stride=8), :] = fine[
                32 * child : 32 * child + channels, i * LANES : (i + 1) * LANES
            ]
        fine_ref[:, i * LANES : (i + 1) * LANES] = turn_ref[i]


def combine_kernel(channels, source_ref, zero_ref, one_ref, two_ref, three_ref,
                   table_ref, out_ref, hold_ref):
    tile_id = lax.axis_index("tile")
    for delta, ref in enumerate((zero_ref, one_ref, two_ref, three_ref)):
        hold_ref[tile_id ^ delta] = ref[...]

    def part(tile, which):
        return hold_ref[tile, pl.ds(which, channels, stride=3), :]

    skins = [part(2, 2), part(3, 2)] + [part(j, 1) for j in range(4)] + [part(0, 2), part(1, 2)]
    gathered = []
    for i in range(4):
        source = jnp.broadcast_to(source_ref[i, :1], (channels, LANES))
        first = 0 if i < 2 else 4
        value = jnp.zeros((channels, LANES), jnp.float32)
        for e in range(first, first + 4):
            value = jnp.where(source == e, skins[e], value)
        gathered.append(value)
    table = table_ref[tile_id // 2]
    for i in range(4):
        high_part, low_part = split_two(gathered[i])
        moved = jnp.dot(high_part, table, preferred_element_type=jnp.float32) + jnp.dot(
            low_part, table, preferred_element_type=jnp.float32
        )
        out_ref[pl.ds(i, channels, stride=4), :] = part(i, 0) + moved


def family_body(sample_grad, sample_brick, sample_slot, neighbour):
    tile_count = lax.axis_size("tile")
    owners = lax.axis_size("brick")
    channels, samples = sample_grad.shape
    dests = owners * tile_count
    group_len = FB_DEV // tile_count
    vmem = pl.BlockSpec(memory_space=pltpu.VMEM)
    hbm = pl.BlockSpec(memory_space=pltpu.HBM)
    limit = pltpu.CompilerParams(vmem_limit_bytes=KERNEL_VMEM)
    partners = []
    for b in range(owners):
        for t in range(tile_count):
            step = -1 if t >= tile_count // 2 else 1
            partners.append((b + step) % owners * tile_count + t)
    inputs = (
        sample_brick.reshape(samples // LANES, LANES),
        sample_slot.reshape(samples // LANES, LANES),
        sample_grad,
        jnp.asarray(fold_table(E), jnp.bfloat16),
    )
    packed, table = pl.pallas_call(
        functools.partial(pack_kernel, group_len, tile_count, tuple(partners)),
        out_shape=(
            jax.ShapeDtypeStruct((dests, 2, 16, LANES), jnp.bfloat16),
            jax.ShapeDtypeStruct((LANES, 2 * LANES), jnp.bfloat16),
        ),
        in_specs=[hbm] * 4,
        out_specs=(vmem, vmem),
        scratch_shapes=[
            pltpu.VMEM((samples // LANES, LANES), jnp.int32),
            pltpu.VMEM((samples // LANES, LANES), jnp.int32),
            pltpu.VMEM((channels, samples), jnp.bfloat16),
            pltpu.VMEM((16, samples), jnp.bfloat16),
            pltpu.SemaphoreType.DMA((4,)),
        ],
        compiler_params=limit,
        name="pack",
    )(*[pltpu.with_memory_space_constraint(value, pltpu.HBM) for value in inputs])
    arrived = lax.all_to_all(packed, ("brick", "tile"), 0, 0, tiled=True)
    message = jax.ShapeDtypeStruct((3 * channels, LANES), jnp.float32)
    messages = pl.pallas_call(
        functools.partial(coarse_kernel, channels),
        out_shape=(message,) * 4,
        in_specs=[vmem, vmem],
        out_specs=(vmem,) * 4,
        scratch_shapes=[
            pltpu.VMEM((4, 3, 32, LANES), jnp.float32),
            pltpu.VMEM((2, dests // 2, 3, 8, LANES), jnp.float32),
        ],
        compiler_params=limit,
        name="coarse",
    )(arrived, table)
    arrivals = {}
    for delta in (3, 1, 2):
        arrivals[delta] = lax.ppermute(messages[delta], "tile", [(t, t ^ delta) for t in range(tile_count)])
    fine, source = pl.pallas_call(
        functools.partial(fine_kernel, channels, CB_DEV * owners),
        out_shape=(
            jax.ShapeDtypeStruct((channels * 8, V), jnp.float32),
            jax.ShapeDtypeStruct((CB_DEV, 8, LANES), jnp.int32),
        ),
        in_specs=[vmem, pl.BlockSpec(memory_space=pltpu.SMEM)],
        out_specs=(vmem, vmem),
        scratch_shapes=[pltpu.VMEM((V // LANES, channels * 8, LANES), jnp.float32)],
        compiler_params=limit,
        name="fine",
    )(arrived, neighbour)
    coarse = pl.pallas_call(
        functools.partial(combine_kernel, channels),
        out_shape=jax.ShapeDtypeStruct((channels * CB_DEV, LANES), jnp.float32),
        in_specs=[vmem] * 6,
        out_specs=vmem,
        scratch_shapes=[pltpu.VMEM((4, 3 * channels, LANES), jnp.float32)],
        compiler_params=limit,
        name="combine",
    )(source, messages[0], arrivals[1], arrivals[2], arrivals[3], jnp.asarray(expand_tables(E), jnp.bfloat16))
    fine_grad = fine.reshape(channels, 8, V).transpose(1, 0, 2)
    coarse_grad = coarse.reshape(channels, CB_DEV, LANES).transpose(1, 0, 2)
    return fine_grad, coarse_grad


def solution(mesh):
    in_specs = (
        P(None, ("brick", "tile")),
        P(("brick", "tile")),
        P(("brick", "tile")),
        P("brick", None),
    )
    out_specs = (P(("brick", "tile"), None, None), P("brick", None, "tile"))

    def step(sample_grad, sample_brick, sample_slot, neighbour):
        owners, tile_count = mesh.shape["brick"], mesh.shape["tile"]
        samples = sample_grad.shape[1] // (owners * tile_count)
        whole_family = FB_DEV == 8 * tile_count == 2 * 4 * CB_DEV and tile_count == CB_DEV
        full_messages = 2 * samples == (LANES // 2) * owners * tile_count and samples % LANES == 0
        fits = whole_family and full_messages and sample_grad.shape[0] == 28 and owners > 2
        if not fits:
            mapped = jax.shard_map(body, mesh=mesh, in_specs=in_specs, out_specs=out_specs, check_vma=False)
        else:
            mapped = jax.shard_map(family_body, mesh=mesh, in_specs=in_specs, out_specs=out_specs, check_vma=False)
        return mapped(sample_grad, sample_brick, sample_slot, neighbour)

    return step
```
